128 devices in a mesh: lon: 32 (over z, x, core), lat: 4 (over y).
Axes of the slice: x: 4, y: 4, z: 4, core: 2. Of those that a mesh axis runs over, the one named last changes fastest.
Arguments:
- state_field: float32 [2, 137, 128, 4096], P(None, None, 'lat', 'lon'), may hold values from -6 to 6
- jacobian: bfloat16 [4, 2048, 2, 137, 128], P('lat', 'lon'), may hold values from -0.375 to 0.375
- observed: bfloat16 [4, 2048, 128], P('lat', 'lon'), may hold values from -6 to 6
- inverse_var: bfloat16 [4, 2048, 128], P('lat', 'lon'), may hold values from 0.25 to 4
- valid_count: int32 [4, 2048], P('lat', 'lon'), may hold values from 32 to 128
- destination: int32 [4, 2048, 1], P('lat', 'lon'), may hold values from 0 to 31; in each aligned block of 64 rows (0 to 63, 64 to 127, ..., all dimensions but the last counted through in order) at most 4 rows name the same one
- column: int32 [4, 2048], P('lat', 'lon'), may hold values from 0 to 4095
- vertical: bfloat16 [2, 137, 137], replicated, may hold values from -0.5 to 0.5
- lon_taps: float32 [2, 137, 9], replicated, may hold values from 0.05 to 0.3
- lat_taps: float32 [2, 137, 9], replicated, may hold values from 0.05 to 0.3
Outputs:
- gradient: float32 [2, 137, 128, 4096], P(None, None, 'lat', 'lon')
The draws below stay inside these ranges and needn't reach their ends.
Inputs may be any that keep to these rules, and one draw needn't show every extreme that they name: `destination`: among the 64 records of one device no longitude tile is named more than 4 times, a bound that some block reaches.
All inputs are finite; a program needn't handle non-finite values.
Results may differ from the reference program's by a relative error of at most 0.0045.
Values may be sent and summed in bfloat16 or wider, within the bound.
A program may use at most 128 MiB of HBM per device.

```python
import math
import jax
import jax.numpy as jnp
import numpy as np
from jax import lax

VARS = 2
LEVELS = 137
CH = 128
TAPS = 9
CLON = 128
CLAT = 32
REC_DEV = 64
BANDS = 4
NLAT = 128
NLON = 4096
RECS = 2048
CAP = 4
N_LON = 32


def touch_ends(drawn, own_key, least, high):
    index_at = [jax.random.randint(jax.random.fold_in(own_key, axis), (), 0, length) for axis, length in enumerate(drawn.shape)]
    main_axis = drawn.shape.index(max(drawn.shape))
    neighbour = index_at[:main_axis] + [(index_at[main_axis] + 1) % drawn.shape[main_axis]] + index_at[main_axis + 1:]
    return drawn.at[tuple(index_at)].set(least).at[tuple(neighbour)].set(high)


def steps_of(key, extent, split, low, largest):
    factor_of, own = 1.0, jax.random.fold_in(key, 6)
    for dim, shards_of in split:
        steps = jnp.exp(jax.random.uniform(jax.random.fold_in(own, dim), (shards_of,), jnp.float32, low / len(split), largest / len(split)))
        factor_of = factor_of * jnp.repeat(steps, extent[dim] // shards_of).reshape([-1 if axis == dim else 1 for axis in range(len(extent))])
    return factor_of


def shared_out(rng, own, number, rows, number_of, top, limit, lean):
    order = jax.random.permutation(rng, number_of)
    crowded, ordinary = portions_of(number_of, rows * top, limit, lean, True), portions_of(number_of, rows * top, limit, lean, False)
    places = jnp.arange(number_of)

    def named(tallies, turn):
        used = int((tallies > 0).sum())
        fixed = max(1, used // 4)
        moved = fixed + (places - fixed + turn * (used - fixed)) % max(1, number_of - fixed)
        return jnp.zeros((number_of,), jnp.int32).at[order[jnp.where(places < fixed, places, moved)]].set(jnp.asarray(tallies, jnp.int32))

    tallies = jnp.where(number % 4 == 0, named(crowded, number // 4), named(ordinary, number - number // 4 - 1))
    mixed = jax.random.permutation(jax.random.fold_in(own, 3), number_of)
    giver, receiver = mixed[0:number_of // 2 * 2:2], mixed[1:number_of // 2 * 2:2]
    room = jnp.minimum(tallies[giver] - 1, limit - tallies[receiver]) // 2
    room = jnp.where((giver == order[0]) | (receiver == order[0]) | (tallies[receiver] == 0), 0, jnp.maximum(room, 0))
    moved = jax.random.randint(jax.random.fold_in(own, 4), (number_of // 2,), 0, 1 << 20) % (room + 1)
    tallies = tallies.at[giver].add(-moved).at[receiver].add(moved)
    labels = jnp.searchsorted(jnp.cumsum(tallies), jnp.arange(rows * top), side="right").astype(jnp.int32)
    grid = labels.reshape(top, rows).T
    grid = grid[jax.random.permutation(jax.random.fold_in(own, 1), rows)]
    turn = jax.random.randint(jax.random.fold_in(own, 2), (rows, 1), 0, top)
    return jnp.take_along_axis(grid, (jnp.arange(top)[None, :] + turn) % top, axis=1)


def portions_of(count, total, bound, lean, full):
    loads = [(1 << 20) // math.isqrt(standing ** lean) + 1 for standing in range(1, count + 1)]
    largest = bound if full else min(bound, max(-(-total // count), total * loads[0] // sum(loads)))
    least = 1 if total - largest >= count - 1 else 0
    counts, spare = [largest] + [least] * (count - 1), total - largest - least * (count - 1)
    while spare > 0:
        candidates = [i for i in range(1, count) if counts[i] < largest] or [i for i in range(1, count) if counts[i] < bound]
        pool, budget = sum([loads[i] for i in candidates]), spare
        for i in candidates:
            addition = min(bound - counts[i], max(1, budget * loads[i] // pool), spare)
            counts[i] = counts[i] + addition
            spare = spare - addition
    return np.array(counts)


def normal_values(key, extent, deviation, limit, shards=(), kind=jnp.bfloat16):
    values = jax.random.normal(key, extent, jnp.float32) * deviation
    if len(shards) > 0:
        values = steps_of(key, extent, shards, -0.22, 0.18) * values
    return jnp.clip(values, min=-limit, max=limit).astype(kind)


def setup_inputs(seed: int = 0) -> dict:
    splits = jax.random.split(jax.random.key(seed), 11)
    state_field = normal_values(splits[0], (VARS, LEVELS, NLAT, NLON), 1.0, 6.0, ((2, 4), (3, 32)), jnp.float32)
    jacobian = normal_values(splits[1], (BANDS, RECS, VARS, LEVELS, CH), (VARS * LEVELS) ** -0.5, 0.375, ((0, 4), (1, 32)))
    observed = normal_values(splits[2], (BANDS, RECS, CH), 1.0, 6.0, ((0, 4), (1, 32)))
    inverse_var = jnp.clip(jnp.exp(math.log(4.0) - 2.7725887 * jax.random.uniform(splits[3], (BANDS, RECS, CH), jnp.float32) ** steps_of(splits[3], (BANDS, RECS, CH), ((0, 4), (1, 32)), -0.2, 0.2)), 0.25, 4.0).astype(jnp.bfloat16)
    valid_count = touch_ends(jax.random.randint(splits[4], (BANDS, RECS), CH // 4, CH + 1), jax.random.fold_in(splits[4], 1), CH // 4, CH).astype(jnp.int32)
    destination_keys = jax.random.split(jax.random.fold_in(splits[5], 1), BANDS * RECS // REC_DEV)
    destination_turns = jax.random.permutation(jax.random.fold_in(splits[5], 3), BANDS * RECS // REC_DEV)
    destination = jax.vmap(lambda own, number: shared_out(jax.random.fold_in(splits[5], 2), own, number, REC_DEV, N_LON, 1, CAP, 2))(destination_keys, destination_turns).reshape((BANDS, RECS, 1))
    column = touch_ends(jax.random.randint(splits[6], (BANDS, RECS), 0, CLAT * CLON), jax.random.fold_in(splits[6], 1), 0, (CLAT * CLON) - 1).astype(jnp.int32)
    vertical = normal_values(splits[7], (VARS, LEVELS, LEVELS), LEVELS ** -0.5, 0.5)
    lon_taps = jnp.clip(jax.random.uniform(splits[8], (VARS, LEVELS, TAPS), jnp.float32, 0.05, 0.3), 0.05, 0.3)
    lat_taps = jnp.clip(jax.random.uniform(splits[9], (VARS, LEVELS, TAPS), jnp.float32, 0.05, 0.3), 0.05, 0.3)
    return dict(state_field=state_field, jacobian=jacobian, observed=observed, inverse_var=inverse_var, valid_count=valid_count, destination=destination, column=column, vertical=vertical, lon_taps=lon_taps, lat_taps=lat_taps)


def reference(state_field, jacobian, observed, inverse_var, valid_count, destination, column, vertical, lon_taps, lat_taps):
    features = VARS * LEVELS
    highest = lax.Precision.HIGHEST
    rounded = lax.optimization_barrier(state_field.astype(jnp.bfloat16)).astype(jnp.float32)
    rounded = rounded.reshape(features, NLAT * NLON)
    band_start = (jnp.arange(BANDS, dtype=jnp.int32) * CLAT)[:, None]
    lat_index = band_start + column // CLON
    lon_index = destination[..., 0] * CLON + column % CLON
    flat_index = (lat_index * NLON + lon_index).astype(jnp.int32)
    alive_mask = jnp.arange(CH, dtype=jnp.int32)[None, None, :] < valid_count[..., None]

    def one_band(pieces):
        jac_band, obs_band, inv_band, alive_band, index_band = pieces
        jac_full = jac_band.astype(jnp.float32).reshape(RECS, features, CH)
        state_cols = jnp.take(rounded, index_band, axis=1).T
        model = jnp.einsum('rfc,rf->rc', jac_full, state_cols, precision=highest)
        misfit = jnp.where(alive_band, inv_band.astype(jnp.float32), jnp.float32(0.0)) * (model - obs_band.astype(jnp.float32))
        scaled = lax.optimization_barrier(misfit.astype(jnp.bfloat16)).astype(jnp.float32)
        return jnp.einsum('rfc,rc->rf', jac_full, scaled, precision=highest)

    products = lax.map(one_band, (jacobian, observed, inverse_var, alive_mask, flat_index))
    impact = jnp.zeros((features, NLAT * NLON), jnp.float32)
    impact = impact.at[:, flat_index.reshape(-1)].add(products.reshape(-1, features).T)
    impact = impact.reshape(VARS, LEVELS, NLAT, NLON)
    reach = TAPS // 2

    def one_variable(pieces):
        impact_var, vert_var, lon_var, lat_var = pieces
        impact_low = lax.optimization_barrier(impact_var.astype(jnp.bfloat16)).astype(jnp.float32)
        mixed = jnp.einsum('lm,lij->mij', vert_var.astype(jnp.float32), impact_low, precision=highest)
        along = jnp.zeros_like(mixed)
        for offset in range(TAPS):
            along = along + lon_var[:, offset][:, None, None] * jnp.roll(mixed, reach - offset, axis=2)
        padded = jnp.pad(along, ((0, 0), (reach, reach), (0, 0)))
        result = jnp.zeros_like(mixed)
        for offset in range(TAPS):
            result = result + lat_var[:, offset][:, None, None] * padded[:, offset:offset + NLAT, :]
        return result

    return lax.map(one_variable, (impact, vertical, lon_taps, lat_taps))
```

```python
import jax
import jax.numpy as jnp
from jax import lax
from jax.sharding import PartitionSpec as P


def padded(cells, sides, width, closed):
    for axis, dim in sides:
        count = lax.axis_size(axis)
        ends = count if closed else count - 1
        head = lax.slice_in_dim(cells, 0, width, axis=dim)
        tail = lax.slice_in_dim(cells, cells.shape[dim] - width, cells.shape[dim], axis=dim)
        cells = jnp.concatenate(
            [
                lax.ppermute(tail, axis, [(i, (i + 1) % count) for i in range(ends)]),
                cells,
                lax.ppermute(head, axis, [((i + 1) % count, i) for i in range(ends)]),
            ],
            axis=dim,
        )
    return cells


def slot_layout(dest_local, lon_devices, capacity):
    onehot = (dest_local[:, None] == jnp.arange(lon_devices, dtype=jnp.int32)[None, :]).astype(
        jnp.int32
    )
    before = jnp.cumsum(onehot, axis=0) - onehot
    ranking = jnp.sum(before * onehot, axis=1)
    return dest_local * capacity + ranking


def lon_filter(extended, taps, width):
    result = jnp.zeros(extended.shape[:-1] + (width,), jnp.float32)
    for offset in range(taps.shape[-1]):
        result = (
            result + taps[:, :, offset][:, :, None, None] * extended[..., offset : offset + width]
        )
    return result


def lat_filter(extended, taps, height):
    result = jnp.zeros(extended.shape[:2] + (height, extended.shape[3]), jnp.float32)
    for offset in range(taps.shape[-1]):
        result = (
            result
            + taps[:, :, offset][:, :, None, None] * extended[:, :, offset : offset + height, :]
        )
    return result


def body(
    state_field,
    jacobian,
    observed,
    inverse_var,
    valid_count,
    destination,
    column,
    vertical,
    lon_taps,
    lat_taps,
):
    lon_devices = lax.axis_size("lon")
    var_count, level_count, row_count, col_count = state_field.shape
    features = var_count * level_count
    records = jacobian.shape[1]
    channels = jacobian.shape[-1]
    capacity = max(2, 2 * records // lon_devices)
    slot_total = lon_devices * capacity
    jac = jacobian.reshape(records, var_count, level_count, channels)
    dest_local = destination.reshape(records)
    col_local = column.reshape(records)
    alive_mask = (
        jnp.arange(channels, dtype=jnp.int32)[None, :] < valid_count.reshape(records)[:, None]
    )
    weight_rows = jnp.where(
        alive_mask, inverse_var.reshape(records, channels), jnp.zeros((), jnp.bfloat16)
    )
    obs_rows = observed.reshape(records, channels)
    slots = slot_layout(dest_local, lon_devices, capacity)
    place = (slots[:, None] == jnp.arange(slot_total, dtype=jnp.int32)[None, :]).astype(jnp.bfloat16)
    col_buffer = (
        jnp.zeros((slot_total,), jnp.int32).at[slots].set(col_local).reshape(lon_devices, capacity)
    )
    col_in = lax.all_to_all(col_buffer, "lon", split_axis=0, concat_axis=0, tiled=True)
    cells = col_in.reshape(-1)
    grid = row_count * col_count
    pick = (cells[:, None] == jnp.arange(grid, dtype=jnp.int32)[None, :]).astype(jnp.bfloat16)
    state_low = state_field.astype(jnp.bfloat16).reshape(features, grid)
    columns = jnp.einsum("sp,fp->sf", pick, state_low, preferred_element_type=jnp.float32)
    columns = columns.astype(jnp.bfloat16).reshape(lon_devices, capacity, features)
    back = lax.all_to_all(columns, "lon", split_axis=0, concat_axis=0, tiled=True)
    mine = jnp.einsum(
        "rs,sf->rf", place, back.reshape(slot_total, features), preferred_element_type=jnp.float32
    ).astype(jnp.bfloat16).reshape(records, var_count, level_count)
    model = jnp.einsum("rvlc,rvl->rc", jac, mine, preferred_element_type=jnp.float32)
    misfit = weight_rows.astype(jnp.float32) * (model - obs_rows.astype(jnp.float32))
    scaled = misfit.astype(jnp.bfloat16)
    terms = jnp.einsum("rvlc,rc->rvl", jac, scaled, preferred_element_type=jnp.float32)
    terms = terms.reshape(records, features).astype(jnp.bfloat16)
    sent = jnp.einsum("rs,rf->sf", place, terms, preferred_element_type=jnp.float32)
    sent = sent.astype(jnp.bfloat16).reshape(lon_devices, capacity, features)
    got = lax.all_to_all(sent, "lon", split_axis=0, concat_axis=0, tiled=True)
    impact = jnp.einsum(
        "sf,sp->fp", got.reshape(slot_total, features), pick, preferred_element_type=jnp.float32
    )
    impact_low = impact.reshape(var_count, level_count, grid).astype(jnp.bfloat16)
    mixed = jnp.einsum("vlm,vlp->vmp", vertical, impact_low, preferred_element_type=jnp.float32)
    mixed = mixed.reshape(var_count, level_count, row_count, col_count)
    reach = lon_taps.shape[-1] // 2
    lon_wide = padded(mixed, (("lon", 3),), reach, True)
    filtered = lon_filter(lon_wide, lon_taps, col_count)
    lat_tall = padded(filtered, (("lat", 2),), reach, False)
    return lat_filter(lat_tall, lat_taps, row_count)


def solution(mesh):
    placed = (
        P(None, None, "lat", "lon"),
        P("lat", "lon", None, None, None),
        P("lat", "lon", None),
        P("lat", "lon", None),
        P("lat", "lon"),
        P("lat", "lon", None),
        P("lat", "lon"),
        P(),
        P(),
        P(),
    )
    return jax.shard_map(
        body, mesh=mesh, in_specs=placed, out_specs=P(None, None, "lat", "lon"), check_vma=False
    )
```

```python
import functools

import jax
import jax.numpy as jnp
from jax import lax
from jax.experimental import pallas as pl
from jax.experimental.pallas import tpu as pltpu
from jax.sharding import PartitionSpec as P

F32 = jnp.float32
BF16 = jnp.bfloat16


def slot_layout(dest_local, lon_devices, capacity):
    onehot = (dest_local[:, None] == jnp.arange(lon_devices, dtype=jnp.int32)[None, :]).astype(
        jnp.int32
    )
    before = jnp.cumsum(onehot, axis=0) - onehot
    ranking = jnp.sum(before * onehot, axis=1)
    return dest_local * capacity + ranking


def grid_kernel(rows, halo, lanes, chunk, tab_ref, cor_ref, pos_ref, edge_ref, tap_ref, out_ref, x_ref, d_ref):
    half = tab_ref.shape[1]
    slots = tab_ref.shape[2]
    tall = rows + 2 * halo
    packed = d_ref.shape[1]
    wide = 2 * halo

    @pl.when((pl.program_id(0) == 0) & (pl.program_id(1) == 0))
    def _():
        which = (lax.broadcasted_iota(jnp.int32, (half, slots), 1) // 4) % 2

        def stacked(index):
            table = tab_ref[index].astype(F32)
            return jnp.concatenate(
                [jnp.where(which == v, table, 0.0) for v in range(2)], axis=0
            ).astype(BF16)

        own, up, down = stacked(0), stacked(1), stacked(2)
        left, right = stacked(3), stacked(4)

        def spread(table, index, start, count):
            at = lax.broadcasted_iota(jnp.int32, (slots, count), 1) + start
            hot = jnp.where(pos_ref[:, index : index + 1] == at, 1.0, 0.0).astype(BF16)
            return jnp.dot(table, hot, preferred_element_type=F32)

        x_ref[:, 0 : halo * lanes] = spread(up, 1, 0, halo * lanes)
        x_ref[:, (rows + halo) * lanes : tall * lanes] = spread(
            down, 2, (rows + halo) * lanes, halo * lanes
        )

        @pl.loop(0, rows * lanes // chunk)
        def _(step):
            start = pl.multiple_of(step * chunk + halo * lanes, chunk)
            x_ref[:, pl.ds(start, chunk)] = spread(own, 0, start, chunk)

        at = lax.broadcasted_iota(jnp.int32, (slots, packed), 1)
        total = jnp.zeros((2 * half, packed), F32)
        for index, table in enumerate((own, up, down, left, right)):
            sign = -1.0 if index < 3 else 1.0
            hot = jnp.where(edge_ref[:, index : index + 1] == at, sign, 0.0).astype(BF16)
            total = total + jnp.dot(table, hot, preferred_element_type=F32)
        crow = lax.broadcasted_iota(jnp.int32, (cor_ref.shape[0], packed), 0)
        cat = lax.broadcasted_iota(jnp.int32, (cor_ref.shape[0], packed), 1)
        c, i, j = crow // 32, (crow // 4) % 4, crow % 4
        spot = ((c // 2) * (rows + halo) + i) * wide + (c % 2) * halo + j
        hot = jnp.where(spot == cat, 1.0, 0.0).astype(BF16)
        cv = (lax.broadcasted_iota(jnp.int32, cor_ref.shape, 0) // 16) % 2
        for v in range(2):
            part = jnp.where(cv == v, cor_ref[...].astype(F32), 0.0).astype(BF16)
            got = lax.dot_general(
                part, hot, (((0,), (0,)), ((), ())), preferred_element_type=F32
            )
            d_ref[v * half : (v + 1) * half, :] = (
                total[v * half : (v + 1) * half] + got[0:half]
            )

    base = pl.multiple_of((pl.program_id(0) * pl.num_programs(1) + pl.program_id(1)) * 8, 8)
    lane = lax.broadcasted_iota(jnp.int32, (8, lanes), 1)
    place = lane % wide
    taps = tap_ref[pl.ds(base, 8), :]
    lon = [jnp.broadcast_to(taps[:, k : k + 1], (8, lanes)) for k in range(9)]
    lat = [jnp.broadcast_to(taps[:, 9 + k : 10 + k], (8, lanes)) for k in range(9)]
    fixes = []
    for q in range(packed // lanes):
        d = d_ref[pl.ds(base, 8), q * lanes : (q + 1) * lanes]
        fix = jnp.zeros((8, lanes), F32)
        for k in range(9):
            shift = k - halo
            if shift == 0:
                continue
            if shift > 0:
                reach = (place < halo) & (place + shift >= halo)
            else:
                reach = (place >= halo) & (place + shift < halo)
            fix = fix + jnp.where(reach, lon[k], 0.0) * pltpu.roll(d, (-shift) % lanes, 1)
        fixes.append(fix)
    rim = (lane < halo) | (lane >= lanes - halo)
    along = []
    for i in range(tall):
        x = x_ref[pl.ds(base, 8), i * lanes : (i + 1) * lanes]
        row = lon[halo] * x
        for k in range(9):
            shift = k - halo
            if shift != 0:
                row = row + lon[k] * pltpu.roll(x, (-shift) % lanes, 1)
        q, r = divmod(i * wide, lanes)
        fix = pltpu.roll(fixes[q], (-(r + halo)) % lanes, 1)
        along.append(row + jnp.where(rim, fix, 0.0))
        if i >= 2 * halo:
            out = lat[0] * along[i - 8]
            for k in range(1, 9):
                out = out + lat[k] * along[i - 8 + k]
            out_ref[0, :, i - 8, :] = out


def grid_call(tables, corners, pos, edge, taps, levels, rows, lanes):
    halo = 4
    half = tables.shape[1]
    tall = rows + 2 * halo
    packed = -(-tall * 2 * halo // lanes) * lanes
    whole = lambda array: pl.BlockSpec(array.shape, lambda v, b: (0,) * array.ndim)
    return pl.pallas_call(
        functools.partial(grid_kernel, rows, halo, lanes, 512),
        out_shape=jax.ShapeDtypeStruct((2, levels, rows, lanes), F32),
        grid=(2, half // 8),
        in_specs=[whole(tables), whole(corners), whole(pos), whole(edge), whole(taps)],
        out_specs=pl.BlockSpec((1, 8, rows, lanes), lambda v, b: (v, b, 0, 0)),
        scratch_shapes=[
            pltpu.VMEM((2 * half, tall * lanes), F32),
            pltpu.VMEM((2 * half, packed), F32),
        ],
        compiler_params=pltpu.CompilerParams(vmem_limit_bytes=40 << 20),
        name="grid",
    )(tables, corners, pos, edge, taps)


def body(
    state_field,
    jacobian,
    observed,
    inverse_var,
    valid_count,
    destination,
    column,
    vertical,
    lon_taps,
    lat_taps,
):
    lon_devices = lax.axis_size("lon")
    lat_devices = lax.axis_size("lat")
    var_count, level_count, row_count, col_count = state_field.shape
    features = var_count * level_count
    records = jacobian.shape[1]
    channels = jacobian.shape[-1]
    capacity = max(2, 2 * records // lon_devices)
    slot_total = lon_devices * capacity
    jac = jacobian.reshape(records, var_count, level_count, channels)
    dest_local = destination.reshape(records)
    col_local = column.reshape(records)
    alive_mask = (
        jnp.arange(channels, dtype=jnp.int32)[None, :] < valid_count.reshape(records)[:, None]
    )
    weight_rows = jnp.where(
        alive_mask, inverse_var.reshape(records, channels), jnp.zeros((), jnp.bfloat16)
    )
    obs_rows = observed.reshape(records, channels)
    slots = slot_layout(dest_local, lon_devices, capacity)
    place = (slots[:, None] == jnp.arange(slot_total, dtype=jnp.int32)[None, :]).astype(jnp.bfloat16)
    col_buffer = (
        jnp.full((slot_total,), -1, jnp.int32).at[slots].set(col_local).reshape(lon_devices, capacity)
    )
    col_in = lax.all_to_all(col_buffer, "lon", split_axis=0, concat_axis=0, tiled=True)
    cells = col_in.reshape(-1)
    grid = row_count * col_count
    pick = (cells[:, None] == jnp.arange(grid, dtype=jnp.int32)[None, :]).astype(jnp.bfloat16)
    state_low = state_field.astype(jnp.bfloat16).reshape(features, grid)
    columns = jnp.einsum("sp,fp->sf", pick, state_low, preferred_element_type=jnp.float32)
    columns = columns.astype(jnp.bfloat16).reshape(lon_devices, capacity, features)
    back = lax.all_to_all(columns, "lon", split_axis=0, concat_axis=0, tiled=True)
    mine = jnp.einsum(
        "rs,sf->rf", place, back.reshape(slot_total, features), preferred_element_type=jnp.float32
    ).astype(jnp.bfloat16).reshape(records, var_count, level_count)
    model = jnp.einsum("rvlc,rvl->rc", jac, mine, preferred_element_type=jnp.float32)
    misfit = weight_rows.astype(jnp.float32) * (model - obs_rows.astype(jnp.float32))
    scaled = misfit.astype(jnp.bfloat16)
    terms = jnp.einsum("rvlc,rc->rvl", jac, scaled, preferred_element_type=jnp.float32)
    terms = terms.reshape(records, features).astype(jnp.bfloat16)
    sent = jnp.einsum("rs,rf->sf", place, terms, preferred_element_type=jnp.float32)
    sent = sent.astype(jnp.bfloat16).reshape(lon_devices, capacity, features)
    got = lax.all_to_all(sent, "lon", split_axis=0, concat_axis=0, tiled=True)
    got = got.reshape(lon_devices, capacity, var_count, level_count)
    table = jnp.einsum("vlm,akvl->mavk", vertical, got, preferred_element_type=jnp.float32)
    table = jnp.pad(
        table.astype(BF16).reshape(level_count, 2 * slot_total), ((0, 144 - level_count), (0, 0))
    )

    def shifted(value, axis, step):
        count = lax.axis_size(axis)
        if axis == "lon":
            pairs = [(i, (i + step) % count) for i in range(count)]
        else:
            pairs = [(i, i + step) for i in range(count) if 0 <= i + step < count]
        return lax.ppermute(value, axis, pairs)

    def corner(top, first):
        base_i = 0 if top else row_count - 4
        base_j = 0 if first else col_count - 4
        spots = (base_i + jnp.arange(4))[:, None] * col_count + base_j + jnp.arange(4)[None, :]
        hot = (cells[:, None] == spots.reshape(1, 16)).astype(BF16)
        rows = jnp.einsum(
            "mavk,akx->vxm",
            table[:level_count].reshape(level_count, lon_devices, 2, capacity),
            hot.reshape(lon_devices, capacity, 16),
            preferred_element_type=F32,
        )
        return jnp.pad(rows.reshape(32, level_count).astype(BF16), ((0, 0), (0, 256 - level_count)))

    corners = jnp.concatenate(
        [
            shifted(shifted(corner(False, False), "lat", 1), "lon", 1),
            shifted(shifted(corner(False, True), "lat", 1), "lon", -1),
            shifted(shifted(corner(True, False), "lat", -1), "lon", 1),
            shifted(shifted(corner(True, True), "lat", -1), "lon", -1),
        ]
    )
    tables = jnp.stack(
        [
            table,
            shifted(table, "lat", 1),
            shifted(table, "lat", -1),
            shifted(table, "lon", 1),
            shifted(table, "lon", -1),
        ]
    )
    spots = jnp.broadcast_to(cells.reshape(lon_devices, 1, capacity), (lon_devices, 2, capacity))
    spots = spots.reshape(-1)
    spots = [
        spots,
        shifted(spots, "lat", 1),
        shifted(spots, "lat", -1),
        shifted(spots, "lon", 1),
        shifted(spots, "lon", -1),
    ]
    offsets = [4, 4 - row_count, 4 + row_count, 4, 4]
    pos, edge = [], []
    for index in range(5):
        i = spots[index] // col_count + offsets[index]
        j = spots[index] % col_count
        good = (spots[index] >= 0) & (i >= 0) & (i < row_count + 8)
        pos.append(jnp.where(good, i * col_count + j, -1))
        near = jnp.where(j < 4, j + 4, j - (col_count - 4))
        use = (j < 4) | (j >= col_count - 4)
        if index == 3:
            use = j >= col_count - 4
        if index == 4:
            use = j < 4
        edge.append(jnp.where(good & use, i * 8 + near, -1))
    pos = jnp.stack(pos + pos[:3], axis=1)
    edge = jnp.stack(edge + edge[:3], axis=1)
    taps = jnp.concatenate([lon_taps, lat_taps], axis=2)
    taps = jnp.pad(taps, ((0, 0), (0, 144 - level_count), (0, 0))).reshape(288, 18)
    return grid_call(tables, corners, pos, edge, taps, level_count, row_count, col_count)


def solution(mesh):
    placed = (
        P(None, None, "lat", "lon"),
        P("lat", "lon", None, None, None),
        P("lat", "lon", None),
        P("lat", "lon", None),
        P("lat", "lon"),
        P("lat", "lon", None),
        P("lat", "lon"),
        P(),
        P(),
        P(),
    )
    return jax.shard_map(
        body, mesh=mesh, in_specs=placed, out_specs=P(None, None, "lat", "lon"), check_vma=False
    )
```

```python
import functools

import jax
import jax.numpy as jnp
from jax import lax
from jax.experimental import pallas as pl
from jax.experimental.pallas import tpu as pltpu
from jax.sharding import PartitionSpec as P

F32 = jnp.float32
BF16 = jnp.bfloat16


MESH = pl.DeviceIdType.MESH
NT = (((1,), (1,)), ((), ()))
TN = (((0,), (0,)), ((), ()))


def iota(shape, dim):
    return lax.broadcasted_iota(jnp.int32, shape, dim)


def exchange_kernel(
    sizes,
    state_hbm, jac_hbm, obs_ref, inv_ref, count_ref, dest_ref, col_ref, vert_ref,
    tab_ref, cor_ref, pos_ref,
    state_ref, low_ref, jac_ref, map_ref, bd_ref, model_ref,
    ask, asked, reply, replied, give, given,
    table, tables, corner, corners, spot, spots,
    load_sem, a2a_send, a2a_recv, near_send, near_recv,
):
    lons, lats, levels, rows, lanes, records, channels = sizes
    half = table.shape[0]
    slots = table.shape[1]
    wide = map_ref.shape[1]
    feats = 2 * levels
    me = lax.axis_index("lon")
    band = lax.axis_index("lat")
    east, west = lax.rem(me + 1, lons), lax.rem(me + lons - 1, lons)
    south, north = lax.rem(band + 1, lats), lax.rem(band + lats - 1, lats)

    load_state = pltpu.make_async_copy(state_hbm, state_ref, load_sem.at[0])
    load_jac = pltpu.make_async_copy(jac_hbm, jac_ref, load_sem.at[1])
    load_state.start()
    load_jac.start()

    barrier = pltpu.get_barrier_semaphore()

    @pl.loop(1, lons)
    def _(step):
        peer = lax.rem(me + step, lons)
        pl.semaphore_signal(barrier, inc=1, device_id={"lon": peer}, device_id_type=MESH)

    for there in (north, south):
        pl.semaphore_signal(barrier, inc=1, device_id={"lat": there}, device_id_type=MESH)
        for side in (west, east):
            pl.semaphore_signal(
                barrier, inc=1, device_id={"lat": there, "lon": side}, device_id_type=MESH
            )

    drow = dest_ref[...].astype(F32)
    prow = col_ref[...]
    irow = (prow // lanes).astype(F32)
    jrow = (prow % lanes).astype(F32)
    krow = count_ref[...].astype(F32)
    eye = iota((records, records), 0) == iota((records, records), 1)

    def column_of(row):
        return jnp.sum(jnp.where(eye, row, 0.0), axis=1, keepdims=True)

    dcol, icol, jcol, kcol = (column_of(row) for row in (drow, irow, jrow, krow))
    same = dcol == drow
    before = iota((records, records), 1) < iota((records, records), 0)
    after = iota((records, records), 0) < iota((records, records), 1)
    rank_col = jnp.sum(jnp.where(same & before, 1.0, 0.0), axis=1, keepdims=True)
    rank_row = jnp.sum(jnp.where(same & after, 1.0, 0.0), axis=0, keepdims=True)

    lane = iota((records, 2 * slots), 1)
    mine = ((lane % slots) // 8 == me) & ((lane % 4).astype(F32) == rank_col)
    value = jnp.where(lane < slots, icol + 1.0, jcol)
    values = jnp.where(mine, value, 0.0).astype(BF16)
    toward = jnp.where(iota((lons, records), 0).astype(F32) == drow, 1.0, 0.0).astype(BF16)
    asks = jnp.dot(toward, values, preferred_element_type=F32)
    ask[...] = asks.reshape(lons, 1, 2 * slots)

    pl.semaphore_wait(barrier, lons - 1 + 6)

    def send_all(source, target, phase):
        @pl.loop(1, lons)
        def _(step):
            peer = lax.rem(me + step, lons)
            pltpu.make_async_remote_copy(
                src_ref=source.at[peer],
                dst_ref=target.at[me],
                send_sem=a2a_send.at[phase],
                recv_sem=a2a_recv.at[phase],
                device_id={"lon": peer},
                device_id_type=MESH,
            ).start()

        target[me] = source[me]

    def all_of(source, target, phase):
        return pltpu.make_async_remote_copy(
            src_ref=source.at[pl.ds(0, lons - 1)],
            dst_ref=target.at[pl.ds(0, lons - 1)],
            send_sem=a2a_send.at[phase],
            recv_sem=a2a_recv.at[phase],
            device_id={"lon": east},
            device_id_type=MESH,
        )

    send_all(ask, asked, 0)

    reply[...] = jnp.zeros(reply.shape, BF16)
    load_state.wait()
    for v in range(2):
        low_ref[v, half - 16 : half, :] = jnp.zeros((16, rows * lanes), BF16)

        @pl.loop(0, rows)
        def _(i):
            plane = state_ref[pl.ds(v * levels * rows + i, levels, stride=rows), :]
            start = pl.multiple_of(i * lanes, lanes)
            low_ref[v, 0:levels, pl.ds(start, lanes)] = plane.astype(BF16)

    n = iota((1, wide), 1)
    record_of = jnp.zeros((1, wide), jnp.int32)
    for q in range(1, wide // feats):
        record_of = record_of + jnp.where(n >= q * feats, 1, 0)
    feature = n - feats * record_of
    for v in range(2):
        level = iota((256, wide), 0)
        hit = (feature == 2 * level + v) & (level < levels)
        map_ref[v * 256 : (v + 1) * 256, :] = jnp.where(hit, 1.0, 0.0).astype(BF16)

    all_of(ask, asked, 0).wait_recv()
    seen = jnp.sum(asked[...], axis=0)
    iseen, jseen = seen[:, 0:slots], seen[:, slots : 2 * slots]
    spot[...] = seen
    neighbours = (
        ({"lat": north}, 2), ({"lat": south}, 1), ({"lon": east}, 3), ({"lon": west}, 4),
    )

    def near(source, target, target_index, sem, device):
        return pltpu.make_async_remote_copy(
            src_ref=source,
            dst_ref=target.at[target_index],
            send_sem=near_send.at[sem],
            recv_sem=near_recv.at[sem],
            device_id=device,
            device_id_type=MESH,
        )

    spot_copies = [
        near(spot, spots, index - 1, index - 1, device) for device, index in neighbours
    ]
    for copy in spot_copies:
        copy.start()

    prow_slots = jnp.where(iseen > 0.0, (iseen - 1.0) * lanes + jseen, -1.0)
    pcol = jnp.transpose(jnp.broadcast_to(prow_slots, (8, slots)))[:, 0:1]

    chunk = 512
    got = [jnp.zeros((slots, half), F32) for _ in range(2)]
    for c in range(rows * lanes // chunk):
        at = (iota((slots, chunk), 1) + c * chunk).astype(F32)
        hot = jnp.where(pcol == at, 1.0, 0.0).astype(BF16)
        for v in range(2):
            got[v] = got[v] + lax.dot_general(
                hot, low_ref[v, :, c * chunk : (c + 1) * chunk], NT, preferred_element_type=F32
            )
    var_row = (iota((slots, half), 0) // 4) % 2
    states = jnp.where(var_row == 0, got[0], got[1])
    reply[:, :, 0:half] = states.reshape(lons, 8, half).astype(BF16)
    send_all(reply, replied, 1)

    load_jac.wait()
    all_of(reply, replied, 1).wait_recv()
    answers = replied[...].astype(F32).reshape(slots, 256).astype(BF16)
    slane = iota((records, slots), 1)
    hit = ((slane // 8).astype(F32) == dcol) & ((slane % 4).astype(F32) == rank_col)
    bd = jnp.zeros((records, wide), F32)
    for v in range(2):
        take = jnp.where(hit & ((slane // 4) % 2 == v), 1.0, 0.0).astype(BF16)
        picked = jnp.dot(take, answers, preferred_element_type=F32).astype(BF16)
        bd = bd + jnp.dot(
            picked, map_ref[v * 256 : (v + 1) * 256, :], preferred_element_type=F32
        )
    own_block = record_of == iota((records, wide), 0) % 8
    bd_ref[...] = jnp.where(own_block, bd, 0.0)
    for g in range(records // 8):
        model_ref[g * 8 : (g + 1) * 8, :] = jnp.dot(
            bd_ref[g * 8 : (g + 1) * 8, :].astype(BF16),
            jac_ref[g * wide : (g + 1) * wide, :],
            preferred_element_type=F32,
        )
    alive = iota((records, channels), 1).astype(F32) < kcol
    weight = jnp.where(alive, inv_ref[...].astype(F32), 0.0)
    model_ref[...] = weight * (model_ref[...] - obs_ref[...].astype(F32))
    for g in range(records // 8):
        bd_ref[g * 8 : (g + 1) * 8, :] = lax.dot_general(
            model_ref[g * 8 : (g + 1) * 8, :].astype(BF16),
            jac_ref[g * wide : (g + 1) * wide, :],
            NT,
            preferred_element_type=F32,
        )
    terms = jnp.where(own_block, bd_ref[...], 0.0).astype(BF16)
    srow = iota((slots, records), 0)
    hit = ((srow // 8).astype(F32) == drow) & ((srow % 4).astype(F32) == rank_row)
    gives = jnp.zeros((slots, 256), F32)
    for v in range(2):
        term = lax.dot_general(
            terms, map_ref[v * 256 : (v + 1) * 256, :], NT, preferred_element_type=F32
        ).astype(BF16)
        put = jnp.where(hit & ((srow // 4) % 2 == v), 1.0, 0.0).astype(BF16)
        gives = gives + jnp.dot(put, term, preferred_element_type=F32)
    give[...] = gives.reshape(lons, 8, 256).astype(BF16)
    send_all(give, given, 2)

    for copy in spot_copies:
        copy.wait()
    shifts = (4, 4 - rows, 4 + rows, 4, 4)
    stack = []
    rim = []
    for q in range(5):
        i1 = iseen if q == 0 else spots[q - 1, :, 0:slots]
        j = jseen if q == 0 else spots[q - 1, :, slots : 2 * slots]
        i = i1 - 1.0 + shifts[q]
        good = (i1 > 0.0) & (i >= 0.0) & (i < rows + 8.0)
        if q == 1:
            good = good & (iota((1, slots), 0) + band > 0)
        if q == 2:
            good = good & (iota((1, slots), 0) + band < lats - 1)
        first, last = j < 4.0, j >= lanes - 4.0
        use = last if q == 3 else first if q == 4 else first | last
        near_j = jnp.where(first, j + 4.0, j - (lanes - 4.0))
        stack.append(jnp.where(good, i * lanes + j, -1.0))
        rim.append(jnp.where(good & use, i * 8.0 + near_j, -1.0))
    stack = jnp.concatenate(stack + rim + stack[:5] + stack[:1], axis=0)
    pos_ref[...] = jnp.transpose(stack)

    all_of(give, given, 2).wait_recv()
    terms_in = given[...].astype(F32).reshape(slots, 256).astype(BF16)
    parts = [
        lax.dot_general(
            vert_ref[v * half : (v + 1) * half, :], terms_in, NT, preferred_element_type=F32
        )
        for v in range(2)
    ]
    own = jnp.where((iota((half, slots), 1) // 4) % 2 == 0, parts[0], parts[1]).astype(BF16)
    table[...] = own
    table_copies = [
        near(table, tables, index - 1, 3 + index, device) for device, index in neighbours
    ]
    for copy in table_copies:
        copy.start()
    r = iota((128, slots), 0)
    c, v, i, j = r // 32, (r // 16) % 2, (r // 4) % 4, r % 4
    at = (jnp.where(c < 2, rows - 4, 0) + i) * lanes + jnp.where(c % 2 == 0, lanes - 4, 0) + j
    hot = (prow_slots == at.astype(F32)) & ((iota((128, slots), 1) // 4) % 2 == v)
    cut = lax.dot_general(
        jnp.where(hot, 1.0, 0.0).astype(BF16), own, NT, preferred_element_type=F32
    )
    cut = jnp.concatenate([cut, jnp.zeros((128, 256 - half), F32)], axis=1)
    corner[...] = cut.reshape(4, 32, 256).astype(BF16)
    corner_copies = [
        near(corner.at[q], corners, q, 8 + q, {"lat": there, "lon": side})
        for q, (there, side) in enumerate(
            ((south, east), (south, west), (north, east), (north, west))
        )
    ]
    for copy in corner_copies:
        copy.start()
    tab_ref[0] = own
    for copy in table_copies:
        copy.wait()
    for q in range(4):
        tab_ref[q + 1] = tables[q]
    for copy in corner_copies:
        copy.wait()
    q = iota((4, 32, 256), 0)
    keep = ((q >= 2) | (q * 0 + band > 0)) & ((q < 2) | (q * 0 + band < lats - 1))
    cor_ref[...] = jnp.where(keep, corners[...].astype(F32), 0.0).astype(BF16).reshape(128, 256)
    for phase, source, target in ((0, ask, asked), (1, reply, replied), (2, give, given)):
        all_of(source, target, phase).wait_send()


def exchange_call(sizes, *operands):
    lons, lats, levels, rows, lanes, records, channels = sizes
    half, slots = 144, lons * 8
    wide = 8 * 2 * levels
    vmem = pl.BlockSpec(memory_space=pltpu.VMEM)
    hbm = pl.BlockSpec(memory_space=pl.ANY)
    return pl.pallas_call(
        functools.partial(exchange_kernel, sizes),
        out_shape=(
            jax.ShapeDtypeStruct((5, half, slots), BF16),
            jax.ShapeDtypeStruct((128, 256), BF16),
            jax.ShapeDtypeStruct((slots, 16), F32),
        ),
        in_specs=[hbm, hbm] + [vmem] * 6,
        out_specs=(vmem, vmem, vmem),
        scratch_shapes=[
            pltpu.VMEM((2 * levels * rows, lanes), F32),
            pltpu.VMEM((2, half, rows * lanes), BF16),
            pltpu.VMEM((records * 2 * levels, channels), BF16),
            pltpu.VMEM((512, wide), BF16),
            pltpu.VMEM((records, wide), F32),
            pltpu.VMEM((records, channels), F32),
            pltpu.VMEM((lons, 1, 2 * slots), F32),
            pltpu.VMEM((lons, 1, 2 * slots), F32),
            pltpu.VMEM((lons, 8, 256), BF16),
            pltpu.VMEM((lons, 8, 256), BF16),
            pltpu.VMEM((lons, 8, 256), BF16),
            pltpu.VMEM((lons, 8, 256), BF16),
            pltpu.VMEM((half, slots), BF16),
            pltpu.VMEM((4, half, slots), BF16),
            pltpu.VMEM((4, 32, 256), BF16),
            pltpu.VMEM((4, 32, 256), BF16),
            pltpu.VMEM((1, 2 * slots), F32),
            pltpu.VMEM((4, 1, 2 * slots), F32),
            pltpu.SemaphoreType.DMA((2,)),
            pltpu.SemaphoreType.DMA((3,)),
            pltpu.SemaphoreType.DMA((3,)),
            pltpu.SemaphoreType.DMA((12,)),
            pltpu.SemaphoreType.DMA((12,)),
        ],
        compiler_params=pltpu.CompilerParams(
            collective_id=0, has_side_effects=True, vmem_limit_bytes=48 << 20
        ),
        name="exchange",
    )(*operands)


def grid_kernel(rows, halo, lanes, chunk, tab_ref, cor_ref, pos_ref, tap_ref, out_ref, x_ref, d_ref):
    half = tab_ref.shape[1]
    slots = tab_ref.shape[2]
    tall = rows + 2 * halo
    packed = d_ref.shape[1]
    wide = 2 * halo

    @pl.when((pl.program_id(0) == 0) & (pl.program_id(1) == 0))
    def _():
        which = (lax.broadcasted_iota(jnp.int32, (half, slots), 1) // 4) % 2

        def stacked(index):
            table = tab_ref[index].astype(F32)
            return jnp.concatenate(
                [jnp.where(which == v, table, 0.0) for v in range(2)], axis=0
            ).astype(BF16)

        own, up, down = stacked(0), stacked(1), stacked(2)
        left, right = stacked(3), stacked(4)

        def spread(table, index, start, count):
            at = (iota((slots, count), 1) + start).astype(F32)
            hot = jnp.where(pos_ref[:, index : index + 1] == at, 1.0, 0.0).astype(BF16)
            return jnp.dot(table, hot, preferred_element_type=F32)

        x_ref[:, 0 : halo * lanes] = spread(up, 1, 0, halo * lanes)
        x_ref[:, (rows + halo) * lanes : tall * lanes] = spread(
            down, 2, (rows + halo) * lanes, halo * lanes
        )

        @pl.loop(0, rows * lanes // chunk)
        def _(step):
            start = pl.multiple_of(step * chunk + halo * lanes, chunk)
            x_ref[:, pl.ds(start, chunk)] = spread(own, 0, start, chunk)

        at = iota((slots, packed), 1).astype(F32)
        total = jnp.zeros((2 * half, packed), F32)
        for index, table in enumerate((own, up, down, left, right)):
            sign = -1.0 if index < 3 else 1.0
            hot = jnp.where(pos_ref[:, 5 + index : 6 + index] == at, sign, 0.0).astype(BF16)
            total = total + jnp.dot(table, hot, preferred_element_type=F32)
        crow = lax.broadcasted_iota(jnp.int32, (cor_ref.shape[0], packed), 0)
        cat = lax.broadcasted_iota(jnp.int32, (cor_ref.shape[0], packed), 1)
        c, i, j = crow // 32, (crow // 4) % 4, crow % 4
        spot = ((c // 2) * (rows + halo) + i) * wide + (c % 2) * halo + j
        hot = jnp.where(spot == cat, 1.0, 0.0).astype(BF16)
        cv = (lax.broadcasted_iota(jnp.int32, cor_ref.shape, 0) // 16) % 2
        for v in range(2):
            part = jnp.where(cv == v, cor_ref[...].astype(F32), 0.0).astype(BF16)
            got = lax.dot_general(
                part, hot, (((0,), (0,)), ((), ())), preferred_element_type=F32
            )
            d_ref[v * half : (v + 1) * half, :] = (
                total[v * half : (v + 1) * half] + got[0:half]
            )

    base = pl.multiple_of((pl.program_id(0) * pl.num_programs(1) + pl.program_id(1)) * 8, 8)
    lane = lax.broadcasted_iota(jnp.int32, (8, lanes), 1)
    place = lane % wide
    taps = tap_ref[pl.ds(base, 8), :]
    lon = [jnp.broadcast_to(taps[:, k : k + 1], (8, lanes)) for k in range(9)]
    lat = [jnp.broadcast_to(taps[:, 9 + k : 10 + k], (8, lanes)) for k in range(9)]
    fixes = []
    for q in range(packed // lanes):
        d = d_ref[pl.ds(base, 8), q * lanes : (q + 1) * lanes]
        fix = jnp.zeros((8, lanes), F32)
        for k in range(9):
            shift = k - halo
            if shift == 0:
                continue
            if shift > 0:
                reach = (place < halo) & (place + shift >= halo)
            else:
                reach = (place >= halo) & (place + shift < halo)
            fix = fix + jnp.where(reach, lon[k], 0.0) * pltpu.roll(d, (-shift) % lanes, 1)
        fixes.append(fix)
    rim = (lane < halo) | (lane >= lanes - halo)
    along = []
    for i in range(tall):
        x = x_ref[pl.ds(base, 8), i * lanes : (i + 1) * lanes]
        row = lon[halo] * x
        for k in range(9):
            shift = k - halo
            if shift != 0:
                row = row + lon[k] * pltpu.roll(x, (-shift) % lanes, 1)
        q, r = divmod(i * wide, lanes)
        fix = pltpu.roll(fixes[q], (-(r + halo)) % lanes, 1)
        along.append(row + jnp.where(rim, fix, 0.0))
        if i >= 2 * halo:
            out = lat[0] * along[i - 8]
            for k in range(1, 9):
                out = out + lat[k] * along[i - 8 + k]
            out_ref[0, :, i - 8, :] = out


def grid_call(tables, corners, pos, taps, levels, rows, lanes):
    halo = 4
    half = tables.shape[1]
    tall = rows + 2 * halo
    packed = -(-tall * 2 * halo // lanes) * lanes
    whole = lambda array: pl.BlockSpec(array.shape, lambda v, b: (0,) * array.ndim)
    return pl.pallas_call(
        functools.partial(grid_kernel, rows, halo, lanes, 512),
        out_shape=jax.ShapeDtypeStruct((2, levels, rows, lanes), F32),
        grid=(2, half // 8),
        in_specs=[whole(tables), whole(corners), whole(pos), whole(taps)],
        out_specs=pl.BlockSpec((1, 8, rows, lanes), lambda v, b: (v, b, 0, 0)),
        scratch_shapes=[
            pltpu.VMEM((2 * half, tall * lanes), F32),
            pltpu.VMEM((2 * half, packed), F32),
        ],
        compiler_params=pltpu.CompilerParams(vmem_limit_bytes=40 << 20),
        name="grid",
    )(tables, corners, pos, taps)


def body(
    state_field,
    jacobian,
    observed,
    inverse_var,
    valid_count,
    destination,
    column,
    vertical,
    lon_taps,
    lat_taps,
):
    variables, levels, rows, lanes = state_field.shape
    records, channels = jacobian.shape[1], jacobian.shape[-1]
    sizes = (
        lax.axis_size("lon"), lax.axis_size("lat"), levels, rows, lanes, records, channels,
    )
    turned = jnp.pad(
        vertical.transpose(0, 2, 1), ((0, 0), (0, 144 - levels), (0, 256 - levels))
    ).reshape(288, 256)
    tables, corners, pos = exchange_call(
        sizes,
        state_field.reshape(variables * levels * rows, lanes),
        jacobian.transpose(0, 1, 3, 2, 4).reshape(records * levels * variables, channels),
        observed.reshape(records, channels),
        inverse_var.reshape(records, channels),
        valid_count.reshape(1, records),
        destination.reshape(1, records),
        column.reshape(1, records),
        turned,
    )
    taps = jnp.concatenate([lon_taps, lat_taps], axis=2)
    taps = jnp.pad(taps, ((0, 0), (0, 144 - levels), (0, 0))).reshape(288, 18)
    return grid_call(tables, corners, pos, taps, levels, rows, lanes)


def solution(mesh):
    placed = (
        P(None, None, "lat", "lon"),
        P("lat", "lon", None, None, None),
        P("lat", "lon", None),
        P("lat", "lon", None),
        P("lat", "lon"),
        P("lat", "lon", None),
        P("lat", "lon"),
        P(),
        P(),
        P(),
    )
    return jax.shard_map(
        body, mesh=mesh, in_specs=placed, out_specs=P(None, None, "lat", "lon"), check_vma=False
    )
```

```python
import functools

import jax
import jax.numpy as jnp
from jax import lax
from jax.experimental import pallas as pl
from jax.experimental.pallas import tpu as pltpu
from jax.sharding import PartitionSpec as P

F32 = jnp.float32
BF16 = jnp.bfloat16


MESH = pl.DeviceIdType.MESH
NT = (((1,), (1,)), ((), ()))
TN = (((0,), (0,)), ((), ()))


def iota(shape, dim):
    return lax.broadcasted_iota(jnp.int32, shape, dim)


def exchange_kernel(
    sizes,
    state_hbm, jac_hbm, obs_hbm, inv_hbm, count_hbm, dest_hbm, col_hbm, vert_hbm, lon_hbm, lat_hbm,
    tab_ref, cor_ref, pos_ref, tap_ref,
    state_ref, low_ref, jac_ref, map_ref, bd_ref, model_ref,
    obs_ref, inv_ref, count_ref, dest_ref, col_ref, vert_ref, lon_ref, lat_ref, square_ref, mix_ref,
    ask, asked, reply, replied, give, given,
    table, tables, corner, corners, spot, spots,
    load_sem, a2a_send, a2a_recv, near_send, near_recv,
):
    lons, lats, levels, rows, lanes, records, channels = sizes
    half = low_ref.shape[1]
    slots = 2 * table.shape[1]
    points = table.shape[1]
    wide = map_ref.shape[1]
    feats = 2 * levels
    me = lax.axis_index("lon")
    band = lax.axis_index("lat")
    east, west = lax.rem(me + 1, lons), lax.rem(me + lons - 1, lons)
    south, north = lax.rem(band + 1, lats), lax.rem(band + lats - 1, lats)

    loads = [
        pltpu.make_async_copy(source, target, load_sem.at[q])
        for q, (source, target) in enumerate(
            (
                (dest_hbm, dest_ref), (col_hbm, col_ref), (count_hbm, count_ref),
                (vert_hbm, vert_ref), (lon_hbm, lon_ref), (lat_hbm, lat_ref),
                (obs_hbm, obs_ref), (inv_hbm, inv_ref),
                (state_hbm, state_ref), (jac_hbm, jac_ref),
            )
        )
    ]
    for load in loads:
        load.start()

    barrier = pltpu.get_barrier_semaphore()

    @pl.loop(1, lons)
    def _(step):
        peer = lax.rem(me + step, lons)
        pl.semaphore_signal(barrier, inc=1, device_id={"lon": peer}, device_id_type=MESH)

    for there in (north, south):
        pl.semaphore_signal(barrier, inc=1, device_id={"lat": there}, device_id_type=MESH)
        for side in (west, east):
            pl.semaphore_signal(
                barrier, inc=1, device_id={"lat": there, "lon": side}, device_id_type=MESH
            )

    for load in loads[:3]:
        load.wait()
    drow = dest_ref[...].astype(F32)
    prow = col_ref[...]
    irow = (prow // lanes).astype(F32)
    jrow = (prow % lanes).astype(F32)
    krow = count_ref[...].astype(F32)
    eye = iota((records, records), 0) == iota((records, records), 1)

    def column_of(row):
        return jnp.sum(jnp.where(eye, row, 0.0), axis=1, keepdims=True)

    dcol, icol, jcol, kcol = (column_of(row) for row in (drow, irow, jrow, krow))
    same = dcol == drow
    before = iota((records, records), 1) < iota((records, records), 0)
    after = iota((records, records), 0) < iota((records, records), 1)
    rank_col = jnp.sum(jnp.where(same & before, 1.0, 0.0), axis=1, keepdims=True)
    rank_row = jnp.sum(jnp.where(same & after, 1.0, 0.0), axis=0, keepdims=True)

    lane = iota((records, 3 * slots), 1)
    fine = lane < 2 * slots
    owner = jnp.where(fine, (lane % slots) // 8, (lane % points) // 4)
    mine = (owner == me) & ((lane % 4).astype(F32) == rank_col)
    first = (fine & (lane < slots)) | ((lane >= 2 * slots) & (lane < 2 * slots + points))
    value = jnp.where(first, icol + 1.0, jcol)
    values = jnp.where(mine, value, 0.0).astype(BF16)
    toward = jnp.where(iota((lons, records), 0).astype(F32) == drow, 1.0, 0.0).astype(BF16)
    asks = jnp.dot(toward, values, preferred_element_type=F32)
    ask[...] = asks.reshape(lons, 1, 3 * slots)

    pl.semaphore_wait(barrier, lons - 1 + 6)

    def send_all(source, target, phase):
        @pl.loop(1, lons)
        def _(step):
            peer = lax.rem(me + step, lons)
            pltpu.make_async_remote_copy(
                src_ref=source.at[peer],
                dst_ref=target.at[me],
                send_sem=a2a_send.at[phase],
                recv_sem=a2a_recv.at[phase],
                device_id={"lon": peer},
                device_id_type=MESH,
            ).start()

        target[me] = source[me]

    def all_of(source, target, phase):
        return pltpu.make_async_remote_copy(
            src_ref=source.at[pl.ds(0, lons - 1)],
            dst_ref=target.at[pl.ds(0, lons - 1)],
            send_sem=a2a_send.at[phase],
            recv_sem=a2a_recv.at[phase],
            device_id={"lon": east},
            device_id_type=MESH,
        )

    send_all(ask, asked, 0)

    reply[...] = jnp.zeros(reply.shape, BF16)
    loads[8].wait()
    for v in range(2):
        low_ref[v, half - 16 : half, :] = jnp.zeros((16, rows * lanes), BF16)

        @pl.loop(0, rows)
        def _(i):
            plane = state_ref[pl.ds(v * levels * rows + i, levels, stride=rows), :]
            start = pl.multiple_of(i * lanes, lanes)
            low_ref[v, 0:levels, pl.ds(start, lanes)] = plane.astype(BF16)

    n = iota((1, wide), 1)
    record_of = jnp.zeros((1, wide), jnp.int32)
    for q in range(1, wide // feats):
        record_of = record_of + jnp.where(n >= q * feats, 1, 0)
    feature = n - feats * record_of
    for v in range(2):
        level = iota((256, wide), 0)
        hit = (feature == 2 * level + v) & (level < levels)
        map_ref[v * 256 : (v + 1) * 256, :] = jnp.where(hit, 1.0, 0.0).astype(BF16)

    for load in loads[3:6]:
        load.wait()
    for v in range(2):
        square_ref[...] = jnp.zeros(square_ref.shape, F32)
        square_ref[0:levels, 0:levels] = vert_ref[...].astype(F32)[:, v, :]
        mix_ref[v * half : (v + 1) * half, :] = jnp.transpose(square_ref[...])[0:half].astype(BF16)
        square_ref[0:9, 0:levels] = lon_ref[...][:, v, :]
        square_ref[16:25, 0:levels] = lat_ref[...][:, v, :]
        tap_ref[v * half : (v + 1) * half, :] = jnp.transpose(square_ref[0:128, :])[0:half, 0:32]

    all_of(ask, asked, 0).wait_recv()
    seen = jnp.sum(asked[...], axis=0)
    iseen, jseen = seen[:, 0:slots], seen[:, slots : 2 * slots]
    spot[...] = seen[:, 2 * slots : 3 * slots]
    neighbours = (
        ({"lat": north}, 2), ({"lat": south}, 1), ({"lon": east}, 3), ({"lon": west}, 4),
    )

    def near(source, target, target_index, sem, device):
        return pltpu.make_async_remote_copy(
            src_ref=source,
            dst_ref=target.at[target_index],
            send_sem=near_send.at[sem],
            recv_sem=near_recv.at[sem],
            device_id=device,
            device_id_type=MESH,
        )

    spot_copies = [
        near(spot, spots, index - 1, index - 1, device) for device, index in neighbours
    ]
    for copy in spot_copies:
        copy.start()

    prow_slots = jnp.where(iseen > 0.0, (iseen - 1.0) * lanes + jseen, -1.0)
    pcol = jnp.transpose(jnp.broadcast_to(prow_slots, (8, slots)))[:, 0:1]

    chunk = 512
    got = [jnp.zeros((slots, half), F32) for _ in range(2)]
    for c in range(rows * lanes // chunk):
        at = (iota((slots, chunk), 1) + c * chunk).astype(F32)
        hot = jnp.where(pcol == at, 1.0, 0.0).astype(BF16)
        for v in range(2):
            got[v] = got[v] + lax.dot_general(
                hot, low_ref[v, :, c * chunk : (c + 1) * chunk], NT, preferred_element_type=F32
            )
    var_row = (iota((slots, half), 0) // 4) % 2
    states = jnp.where(var_row == 0, got[0], got[1])
    reply[:, :, 0:half] = states.reshape(lons, 8, half).astype(BF16)
    send_all(reply, replied, 1)

    for load in (loads[6], loads[7], loads[9]):
        load.wait()
    all_of(reply, replied, 1).wait_recv()
    answers = replied[...].astype(F32).reshape(slots, 256).astype(BF16)
    slane = iota((records, slots), 1)
    hit = ((slane // 8).astype(F32) == dcol) & ((slane % 4).astype(F32) == rank_col)
    bd = jnp.zeros((records, wide), F32)
    for v in range(2):
        take = jnp.where(hit & ((slane // 4) % 2 == v), 1.0, 0.0).astype(BF16)
        picked = jnp.dot(take, answers, preferred_element_type=F32).astype(BF16)
        bd = bd + jnp.dot(
            picked, map_ref[v * 256 : (v + 1) * 256, :], preferred_element_type=F32
        )
    own_block = record_of == iota((records, wide), 0) % 8
    bd_ref[...] = jnp.where(own_block, bd, 0.0)
    for g in range(records // 8):
        model_ref[g * 8 : (g + 1) * 8, :] = jnp.dot(
            bd_ref[g * 8 : (g + 1) * 8, :].astype(BF16),
            jac_ref[g * wide : (g + 1) * wide, :],
            preferred_element_type=F32,
        )
    alive = iota((records, channels), 1).astype(F32) < kcol
    weight = jnp.where(alive, inv_ref[...].astype(F32), 0.0)
    model_ref[...] = weight * (model_ref[...] - obs_ref[...].astype(F32))
    for g in range(records // 8):
        bd_ref[g * 8 : (g + 1) * 8, :] = lax.dot_general(
            model_ref[g * 8 : (g + 1) * 8, :].astype(BF16),
            jac_ref[g * wide : (g + 1) * wide, :],
            NT,
            preferred_element_type=F32,
        )
    terms = jnp.where(own_block, bd_ref[...], 0.0).astype(BF16)
    srow = iota((slots, records), 0)
    hit = ((srow // 8).astype(F32) == drow) & ((srow % 4).astype(F32) == rank_row)
    gives = jnp.zeros((slots, 256), F32)
    for v in range(2):
        term = lax.dot_general(
            terms, map_ref[v * 256 : (v + 1) * 256, :], NT, preferred_element_type=F32
        ).astype(BF16)
        put = jnp.where(hit & ((srow // 4) % 2 == v), 1.0, 0.0).astype(BF16)
        gives = gives + jnp.dot(put, term, preferred_element_type=F32)
    give[...] = gives.reshape(lons, 8, 256).astype(BF16)
    send_all(give, given, 2)

    for copy in spot_copies:
        copy.wait()
    shifts = (4, 4 - rows, 4 + rows, 4, 4)
    stack = []
    for q in range(5):
        both = spot[...] if q == 0 else spots[q - 1]
        i1, j = both[:, 0:points], both[:, points : 2 * points]
        i = i1 - 1.0 + shifts[q]
        good = (i1 > 0.0) & (i >= 0.0) & (i < rows + 8.0)
        if q == 1:
            good = good & (iota((1, points), 0) + band > 0)
        if q == 2:
            good = good & (iota((1, points), 0) + band < lats - 1)
        stack += [jnp.where(good, i, -1000.0), j]
    pos_ref[...] = jnp.transpose(jnp.concatenate(stack + stack[:6], axis=0))

    all_of(give, given, 2).wait_recv()
    terms_in = given[...].astype(F32).reshape(slots, 256).astype(BF16)
    s = iota((points, slots), 0)
    wanted = iota((points, slots), 1) - ((s // 4) * 8 + s % 4)
    parts = []
    for v in range(2):
        take = jnp.where(wanted == 4 * v, 1.0, 0.0).astype(BF16)
        term = jnp.dot(take, terms_in, preferred_element_type=F32).astype(BF16)
        parts.append(
            lax.dot_general(
                mix_ref[v * half : (v + 1) * half, :], term, NT, preferred_element_type=F32
            )
        )
    own = jnp.concatenate(parts, axis=0).astype(BF16)
    table[...] = own
    table_copies = [
        near(table, tables, index - 1, 3 + index, device) for device, index in neighbours
    ]
    for copy in table_copies:
        copy.start()
    r = iota((128, points), 0)
    c, v, i, j = r // 32, (r // 16) % 2, (r // 4) % 4, r % 4
    at_i = jnp.where(c < 2, rows - 4, 0) + i
    at_j = jnp.where(c % 2 == 0, lanes - 4, 0) + j
    both = spot[...]
    hot = (both[:, 0:points] == (at_i + 1).astype(F32)) & (both[:, points:] == at_j.astype(F32))
    cut = jnp.zeros((128, half), F32)
    for var in range(2):
        pick = jnp.where(hot & (v == var), 1.0, 0.0).astype(BF16)
        cut = cut + lax.dot_general(
            pick, own[var * half : (var + 1) * half], NT, preferred_element_type=F32
        )
    cut = jnp.concatenate([cut, jnp.zeros((128, 256 - half), F32)], axis=1)
    corner[...] = cut.reshape(4, 32, 256).astype(BF16)
    corner_copies = [
        near(corner.at[q], corners, q, 8 + q, {"lat": there, "lon": side})
        for q, (there, side) in enumerate(
            ((south, east), (south, west), (north, east), (north, west))
        )
    ]
    for copy in corner_copies:
        copy.start()
    tab_ref[0] = own
    for copy in table_copies:
        copy.wait()
    for q in range(4):
        tab_ref[q + 1] = tables[q]
    for copy in corner_copies:
        copy.wait()
    q = iota((4, 32, 256), 0)
    keep = ((q >= 2) | (q * 0 + band > 0)) & ((q < 2) | (q * 0 + band < lats - 1))
    cor_ref[...] = jnp.where(keep, corners[...].astype(F32), 0.0).astype(BF16).reshape(128, 256)
    for phase, source, target in ((0, ask, asked), (1, reply, replied), (2, give, given)):
        all_of(source, target, phase).wait_send()


def exchange_call(sizes, *operands):
    lons, lats, levels, rows, lanes, records, channels = sizes
    half, slots = 144, lons * 8
    wide = 8 * 2 * levels
    points = slots // 2
    vmem = pl.BlockSpec(memory_space=pltpu.VMEM)
    hbm = pl.BlockSpec(memory_space=pltpu.HBM)
    return pl.pallas_call(
        functools.partial(exchange_kernel, sizes),
        out_shape=(
            jax.ShapeDtypeStruct((5, 2 * half, points), BF16),
            jax.ShapeDtypeStruct((128, 256), BF16),
            jax.ShapeDtypeStruct((points, 16), F32),
            jax.ShapeDtypeStruct((2 * half, 32), F32),
        ),
        in_specs=[hbm] * 10,
        out_specs=(vmem, vmem, vmem, vmem),
        scratch_shapes=[
            pltpu.VMEM((2 * levels * rows, lanes), F32),
            pltpu.VMEM((2, half, rows * lanes), BF16),
            pltpu.VMEM((records * 2 * levels, channels), BF16),
            pltpu.VMEM((512, wide), BF16),
            pltpu.VMEM((records, wide), F32),
            pltpu.VMEM((records, channels), F32),
            pltpu.VMEM((records, channels), BF16),
            pltpu.VMEM((records, channels), BF16),
            pltpu.VMEM((1, records), jnp.int32),
            pltpu.VMEM((1, records), jnp.int32),
            pltpu.VMEM((1, records), jnp.int32),
            pltpu.VMEM((levels, 2, levels), BF16),
            pltpu.VMEM((9, 2, levels), F32),
            pltpu.VMEM((9, 2, levels), F32),
            pltpu.VMEM((256, 256), F32),
            pltpu.VMEM((2 * half, 256), BF16),
            pltpu.VMEM((lons, 1, 3 * slots), F32),
            pltpu.VMEM((lons, 1, 3 * slots), F32),
            pltpu.VMEM((lons, 8, 256), BF16),
            pltpu.VMEM((lons, 8, 256), BF16),
            pltpu.VMEM((lons, 8, 256), BF16),
            pltpu.VMEM((lons, 8, 256), BF16),
            pltpu.VMEM((2 * half, points), BF16),
            pltpu.VMEM((4, 2 * half, points), BF16),
            pltpu.VMEM((4, 32, 256), BF16),
            pltpu.VMEM((4, 32, 256), BF16),
            pltpu.VMEM((1, slots), F32),
            pltpu.VMEM((4, 1, slots), F32),
            pltpu.SemaphoreType.DMA((10,)),
            pltpu.SemaphoreType.DMA((3,)),
            pltpu.SemaphoreType.DMA((3,)),
            pltpu.SemaphoreType.DMA((12,)),
            pltpu.SemaphoreType.DMA((12,)),
        ],
        compiler_params=pltpu.CompilerParams(
            collective_id=0, has_side_effects=True, vmem_limit_bytes=48 << 20
        ),
        name="exchange",
    )(*[pltpu.with_memory_space_constraint(x, pltpu.HBM) for x in operands])


def rim_lane(e, lanes, halo):
    return jnp.where(e < halo, lanes - halo + e, e - halo)


def grid_kernel(
    rows, halo, lanes, levels,
    tab_ref, cor_ref, pos_ref, tap_ref, out_hbm,
    lhs_ref, hot_ref, fix_ref, lat_ref, along_ref, out_ref, sem,
):
    size = tab_ref.shape[1]
    half = size // 2
    slots = tab_ref.shape[2]
    tall = rows + 2 * halo
    packed = fix_ref.shape[1]
    taps = 2 * halo + 1
    group = lanes // (2 * halo)

    def tap(k):
        return jnp.broadcast_to(tap_ref[:, k : k + 1], (size, slots))

    lon = [tap(k) for k in range(taps)]
    for index in range(3):
        table = tab_ref[index].astype(F32)
        for k in range(taps):
            lhs_ref[index, :, k * slots : (k + 1) * slots] = (lon[k] * table).astype(BF16)
    for k in range(taps):
        lat_ref[k] = tap(16 + k)

    total = jnp.zeros((size, packed), F32)
    at = iota((slots, packed), 1).astype(F32)
    for index in (3, 4):
        table = tab_ref[index].astype(F32)
        i = pos_ref[:, 2 * index : 2 * index + 1]
        j = pos_ref[:, 2 * index + 1 : 2 * index + 2]
        for q in range(halo):
            k = q if index == 3 else q + halo + 1
            if index == 3:
                e = j - (lanes - 2 * halo) - k
                good = (j >= lanes - halo) & (e >= halo)
            else:
                e = j + 2 * halo - k
                good = (j < halo) & (e < halo)
            spot = jnp.where(good & (i >= 0.0), i * (2.0 * halo) + e, -1.0)
            hot = jnp.where(spot == at, 1.0, 0.0).astype(BF16)
            total = total + jnp.dot(
                (lon[k] * table).astype(BF16), hot, preferred_element_type=F32
            )
    turned = jnp.transpose(cor_ref[...].astype(F32))[0:half]
    lane = iota((half, slots), 1)
    turned = jnp.concatenate(
        [jnp.where((lane // 16) % 2 == v, turned, 0.0) for v in range(2)], axis=0
    )
    row = iota((slots, packed), 0)
    c, i, j = row // 32, (row // 4) % 4, row % 4
    leftward = (iota((size, slots), 1) // 32) % 2 == 0
    for q in range(halo):
        e = jnp.where(c % 2 == 0, halo + j - q, j + halo - 1 - q)
        least = jnp.where(c % 2 == 0, halo, 0)
        good = (e >= least) & (e < least + halo)
        spot = jnp.where(good, ((c // 2) * (rows + halo) + i) * (2 * halo) + e, -1)
        hot = jnp.where(spot == iota((slots, packed), 1), 1.0, 0.0).astype(BF16)
        scale = jnp.where(leftward, lon[q], lon[q + halo + 1])
        total = total + jnp.dot((scale * turned).astype(BF16), hot, preferred_element_type=F32)
    fix_ref[...] = total.astype(BF16)

    lane = iota((slots, lanes), 1)
    for index in range(3):
        j = pos_ref[:, 2 * index + 1 : 2 * index + 2]
        for k in range(taps):
            hit = (lane + (k - halo)).astype(F32) == j
            hot_ref[index, k * slots : (k + 1) * slots, :] = jnp.where(hit, 1.0, 0.0).astype(BF16)
    e = iota((slots, lanes), 0) % (2 * halo)
    place = jnp.where(lane == rim_lane(e, lanes, halo), 1.0, 0.0).astype(BF16)
    turn = iota((slots, lanes), 0) // (2 * halo)
    rows_of = [
        jnp.broadcast_to(pos_ref[:, 2 * index : 2 * index + 1], (slots, lanes))
        for index in range(3)
    ]

    def spread(pair):
        index = 1 if pair < halo // 2 else 2 if pair >= (rows + halo) // 2 else 0
        columns = []
        for i in (2 * pair, 2 * pair + 1):
            here = jnp.where(rows_of[index] == float(i), 1.0, 0.0).astype(BF16)
            parts = [
                hot_ref[index, k * slots : (k + 1) * slots, :] * here for k in range(taps)
            ]
            there = jnp.where(turn == i % group, 1.0, 0.0).astype(BF16)
            columns.append(jnp.concatenate(parts + [place * there], axis=0))
        q = (2 * pair) // group
        left = jnp.concatenate(
            [lhs_ref[index], fix_ref[:, q * lanes : (q + 1) * lanes]], axis=1
        )
        along_ref[:, 2 * pair * lanes : (2 * pair + 2) * lanes] = jnp.dot(
            left, jnp.concatenate(columns, axis=1), preferred_element_type=F32
        )

    flat = out_ref.reshape(size * rows, lanes)

    def filter_rows(block, base):
        lat = [lat_ref[k, base : base + 8, :] for k in range(taps)]
        start = block * 8
        along = [
            along_ref[base : base + 8, i * lanes : (i + 1) * lanes]
            for i in range(start, start + 8 + 2 * halo)
        ]
        for r in range(8):
            out = lat[0] * along[r]
            for k in range(1, taps):
                out = out + lat[k] * along[r + k]
            flat[pl.ds(base * rows + start + r, 8, stride=rows), :] = out

    copies = []
    for pair in range(8):
        spread(pair)
    for block in range(rows // 8):
        ahead = range(8 + 4 * block, min(12 + 4 * block, tall // 2))
        for piece in range(4):
            if piece < len(ahead):
                spread(ahead[piece])
            for base in range(piece * size // 4, (piece + 1) * size // 4, 8):
                filter_rows(block, base)
        copy = pltpu.make_async_copy(
            out_ref.at[:, pl.ds(0, levels), pl.ds(block * 8, 8), :],
            out_hbm.at[:, :, pl.ds(block * 8, 8), :],
            sem.at[block],
        )
        copy.start()
        copies.append(copy)
    for copy in copies:
        copy.wait()


def grid_call(tables, corners, pos, taps, levels, rows, lanes):
    halo = 4
    size, slots = tables.shape[1:]
    tall = rows + 2 * halo
    packed = -(-tall * 2 * halo // lanes) * lanes
    vmem = pl.BlockSpec(memory_space=pltpu.VMEM)
    return pl.pallas_call(
        functools.partial(grid_kernel, rows, halo, lanes, levels),
        out_shape=jax.ShapeDtypeStruct((2, levels, rows, lanes), F32),
        in_specs=[vmem] * 4,
        out_specs=pl.BlockSpec(memory_space=pl.ANY),
        scratch_shapes=[
            pltpu.VMEM((3, size, 9 * slots), BF16),
            pltpu.VMEM((3, 9 * slots, lanes), BF16),
            pltpu.VMEM((size, packed), BF16),
            pltpu.VMEM((9, size, lanes), F32),
            pltpu.VMEM((size, tall * lanes), F32),
            pltpu.VMEM((2, size // 2, rows, lanes), F32),
            pltpu.SemaphoreType.DMA((rows // 8,)),
        ],
        compiler_params=pltpu.CompilerParams(vmem_limit_bytes=40 << 20),
        name="grid",
    )(tables, corners, pos, taps)


def body(
    state_field,
    jacobian,
    observed,
    inverse_var,
    valid_count,
    destination,
    column,
    vertical,
    lon_taps,
    lat_taps,
):
    variables, levels, rows, lanes = state_field.shape
    records, channels = jacobian.shape[1], jacobian.shape[-1]
    sizes = (
        lax.axis_size("lon"), lax.axis_size("lat"), levels, rows, lanes, records, channels,
    )
    tables, corners, pos, taps = exchange_call(
        sizes,
        state_field.reshape(variables * levels * rows, lanes),
        jacobian.transpose(0, 1, 3, 2, 4).reshape(records * levels * variables, channels),
        observed.reshape(records, channels),
        inverse_var.reshape(records, channels),
        valid_count.reshape(1, records),
        destination.reshape(1, records),
        column.reshape(1, records),
        vertical.transpose(1, 0, 2),
        lon_taps.transpose(2, 0, 1),
        lat_taps.transpose(2, 0, 1),
    )
    return grid_call(tables, corners, pos, taps, levels, rows, lanes)


def solution(mesh):
    placed = (
        P(None, None, "lat", "lon"),
        P("lat", "lon", None, None, None),
        P("lat", "lon", None),
        P("lat", "lon", None),
        P("lat", "lon"),
        P("lat", "lon", None),
        P("lat", "lon"),
        P(),
        P(),
        P(),
    )
    return jax.shard_map(
        body, mesh=mesh, in_specs=placed, out_specs=P(None, None, "lat", "lon"), check_vma=False
    )
```

```python
import functools

import jax
import jax.numpy as jnp
from jax import lax
from jax.experimental import pallas as pl
from jax.experimental.pallas import tpu as pltpu
from jax.sharding import PartitionSpec as P

F32 = jnp.float32
BF16 = jnp.bfloat16


MESH = pl.DeviceIdType.MESH
NT = (((1,), (1,)), ((), ()))
TN = (((0,), (0,)), ((), ()))


def iota(shape, dim):
    return lax.broadcasted_iota(jnp.int32, shape, dim)


def far_first(ring):
    steps = [
        (z, x, c) for z in range(ring[0]) for x in range(ring[1]) for c in range(ring[2])
    ][1:]
    return sorted(
        steps, key=lambda s: -(min(s[0], ring[0] - s[0]) + min(s[1], ring[1] - s[1]) + 0.5 * s[2])
    )


def peer_at(me, step, ring):
    z, x, c = me // (ring[1] * ring[2]), (me // ring[2]) % ring[1], me % ring[2]
    z, x, c = (lax.rem(at + go, size) for at, go, size in zip((z, x, c), step, ring))
    return (z * ring[1] + x) * ring[2] + c


def exchange_kernel(
    sizes,
    state_hbm, jac_hbm, obs_hbm, inv_hbm, count_hbm, dest_hbm, col_hbm, vert_hbm, lon_hbm, lat_hbm,
    tab_ref, cor_ref, pos_ref, lon_tap, lat_tap, along_ref,
    state_ref, low_ref, jac_ref, map_ref, bd_ref, model_ref,
    obs_ref, inv_ref, count_ref, dest_ref, col_ref, vert_ref, lon_ref, lat_ref, square_ref, mix_ref, tap_ref, lhs_ref, hot_ref, row_ref, pick_ref,
    ask, asked, reply, replied, give, given,
    table, tables, corner, corners, spot, spots,
    load_sem, a2a_send, a2a_recv, near_send, near_recv,
):
    lons, lats, levels, rows, lanes, records, channels = sizes
    ring = (lons // 8, 4, 2)
    half = low_ref.shape[1]
    slots = 2 * table.shape[1]
    points = table.shape[1]
    wide = map_ref.shape[1]
    feats = 2 * levels
    me = lax.axis_index("lon")
    band = lax.axis_index("lat")
    east, west = lax.rem(me + 1, lons), lax.rem(me + lons - 1, lons)
    south, north = lax.rem(band + 1, lats), lax.rem(band + lats - 1, lats)

    loads = [
        pltpu.make_async_copy(source, target, load_sem.at[q])
        for q, (source, target) in enumerate(
            (
                (dest_hbm, dest_ref), (col_hbm, col_ref), (count_hbm, count_ref),
                (vert_hbm, vert_ref), (lon_hbm, lon_ref), (lat_hbm, lat_ref),
                (obs_hbm, obs_ref), (inv_hbm, inv_ref),
                (state_hbm, state_ref), (jac_hbm, jac_ref),
            )
        )
    ]
    for load in loads:
        load.start()

    barrier = pltpu.get_barrier_semaphore()
    peers = [peer_at(me, step, ring) for step in far_first(ring)]
    for peer in peers:
        pl.semaphore_signal(barrier, inc=1, device_id={"lon": peer}, device_id_type=MESH)

    for there in (north, south):
        pl.semaphore_signal(barrier, inc=1, device_id={"lat": there}, device_id_type=MESH)
        for side in (west, east):
            pl.semaphore_signal(
                barrier, inc=1, device_id={"lat": there, "lon": side}, device_id_type=MESH
            )

    for load in loads[:3]:
        load.wait()
    drow = dest_ref[...].astype(F32)
    prow = col_ref[...]
    irow = (prow // lanes).astype(F32)
    jrow = (prow % lanes).astype(F32)
    krow = count_ref[...].astype(F32)
    eye = iota((records, records), 0) == iota((records, records), 1)

    def column_of(row):
        return jnp.sum(jnp.where(eye, row, 0.0), axis=1, keepdims=True)

    dcol, icol, jcol, kcol = (column_of(row) for row in (drow, irow, jrow, krow))
    same = dcol == drow
    before = iota((records, records), 1) < iota((records, records), 0)
    after = iota((records, records), 0) < iota((records, records), 1)
    rank_col = jnp.sum(jnp.where(same & before, 1.0, 0.0), axis=1, keepdims=True)
    rank_row = jnp.sum(jnp.where(same & after, 1.0, 0.0), axis=0, keepdims=True)

    lane = iota((records, slots), 1)
    mine = ((lane % points) // 4 == me) & ((lane % 4).astype(F32) == rank_col)
    value = jnp.where(lane < points, icol + 1.0, jcol)
    values = jnp.where(mine, value, 0.0).astype(BF16)
    toward = jnp.where(iota((lons, records), 0).astype(F32) == drow, 1.0, 0.0).astype(BF16)
    asks = jnp.dot(toward, values, preferred_element_type=F32)
    ask[...] = asks.reshape(lons, 1, slots)

    pl.semaphore_wait(barrier, lons - 1 + 6)

    def send_all(source, target, phase):
        for peer in peers:
            pltpu.make_async_remote_copy(
                src_ref=source.at[peer],
                dst_ref=target.at[me],
                send_sem=a2a_send.at[phase],
                recv_sem=a2a_recv.at[phase],
                device_id={"lon": peer},
                device_id_type=MESH,
            ).start()

        target[me] = source[me]

    def all_of(source, target, phase):
        return pltpu.make_async_remote_copy(
            src_ref=source.at[pl.ds(0, lons - 1)],
            dst_ref=target.at[pl.ds(0, lons - 1)],
            send_sem=a2a_send.at[phase],
            recv_sem=a2a_recv.at[phase],
            device_id={"lon": east},
            device_id_type=MESH,
        )

    send_all(ask, asked, 0)

    reply[...] = jnp.zeros(reply.shape, BF16)
    loads[8].wait()
    for v in range(2):
        low_ref[v, half - 16 : half, :] = jnp.zeros((16, rows * lanes), BF16)

        @pl.loop(0, rows)
        def _(i):
            plane = state_ref[pl.ds(v * levels * rows + i, levels, stride=rows), :]
            start = pl.multiple_of(i * lanes, lanes)
            low_ref[v, 0:levels, pl.ds(start, lanes)] = plane.astype(BF16)

    n = iota((1, wide), 1)
    record_of = jnp.zeros((1, wide), jnp.int32)
    for q in range(1, wide // feats):
        record_of = record_of + jnp.where(n >= q * feats, 1, 0)
    feature = n - feats * record_of
    for v in range(2):
        level = iota((256, wide), 0)
        hit = (feature == 2 * level + v) & (level < levels)
        map_ref[v * 256 : (v + 1) * 256, :] = jnp.where(hit, 1.0, 0.0).astype(BF16)

    for load in loads[3:6]:
        load.wait()
    for v in range(2):
        square_ref[...] = jnp.zeros(square_ref.shape, F32)
        square_ref[0:levels, 0:levels] = vert_ref[...].astype(F32)[:, v, :]
        mix_ref[v * half : (v + 1) * half, :] = jnp.transpose(square_ref[...])[0:half].astype(BF16)
        square_ref[0:9, 0:levels] = lon_ref[...][:, v, :]
        square_ref[16:25, 0:levels] = lat_ref[...][:, v, :]
        tap_ref[v * half : (v + 1) * half, :] = jnp.transpose(square_ref[0:128, :])[0:half, 0:32]

    all_of(ask, asked, 0).wait_recv()
    seen = jnp.sum(asked[...], axis=0)
    spot[...] = seen
    neighbours = (
        ({"lat": north}, 2), ({"lat": south}, 1), ({"lon": east}, 3), ({"lon": west}, 4),
    )

    def near(source, target, target_index, sem, device):
        return pltpu.make_async_remote_copy(
            src_ref=source,
            dst_ref=target.at[target_index],
            send_sem=near_send.at[sem],
            recv_sem=near_recv.at[sem],
            device_id=device,
            device_id_type=MESH,
        )

    spot_copies = [
        near(spot, spots, index - 1, index - 1, device) for device, index in neighbours
    ]
    for copy in spot_copies:
        copy.start()

    points_row = jnp.concatenate(
        [seen[:, 0:points], seen[:, points:]]
        + [jnp.zeros((6, points), F32)],
        axis=0,
    )
    points_col = jnp.transpose(points_row)
    icol_own, jcol_own = points_col[:, 0:1] - 1.0, points_col[:, 1:2]
    spot_col = jnp.where(icol_own >= 0.0, icol_own * lanes + jcol_own, -1.0)
    chunk = 512
    for c in range(rows * lanes // chunk):
        at = (iota((points, chunk), 1) + c * chunk).astype(F32)
        pick_ref[:, c * chunk : (c + 1) * chunk] = jnp.where(spot_col == at, 1.0, 0.0).astype(BF16)
    n = iota((slots, points), 0)
    expand = iota((slots, points), 1) == (n // 8) * 4 + n % 4
    states = jnp.zeros((slots, half), F32)
    for v in range(2):
        found = lax.dot_general(
            pick_ref[...], low_ref[v], NT, preferred_element_type=F32
        ).astype(BF16)
        put = jnp.where(expand & ((n // 4) % 2 == v), 1.0, 0.0).astype(BF16)
        states = states + jnp.dot(put, found, preferred_element_type=F32)
    reply[:, :, 0:half] = states.reshape(lons, 8, half).astype(BF16)
    send_all(reply, replied, 1)

    for k in range(9):
        lon_tap[k] = jnp.broadcast_to(tap_ref[:, k : k + 1], (2 * half, points))
        lat_tap[k] = jnp.broadcast_to(tap_ref[:, 16 + k : 17 + k], (2 * half, points))

    def mark(index, i, j):
        lane = iota((points, lanes), 1)
        for k in range(9):
            hit = (lane + (k - 4)).astype(F32) == j
            hot_ref[index, k * points : (k + 1) * points, :] = jnp.where(hit, 1.0, 0.0).astype(BF16)
        row_ref[index] = jnp.broadcast_to(i, (points, lanes))

    def spread(index, pair):
        columns = []
        for i in (2 * pair, 2 * pair + 1):
            here = jnp.where(row_ref[index] == float(i), 1.0, 0.0).astype(BF16)
            columns.append(
                jnp.concatenate(
                    [hot_ref[index, k * points : (k + 1) * points, :] * here for k in range(9)],
                    axis=0,
                )
            )
        along_ref[:, 2 * pair * lanes : (2 * pair + 2) * lanes] = jnp.dot(
            lhs_ref[index], jnp.concatenate(columns, axis=1), preferred_element_type=F32
        )

    def scale(index, values):
        for k in range(9):
            lhs_ref[index, :, k * points : (k + 1) * points] = (lon_tap[k] * values).astype(BF16)

    mark(0, icol_own + 4.0, jcol_own)
    for load in (loads[6], loads[7], loads[9]):
        load.wait()
    all_of(reply, replied, 1).wait_recv()
    answers = replied[...].astype(F32).reshape(slots, 256).astype(BF16)
    slane = iota((records, slots), 1)
    hit = ((slane // 8).astype(F32) == dcol) & ((slane % 4).astype(F32) == rank_col)
    bd = jnp.zeros((records, wide), F32)
    for v in range(2):
        take = jnp.where(hit & ((slane // 4) % 2 == v), 1.0, 0.0).astype(BF16)
        picked = jnp.dot(take, answers, preferred_element_type=F32).astype(BF16)
        bd = bd + jnp.dot(
            picked, map_ref[v * 256 : (v + 1) * 256, :], preferred_element_type=F32
        )
    own_block = record_of == iota((records, wide), 0) % 8
    bd_ref[...] = jnp.where(own_block, bd, 0.0)
    for g in range(records // 8):
        model_ref[g * 8 : (g + 1) * 8, :] = jnp.dot(
            bd_ref[g * 8 : (g + 1) * 8, :].astype(BF16),
            jac_ref[g * wide : (g + 1) * wide, :],
            preferred_element_type=F32,
        )
    alive = iota((records, channels), 1).astype(F32) < kcol
    weight = jnp.where(alive, inv_ref[...].astype(F32), 0.0)
    model_ref[...] = weight * (model_ref[...] - obs_ref[...].astype(F32))
    for g in range(records // 8):
        bd_ref[g * 8 : (g + 1) * 8, :] = lax.dot_general(
            model_ref[g * 8 : (g + 1) * 8, :].astype(BF16),
            jac_ref[g * wide : (g + 1) * wide, :],
            NT,
            preferred_element_type=F32,
        )
    terms = jnp.where(own_block, bd_ref[...], 0.0).astype(BF16)
    srow = iota((slots, records), 0)
    hit = ((srow // 8).astype(F32) == drow) & ((srow % 4).astype(F32) == rank_row)
    gives = jnp.zeros((slots, 256), F32)
    for v in range(2):
        term = lax.dot_general(
            terms, map_ref[v * 256 : (v + 1) * 256, :], NT, preferred_element_type=F32
        ).astype(BF16)
        put = jnp.where(hit & ((srow // 4) % 2 == v), 1.0, 0.0).astype(BF16)
        gives = gives + jnp.dot(put, term, preferred_element_type=F32)
    give[...] = gives.reshape(lons, 8, 256).astype(BF16)
    send_all(give, given, 2)

    for copy in spot_copies:
        copy.wait()
    shifts = (4, 4 - rows, 4 + rows, 4, 4)
    stack = []
    for q in range(5):
        both = spot[...] if q == 0 else spots[q - 1]
        i1, j = both[:, 0:points], both[:, points : 2 * points]
        i = i1 - 1.0 + shifts[q]
        good = (i1 > 0.0) & (i >= 0.0) & (i < rows + 8.0)
        if q == 1:
            good = good & (iota((1, points), 0) + band > 0)
        if q == 2:
            good = good & (iota((1, points), 0) + band < lats - 1)
        stack += [jnp.where(good, i, -1000.0), j]
    where = jnp.transpose(jnp.concatenate(stack + stack[:6], axis=0))
    pos_ref[...] = where
    for q in (1, 2):
        mark(q, where[:, 2 * q : 2 * q + 1], where[:, 2 * q + 1 : 2 * q + 2])

    all_of(give, given, 2).wait_recv()
    terms_in = given[...].astype(F32).reshape(slots, 256).astype(BF16)
    s = iota((points, slots), 0)
    wanted = iota((points, slots), 1) - ((s // 4) * 8 + s % 4)
    parts = []
    for v in range(2):
        take = jnp.where(wanted == 4 * v, 1.0, 0.0).astype(BF16)
        term = jnp.dot(take, terms_in, preferred_element_type=F32).astype(BF16)
        parts.append(
            lax.dot_general(
                mix_ref[v * half : (v + 1) * half, :], term, NT, preferred_element_type=F32
            )
        )
    exact = jnp.concatenate(parts, axis=0)
    own = exact.astype(BF16)
    table[...] = own
    table_copies = [
        near(table, tables, index - 1, 3 + index, device) for device, index in neighbours
    ]
    for copy in table_copies:
        copy.start()
    r = iota((128, points), 0)
    c, v, i, j = r // 32, (r // 16) % 2, (r // 4) % 4, r % 4
    at_i = jnp.where(c < 2, rows - 4, 0) + i
    at_j = jnp.where(c % 2 == 0, lanes - 4, 0) + j
    both = spot[...]
    hot = (both[:, 0:points] == (at_i + 1).astype(F32)) & (both[:, points:] == at_j.astype(F32))
    cut = jnp.zeros((128, half), F32)
    for var in range(2):
        pick = jnp.where(hot & (v == var), 1.0, 0.0).astype(BF16)
        cut = cut + lax.dot_general(
            pick, own[var * half : (var + 1) * half], NT, preferred_element_type=F32
        )
    cut = jnp.concatenate([cut, jnp.zeros((128, 256 - half), F32)], axis=1)
    corner[...] = cut.reshape(4, 32, 256).astype(BF16)
    corner_copies = [
        near(corner.at[q], corners, q, 8 + q, {"lat": there, "lon": side})
        for q, (there, side) in enumerate(
            ((south, east), (south, west), (north, east), (north, west))
        )
    ]
    for copy in corner_copies:
        copy.start()
    scale(0, exact)
    for pair in range(2, rows // 2 + 2):
        spread(0, pair)
    for copy in table_copies:
        copy.wait()
    for q in (1, 2):
        scale(q, tables[q - 1].astype(F32))
    for pair in (0, 1):
        spread(1, pair)
        spread(2, rows // 2 + 2 + pair)
    for q in (2, 3):
        tab_ref[q - 2] = tables[q]
    for copy in corner_copies:
        copy.wait()
    q = iota((4, 32, 256), 0)
    keep = ((q >= 2) | (q * 0 + band > 0)) & ((q < 2) | (q * 0 + band < lats - 1))
    cor_ref[...] = jnp.where(keep, corners[...].astype(F32), 0.0).astype(BF16).reshape(128, 256)
    for phase, source, target in ((0, ask, asked), (1, reply, replied), (2, give, given)):
        all_of(source, target, phase).wait_send()


def exchange_call(sizes, *operands):
    lons, lats, levels, rows, lanes, records, channels = sizes
    half, slots = 144, lons * 8
    wide = 8 * 2 * levels
    points = slots // 2
    vmem = pl.BlockSpec(memory_space=pltpu.VMEM)
    hbm = pl.BlockSpec(memory_space=pltpu.HBM)
    return pl.pallas_call(
        functools.partial(exchange_kernel, sizes),
        out_shape=(
            jax.ShapeDtypeStruct((2, 2 * half, points), BF16),
            jax.ShapeDtypeStruct((128, 256), BF16),
            jax.ShapeDtypeStruct((points, 16), F32),
            jax.ShapeDtypeStruct((9, 2 * half, lanes), F32),
            jax.ShapeDtypeStruct((9, 2 * half, lanes), F32),
            jax.ShapeDtypeStruct((2 * half, (rows + 8) * lanes), F32),
        ),
        in_specs=[hbm] * 10,
        out_specs=(vmem,) * 6,
        scratch_shapes=[
            pltpu.VMEM((2 * levels * rows, lanes), F32),
            pltpu.VMEM((2, half, rows * lanes), BF16),
            pltpu.VMEM((records * 2 * levels, channels), BF16),
            pltpu.VMEM((512, wide), BF16),
            pltpu.VMEM((records, wide), F32),
            pltpu.VMEM((records, channels), F32),
            pltpu.VMEM((records, channels), BF16),
            pltpu.VMEM((records, channels), BF16),
            pltpu.VMEM((1, records), jnp.int32),
            pltpu.VMEM((1, records), jnp.int32),
            pltpu.VMEM((1, records), jnp.int32),
            pltpu.VMEM((levels, 2, levels), BF16),
            pltpu.VMEM((9, 2, levels), F32),
            pltpu.VMEM((9, 2, levels), F32),
            pltpu.VMEM((256, 256), F32),
            pltpu.VMEM((2 * half, 256), BF16),
            pltpu.VMEM((2 * half, 32), F32),
            pltpu.VMEM((3, 2 * half, 9 * points), BF16),
            pltpu.VMEM((3, 9 * points, lanes), BF16),
            pltpu.VMEM((3, points, lanes), F32),
            pltpu.VMEM((points, rows * lanes), BF16),
            pltpu.VMEM((lons, 1, slots), F32),
            pltpu.VMEM((lons, 1, slots), F32),
            pltpu.VMEM((lons, 8, 256), BF16),
            pltpu.VMEM((lons, 8, 256), BF16),
            pltpu.VMEM((lons, 8, 256), BF16),
            pltpu.VMEM((lons, 8, 256), BF16),
            pltpu.VMEM((2 * half, points), BF16),
            pltpu.VMEM((4, 2 * half, points), BF16),
            pltpu.VMEM((4, 32, 256), BF16),
            pltpu.VMEM((4, 32, 256), BF16),
            pltpu.VMEM((1, slots), F32),
            pltpu.VMEM((4, 1, slots), F32),
            pltpu.SemaphoreType.DMA((10,)),
            pltpu.SemaphoreType.DMA((3,)),
            pltpu.SemaphoreType.DMA((3,)),
            pltpu.SemaphoreType.DMA((12,)),
            pltpu.SemaphoreType.DMA((12,)),
        ],
        compiler_params=pltpu.CompilerParams(
            collective_id=0, has_side_effects=True, vmem_limit_bytes=36 << 20
        ),
        name="exchange",
    )(*[pltpu.with_memory_space_constraint(x, pltpu.HBM) for x in operands])


def rim_lane(e, lanes, halo):
    return jnp.where(e < halo, lanes - halo + e, e - halo)


def grid_kernel(
    rows, halo, lanes, levels,
    tab_ref, cor_ref, pos_ref, lon_tap, lat_tap, part_ref, out_hbm,
    fix_ref, along_ref, out_ref, sem,
):
    size = tab_ref.shape[1]
    half = size // 2
    slots = tab_ref.shape[2]
    tall = rows + 2 * halo
    packed = fix_ref.shape[1]
    taps = 2 * halo + 1
    group = lanes // (2 * halo)

    total = jnp.zeros((size, packed), F32)
    at = iota((slots, packed), 1).astype(F32)
    for index in (3, 4):
        table = tab_ref[index - 3].astype(F32)
        i = pos_ref[:, 2 * index : 2 * index + 1]
        j = pos_ref[:, 2 * index + 1 : 2 * index + 2]
        for q in range(halo):
            k = q if index == 3 else q + halo + 1
            if index == 3:
                e = j - (lanes - 2 * halo) - k
                good = (j >= lanes - halo) & (e >= halo)
            else:
                e = j + 2 * halo - k
                good = (j < halo) & (e < halo)
            spot = jnp.where(good & (i >= 0.0), i * (2.0 * halo) + e, -1.0)
            hot = jnp.where(spot == at, 1.0, 0.0).astype(BF16)
            total = total + jnp.dot(
                (lon_tap[k] * table).astype(BF16), hot, preferred_element_type=F32
            )
    turned = jnp.transpose(cor_ref[...].astype(F32))[0:half]
    lane = iota((half, slots), 1)
    turned = jnp.concatenate(
        [jnp.where((lane // 16) % 2 == v, turned, 0.0) for v in range(2)], axis=0
    )
    row = iota((slots, packed), 0)
    c, i, j = row // 32, (row // 4) % 4, row % 4
    leftward = (iota((size, slots), 1) // 32) % 2 == 0
    for q in range(halo):
        e = jnp.where(c % 2 == 0, halo + j - q, j + halo - 1 - q)
        least = jnp.where(c % 2 == 0, halo, 0)
        good = (e >= least) & (e < least + halo)
        spot = jnp.where(good, ((c // 2) * (rows + halo) + i) * (2 * halo) + e, -1)
        hot = jnp.where(spot == iota((slots, packed), 1), 1.0, 0.0).astype(BF16)
        factor = jnp.where(leftward, lon_tap[q], lon_tap[q + halo + 1])
        total = total + jnp.dot((factor * turned).astype(BF16), hot, preferred_element_type=F32)
    fix_ref[...] = total.astype(BF16)

    lane = iota((slots, lanes), 1)
    e = iota((slots, lanes), 0) % (2 * halo)
    place = lane == rim_lane(e, lanes, halo)
    turn = iota((slots, lanes), 0) // (2 * halo)
    for pair in range(tall // 2):
        spots = [
            jnp.where(place & (turn == i % group), 1.0, 0.0).astype(BF16)
            for i in (2 * pair, 2 * pair + 1)
        ]
        q = (2 * pair) // group
        columns = slice(2 * pair * lanes, (2 * pair + 2) * lanes)
        along_ref[:, columns] = part_ref[:, columns] + jnp.dot(
            fix_ref[:, q * lanes : (q + 1) * lanes],
            jnp.concatenate(spots, axis=1),
            preferred_element_type=F32,
        )

    flat = out_ref.reshape(size * rows, lanes)

    def filter_rows(block, base):
        lat = [lat_tap[k, pl.ds(base, 8), :] for k in range(taps)]
        start = block * 8
        along = [
            along_ref[pl.ds(base, 8), i * lanes : (i + 1) * lanes]
            for i in range(start, start + 8 + 2 * halo)
        ]
        for r in range(8):
            out = lat[0] * along[r]
            for k in range(1, taps):
                out = out + lat[k] * along[r + k]
            flat[pl.ds(base * rows + start + r, 8, stride=rows), :] = out

    copies = []
    for block in range(rows // 8):

        @pl.loop(0, size // 32)
        def _(step):
            for part in range(4):
                filter_rows(block, pl.multiple_of(step * 32 + part * 8, 8))

        copy = pltpu.make_async_copy(
            out_ref.at[:, pl.ds(0, levels), pl.ds(block * 8, 8), :],
            out_hbm.at[:, :, pl.ds(block * 8, 8), :],
            sem.at[block],
        )
        copy.start()
        copies.append(copy)
    for copy in copies:
        copy.wait()


def grid_call(tables, corners, pos, lon_tap, lat_tap, part, levels, rows, lanes):
    halo = 4
    size = tables.shape[1]
    tall = rows + 2 * halo
    packed = -(-tall * 2 * halo // lanes) * lanes
    vmem = pl.BlockSpec(memory_space=pltpu.VMEM)
    return pl.pallas_call(
        functools.partial(grid_kernel, rows, halo, lanes, levels),
        out_shape=jax.ShapeDtypeStruct((2, levels, rows, lanes), F32),
        in_specs=[vmem] * 6,
        out_specs=pl.BlockSpec(memory_space=pl.ANY),
        scratch_shapes=[
            pltpu.VMEM((size, packed), BF16),
            pltpu.VMEM((size, tall * lanes), F32),
            pltpu.VMEM((2, size // 2, rows, lanes), F32),
            pltpu.SemaphoreType.DMA((rows // 8,)),
        ],
        compiler_params=pltpu.CompilerParams(vmem_limit_bytes=24 << 20),
        name="grid",
    )(tables, corners, pos, lon_tap, lat_tap, part)


def body(
    state_field,
    jacobian,
    observed,
    inverse_var,
    valid_count,
    destination,
    column,
    vertical,
    lon_taps,
    lat_taps,
):
    variables, levels, rows, lanes = state_field.shape
    records, channels = jacobian.shape[1], jacobian.shape[-1]
    sizes = (
        lax.axis_size("lon"), lax.axis_size("lat"), levels, rows, lanes, records, channels,
    )
    tables, corners, pos, lon_tap, lat_tap, part = exchange_call(
        sizes,
        state_field.reshape(variables * levels * rows, lanes),
        jacobian.transpose(0, 1, 3, 2, 4).reshape(records * levels * variables, channels),
        observed.reshape(records, channels),
        inverse_var.reshape(records, channels),
        valid_count.reshape(1, records),
        destination.reshape(1, records),
        column.reshape(1, records),
        vertical.transpose(1, 0, 2),
        lon_taps.transpose(2, 0, 1),
        lat_taps.transpose(2, 0, 1),
    )
    return grid_call(tables, corners, pos, lon_tap, lat_tap, part, levels, rows, lanes)


def solution(mesh):
    placed = (
        P(None, None, "lat", "lon"),
        P("lat", "lon", None, None, None),
        P("lat", "lon", None),
        P("lat", "lon", None),
        P("lat", "lon"),
        P("lat", "lon", None),
        P("lat", "lon"),
        P(),
        P(),
        P(),
    )
    return jax.shard_map(
        body, mesh=mesh, in_specs=placed, out_specs=P(None, None, "lat", "lon"), check_vma=False
    )
```

```python
import functools

import jax
import jax.numpy as jnp
from jax import lax
from jax.experimental import pallas as pl
from jax.experimental.pallas import tpu as pltpu
from jax.sharding import PartitionSpec as P

F32 = jnp.float32
BF16 = jnp.bfloat16


MESH = pl.DeviceIdType.MESH
NT = (((1,), (1,)), ((), ()))
TN = (((0,), (0,)), ((), ()))


def iota(shape, dim):
    return lax.broadcasted_iota(jnp.int32, shape, dim)


def far_first(ring):
    steps = [
        (z, x, c) for z in range(ring[0]) for x in range(ring[1]) for c in range(ring[2])
    ][1:]
    return sorted(
        steps, key=lambda s: -(min(s[0], ring[0] - s[0]) + min(s[1], ring[1] - s[1]) + 0.5 * s[2])
    )


def peer_at(me, step, ring):
    z, x, c = me // (ring[1] * ring[2]), (me // ring[2]) % ring[1], me % ring[2]
    z, x, c = (lax.rem(at + go, size) for at, go, size in zip((z, x, c), step, ring))
    return (z * ring[1] + x) * ring[2] + c


def exchange_kernel(
    sizes,
    state_hbm, jac_hbm, obs_hbm, inv_hbm, count_hbm, dest_hbm, col_hbm, vert_hbm, lon_hbm, lat_hbm,
    tab_ref, cor_ref, pos_ref, lon_tap, lat_tap, along_ref,
    state_ref, low_ref, jac_ref, map_ref, part_ref, model_ref,
    obs_ref, inv_ref, count_ref, dest_ref, col_ref, vert_ref, lon_ref, lat_ref, square_ref, mix_ref, tap_ref, lhs_ref, hot_ref, row_ref, pick_ref,
    ask, asked, reply, replied, give, given,
    table, tables, corner, corners, spot, spots,
    load_sem, a2a_send, a2a_recv, near_send, near_recv,
):
    lons, lats, levels, rows, lanes, records, channels = sizes
    ring = (lons // 8, 4, 2)
    half = low_ref.shape[1]
    slots = 2 * table.shape[1]
    points = table.shape[1]
    span = 512
    feats = 2 * levels
    wide = 8 * feats
    me = lax.axis_index("lon")
    band = lax.axis_index("lat")
    east, west = lax.rem(me + 1, lons), lax.rem(me + lons - 1, lons)
    south, north = lax.rem(band + 1, lats), lax.rem(band + lats - 1, lats)

    loads = [
        pltpu.make_async_copy(source, target, load_sem.at[q])
        for q, (source, target) in enumerate(
            (
                (dest_hbm, dest_ref), (col_hbm, col_ref), (count_hbm, count_ref),
                (vert_hbm, vert_ref), (lon_hbm, lon_ref), (lat_hbm, lat_ref),
                (obs_hbm, obs_ref), (inv_hbm, inv_ref),
                (state_hbm, state_ref), (jac_hbm, jac_ref),
            )
        )
    ]
    for load in loads:
        load.start()

    barrier = pltpu.get_barrier_semaphore()
    peers = [peer_at(me, step, ring) for step in far_first(ring)]
    for peer in peers:
        pl.semaphore_signal(barrier, inc=1, device_id={"lon": peer}, device_id_type=MESH)

    for there in (north, south):
        pl.semaphore_signal(barrier, inc=1, device_id={"lat": there}, device_id_type=MESH)
        for side in (west, east):
            pl.semaphore_signal(
                barrier, inc=1, device_id={"lat": there, "lon": side}, device_id_type=MESH
            )

    for load in loads[:3]:
        load.wait()
    drow = dest_ref[...].astype(F32)
    prow = col_ref[...]
    irow = (prow // lanes).astype(F32)
    jrow = (prow % lanes).astype(F32)
    krow = count_ref[...].astype(F32)
    eye = iota((records, records), 0) == iota((records, records), 1)

    def column_of(row):
        return jnp.sum(jnp.where(eye, row, 0.0), axis=1, keepdims=True)

    dcol, icol, jcol, kcol = (column_of(row) for row in (drow, irow, jrow, krow))
    same = dcol == drow
    before = iota((records, records), 1) < iota((records, records), 0)
    after = iota((records, records), 0) < iota((records, records), 1)
    rank_col = jnp.sum(jnp.where(same & before, 1.0, 0.0), axis=1, keepdims=True)
    rank_row = jnp.sum(jnp.where(same & after, 1.0, 0.0), axis=0, keepdims=True)

    lane = iota((records, slots), 1)
    mine = ((lane % points) // 4 == me) & ((lane % 4).astype(F32) == rank_col)
    value = jnp.where(lane < points, icol + 1.0, jcol)
    values = jnp.where(mine, value, 0.0).astype(BF16)
    toward = jnp.where(iota((lons, records), 0).astype(F32) == drow, 1.0, 0.0).astype(BF16)
    asks = jnp.dot(toward, values, preferred_element_type=F32)
    ask[...] = asks.reshape(lons, 1, slots)

    pl.semaphore_wait(barrier, lons - 1 + 6)

    def send_all(source, target, phase):
        for peer in peers:
            pltpu.make_async_remote_copy(
                src_ref=source.at[peer],
                dst_ref=target.at[me],
                send_sem=a2a_send.at[phase],
                recv_sem=a2a_recv.at[phase],
                device_id={"lon": peer},
                device_id_type=MESH,
            ).start()

        target[me] = source[me]

    def all_of(source, target, phase):
        return pltpu.make_async_remote_copy(
            src_ref=source.at[pl.ds(0, lons - 1)],
            dst_ref=target.at[pl.ds(0, lons - 1)],
            send_sem=a2a_send.at[phase],
            recv_sem=a2a_recv.at[phase],
            device_id={"lon": east},
            device_id_type=MESH,
        )

    send_all(ask, asked, 0)

    loads[8].wait()
    for v in range(2):
        low_ref[v, half - 16 : half, :] = jnp.zeros((16, rows * lanes), BF16)

        @pl.loop(0, rows)
        def _(i):
            plane = state_ref[pl.ds(v * levels * rows + i, levels, stride=rows), :]
            start = pl.multiple_of(i * lanes, lanes)
            low_ref[v, 0:levels, pl.ds(start, lanes)] = plane.astype(BF16)

    for v in range(2):
        hit = iota((half, 384), 1) == 2 * iota((half, 384), 0) + v
        hit = hit & (iota((half, 384), 0) < levels)
        map_ref[v] = jnp.where(hit, 1.0, 0.0).astype(BF16)

    for load in loads[3:6]:
        load.wait()
    for v in range(2):
        square_ref[...] = jnp.zeros(square_ref.shape, F32)
        square_ref[0:levels, 0:levels] = vert_ref[...].astype(F32)[:, v, :]
        turned = jnp.transpose(square_ref[...])[0:half].astype(BF16)
        mix_ref[v * half : (v + 1) * half, :] = jnp.dot(
            turned[:, 0:half], map_ref[v], preferred_element_type=F32
        ).astype(BF16)
        square_ref[0:9, 0:levels] = lon_ref[...][:, v, :]
        square_ref[16:25, 0:levels] = lat_ref[...][:, v, :]
        tap_ref[v * half : (v + 1) * half, :] = jnp.transpose(square_ref[0:128, :])[0:half, 0:32]

    all_of(ask, asked, 0).wait_recv()
    seen = jnp.sum(asked[...], axis=0)
    spot[...] = seen
    neighbours = (
        ({"lat": north}, 2), ({"lat": south}, 1), ({"lon": east}, 3), ({"lon": west}, 4),
    )

    def near(source, target, target_index, sem, device):
        return pltpu.make_async_remote_copy(
            src_ref=source,
            dst_ref=target.at[target_index],
            send_sem=near_send.at[sem],
            recv_sem=near_recv.at[sem],
            device_id=device,
            device_id_type=MESH,
        )

    spot_copies = [
        near(spot, spots, index - 1, index - 1, device) for device, index in neighbours
    ]
    for copy in spot_copies:
        copy.start()

    points_row = jnp.concatenate(
        [seen[:, 0:points], seen[:, points:]]
        + [jnp.zeros((6, points), F32)],
        axis=0,
    )
    points_col = jnp.transpose(points_row)
    icol_own, jcol_own = points_col[:, 0:1] - 1.0, points_col[:, 1:2]
    spot_col = jnp.where(icol_own >= 0.0, icol_own * lanes + jcol_own, -1.0)
    chunk = 512
    for c in range(rows * lanes // chunk):
        at = (iota((points, chunk), 1) + c * chunk).astype(F32)
        pick_ref[:, c * chunk : (c + 1) * chunk] = jnp.where(spot_col == at, 1.0, 0.0).astype(BF16)
    states = jnp.zeros((points, 384), F32)
    for v in range(2):
        found = lax.dot_general(
            pick_ref[...], low_ref[v], NT, preferred_element_type=F32
        ).astype(BF16)
        states = states + jnp.dot(found, map_ref[v], preferred_element_type=F32)
    reply[...] = states.reshape(lons, 4, 384).astype(BF16)
    send_all(reply, replied, 1)

    for k in range(9):
        lon_tap[k] = jnp.broadcast_to(tap_ref[:, k : k + 1], (2 * half, points))
        lat_tap[k] = jnp.broadcast_to(tap_ref[:, 16 + k : 17 + k], (2 * half, points))

    def mark(index, i, j):
        lane = iota((points, lanes), 1)
        for k in range(9):
            hit = (lane + (k - 4)).astype(F32) == j
            hot_ref[index, k * points : (k + 1) * points, :] = jnp.where(hit, 1.0, 0.0).astype(BF16)
        row_ref[index] = jnp.broadcast_to(i, (points, lanes))

    def spread(index, pair):
        columns = []
        for i in (2 * pair, 2 * pair + 1):
            here = jnp.where(row_ref[index] == float(i), 1.0, 0.0).astype(BF16)
            columns.append(
                jnp.concatenate(
                    [hot_ref[index, k * points : (k + 1) * points, :] * here for k in range(9)],
                    axis=0,
                )
            )
        along_ref[:, 2 * pair * lanes : (2 * pair + 2) * lanes] = jnp.dot(
            lhs_ref[index], jnp.concatenate(columns, axis=1), preferred_element_type=F32
        )

    def scale(index, values):
        for k in range(9):
            lhs_ref[index, :, k * points : (k + 1) * points] = (lon_tap[k] * values).astype(BF16)

    mark(0, icol_own + 4.0, jcol_own)
    for load in (loads[6], loads[7], loads[9]):
        load.wait()
    all_of(reply, replied, 1).wait_recv()
    answers = replied[...].astype(F32).reshape(points, 384).astype(BF16)
    slane = iota((records, points), 1)
    take = ((slane // 4).astype(F32) == dcol) & ((slane % 4).astype(F32) == rank_col)
    picked = jnp.dot(
        jnp.where(take, 1.0, 0.0).astype(BF16), answers, preferred_element_type=F32
    )
    part_ref[:, 0:384] = picked
    part_ref[:, 384:span] = jnp.zeros((records, span - 384), F32)
    tiles = -(-wide // lanes)
    extra = feats - 2 * lanes
    eighth = iota((8, lanes), 0)

    def blocks(group):
        part = part_ref[8 * group : 8 * group + 8, :]
        turned = [pltpu.roll(part, extra * q, 1) if q else part for q in range(8)]
        line = []
        for tile in range(tiles):
            value = jnp.zeros((8, lanes), F32)
            for q in range(8):
                j = tile - 2 * q
                if 0 <= j < span // lanes:
                    value = jnp.where(
                        eighth == q, turned[q][:, j * lanes : (j + 1) * lanes], value
                    )
            line.append(value)
        return jnp.concatenate(line, axis=1)[:, 0:wide]

    def gather_blocks(value, group):
        total = jnp.zeros((8, span), F32)
        column = iota((8, span), 1)
        value = jnp.concatenate(
            [value, jnp.zeros((8, (tiles + 2) * lanes - wide), F32)], axis=1
        )
        for q in range(8):
            piece = value[:, 2 * lanes * q : 2 * lanes * q + span]
            piece = pltpu.roll(piece, span - extra * q, 1) if q else piece
            total = jnp.where((iota((8, span), 0) == q) & (column < feats), piece, total)
        part_ref[8 * group : 8 * group + 8, :] = total

    def two_groups(group):
        return jnp.concatenate(
            [
                jac_ref[group * wide : (group + 1) * wide, :],
                jac_ref[(group + 1) * wide : (group + 2) * wide, :],
            ],
            axis=1,
        )

    for g in range(0, records // 8, 2):
        left = jnp.concatenate([blocks(g), blocks(g + 1)], axis=0).astype(BF16)
        both = jnp.dot(left, two_groups(g), preferred_element_type=F32)
        model_ref[8 * g : 8 * g + 8, :] = both[0:8, 0:channels]
        model_ref[8 * g + 8 : 8 * g + 16, :] = both[8:16, channels:]
    alive = iota((records, channels), 1).astype(F32) < kcol
    weight = jnp.where(alive, inv_ref[...].astype(F32), 0.0)
    model_ref[...] = weight * (model_ref[...] - obs_ref[...].astype(F32))
    for g in range(0, records // 8, 2):
        none = jnp.zeros((8, channels), F32)
        one, two = model_ref[8 * g : 8 * g + 8, :], model_ref[8 * g + 8 : 8 * g + 16, :]
        left = jnp.concatenate(
            [jnp.concatenate([one, none], axis=1), jnp.concatenate([none, two], axis=1)], axis=0
        ).astype(BF16)
        both = lax.dot_general(left, two_groups(g), NT, preferred_element_type=F32)
        gather_blocks(both[0:8], g)
        gather_blocks(both[8:16], g + 1)
    srow = iota((points, records), 0)
    put = ((srow // 4).astype(F32) == drow) & ((srow % 4).astype(F32) == rank_row)
    gives = jnp.dot(
        jnp.where(put, 1.0, 0.0).astype(BF16),
        part_ref[:, 0:384].astype(BF16),
        preferred_element_type=F32,
    )
    give[...] = gives.reshape(lons, 4, 384).astype(BF16)
    send_all(give, given, 2)

    for copy in spot_copies:
        copy.wait()
    shifts = (4, 4 - rows, 4 + rows, 4, 4)
    stack = []
    for q in range(5):
        both = spot[...] if q == 0 else spots[q - 1]
        i1, j = both[:, 0:points], both[:, points : 2 * points]
        i = i1 - 1.0 + shifts[q]
        good = (i1 > 0.0) & (i >= 0.0) & (i < rows + 8.0)
        if q == 1:
            good = good & (iota((1, points), 0) + band > 0)
        if q == 2:
            good = good & (iota((1, points), 0) + band < lats - 1)
        stack += [jnp.where(good, i, -1000.0), j]
    where = jnp.transpose(jnp.concatenate(stack + stack[:6], axis=0))
    pos_ref[...] = where
    for q in (1, 2):
        mark(q, where[:, 2 * q : 2 * q + 1], where[:, 2 * q + 1 : 2 * q + 2])

    all_of(give, given, 2).wait_recv()
    terms_in = given[...].astype(F32).reshape(points, 384).astype(BF16)
    parts = [
        lax.dot_general(
            mix_ref[v * half : (v + 1) * half, :], terms_in, NT, preferred_element_type=F32
        )
        for v in range(2)
    ]
    exact = jnp.concatenate(parts, axis=0)
    own = exact.astype(BF16)
    table[...] = own
    table_copies = [
        near(table, tables, index - 1, 3 + index, device) for device, index in neighbours
    ]
    for copy in table_copies:
        copy.start()
    r = iota((128, points), 0)
    c, v, i, j = r // 32, (r // 16) % 2, (r // 4) % 4, r % 4
    at_i = jnp.where(c < 2, rows - 4, 0) + i
    at_j = jnp.where(c % 2 == 0, lanes - 4, 0) + j
    both = spot[...]
    hot = (both[:, 0:points] == (at_i + 1).astype(F32)) & (both[:, points:] == at_j.astype(F32))
    cut = jnp.zeros((128, half), F32)
    for var in range(2):
        pick = jnp.where(hot & (v == var), 1.0, 0.0).astype(BF16)
        cut = cut + lax.dot_general(
            pick, own[var * half : (var + 1) * half], NT, preferred_element_type=F32
        )
    cut = jnp.concatenate([cut, jnp.zeros((128, 256 - half), F32)], axis=1)
    corner[...] = cut.reshape(4, 32, 256).astype(BF16)
    corner_copies = [
        near(corner.at[q], corners, q, 8 + q, {"lat": there, "lon": side})
        for q, (there, side) in enumerate(
            ((south, east), (south, west), (north, east), (north, west))
        )
    ]
    for copy in corner_copies:
        copy.start()
    scale(0, exact)
    for pair in range(2, rows // 2 + 2):
        spread(0, pair)
    for copy in table_copies:
        copy.wait()
    for q in (1, 2):
        scale(q, tables[q - 1].astype(F32))
    for pair in (0, 1):
        spread(1, pair)
        spread(2, rows // 2 + 2 + pair)
    for q in (2, 3):
        tab_ref[q - 2] = tables[q]
    for copy in corner_copies:
        copy.wait()
    q = iota((4, 32, 256), 0)
    keep = ((q >= 2) | (q * 0 + band > 0)) & ((q < 2) | (q * 0 + band < lats - 1))
    cor_ref[...] = jnp.where(keep, corners[...].astype(F32), 0.0).astype(BF16).reshape(128, 256)
    for phase, source, target in ((0, ask, asked), (1, reply, replied), (2, give, given)):
        all_of(source, target, phase).wait_send()


def exchange_call(sizes, *operands):
    lons, lats, levels, rows, lanes, records, channels = sizes
    half, slots = 144, lons * 8
    points = slots // 2
    vmem = pl.BlockSpec(memory_space=pltpu.VMEM)
    hbm = pl.BlockSpec(memory_space=pltpu.HBM)
    return pl.pallas_call(
        functools.partial(exchange_kernel, sizes),
        out_shape=(
            jax.ShapeDtypeStruct((2, 2 * half, points), BF16),
            jax.ShapeDtypeStruct((128, 256), BF16),
            jax.ShapeDtypeStruct((points, 16), F32),
            jax.ShapeDtypeStruct((9, 2 * half, lanes), F32),
            jax.ShapeDtypeStruct((9, 2 * half, lanes), F32),
            jax.ShapeDtypeStruct((2 * half, (rows + 8) * lanes), F32),
        ),
        in_specs=[hbm] * 10,
        out_specs=(vmem,) * 6,
        scratch_shapes=[
            pltpu.VMEM((2 * levels * rows, lanes), F32),
            pltpu.VMEM((2, half, rows * lanes), BF16),
            pltpu.VMEM((records * 2 * levels, channels), BF16),
            pltpu.VMEM((2, half, 384), BF16),
            pltpu.VMEM((records, 512), F32),
            pltpu.VMEM((records, channels), F32),
            pltpu.VMEM((records, channels), BF16),
            pltpu.VMEM((records, channels), BF16),
            pltpu.VMEM((1, records), jnp.int32),
            pltpu.VMEM((1, records), jnp.int32),
            pltpu.VMEM((1, records), jnp.int32),
            pltpu.VMEM((levels, 2, levels), BF16),
            pltpu.VMEM((9, 2, levels), F32),
            pltpu.VMEM((9, 2, levels), F32),
            pltpu.VMEM((256, 256), F32),
            pltpu.VMEM((2 * half, 384), BF16),
            pltpu.VMEM((2 * half, 32), F32),
            pltpu.VMEM((3, 2 * half, 9 * points), BF16),
            pltpu.VMEM((3, 9 * points, lanes), BF16),
            pltpu.VMEM((3, points, lanes), F32),
            pltpu.VMEM((points, rows * lanes), BF16),
            pltpu.VMEM((lons, 1, slots), F32),
            pltpu.VMEM((lons, 1, slots), F32),
            pltpu.VMEM((lons, 4, 384), BF16),
            pltpu.VMEM((lons, 4, 384), BF16),
            pltpu.VMEM((lons, 4, 384), BF16),
            pltpu.VMEM((lons, 4, 384), BF16),
            pltpu.VMEM((2 * half, points), BF16),
            pltpu.VMEM((4, 2 * half, points), BF16),
            pltpu.VMEM((4, 32, 256), BF16),
            pltpu.VMEM((4, 32, 256), BF16),
            pltpu.VMEM((1, slots), F32),
            pltpu.VMEM((4, 1, slots), F32),
            pltpu.SemaphoreType.DMA((10,)),
            pltpu.SemaphoreType.DMA((3,)),
            pltpu.SemaphoreType.DMA((3,)),
            pltpu.SemaphoreType.DMA((12,)),
            pltpu.SemaphoreType.DMA((12,)),
        ],
        compiler_params=pltpu.CompilerParams(
            collective_id=0, has_side_effects=True, vmem_limit_bytes=36 << 20
        ),
        name="exchange",
    )(*[pltpu.with_memory_space_constraint(x, pltpu.HBM) for x in operands])


def rim_lane(e, lanes, halo):
    return jnp.where(e < halo, lanes - halo + e, e - halo)


def grid_kernel(
    rows, halo, lanes, levels,
    tab_ref, cor_ref, pos_ref, lon_tap, lat_tap, part_ref, out_hbm,
    fix_ref, along_ref, out_ref, sem,
):
    size = tab_ref.shape[1]
    half = size // 2
    slots = tab_ref.shape[2]
    tall = rows + 2 * halo
    packed = fix_ref.shape[1]
    taps = 2 * halo + 1
    group = lanes // (2 * halo)

    total = jnp.zeros((size, packed), F32)
    at = iota((slots, packed), 1).astype(F32)
    for index in (3, 4):
        table = tab_ref[index - 3].astype(F32)
        i = pos_ref[:, 2 * index : 2 * index + 1]
        j = pos_ref[:, 2 * index + 1 : 2 * index + 2]
        for q in range(halo):
            k = q if index == 3 else q + halo + 1
            if index == 3:
                e = j - (lanes - 2 * halo) - k
                good = (j >= lanes - halo) & (e >= halo)
            else:
                e = j + 2 * halo - k
                good = (j < halo) & (e < halo)
            spot = jnp.where(good & (i >= 0.0), i * (2.0 * halo) + e, -1.0)
            hot = jnp.where(spot == at, 1.0, 0.0).astype(BF16)
            total = total + jnp.dot(
                (lon_tap[k] * table).astype(BF16), hot, preferred_element_type=F32
            )
    turned = jnp.transpose(cor_ref[...].astype(F32))[0:half]
    lane = iota((half, slots), 1)
    turned = jnp.concatenate(
        [jnp.where((lane // 16) % 2 == v, turned, 0.0) for v in range(2)], axis=0
    )
    row = iota((slots, packed), 0)
    c, i, j = row // 32, (row // 4) % 4, row % 4
    leftward = (iota((size, slots), 1) // 32) % 2 == 0
    for q in range(halo):
        e = jnp.where(c % 2 == 0, halo + j - q, j + halo - 1 - q)
        least = jnp.where(c % 2 == 0, halo, 0)
        good = (e >= least) & (e < least + halo)
        spot = jnp.where(good, ((c // 2) * (rows + halo) + i) * (2 * halo) + e, -1)
        hot = jnp.where(spot == iota((slots, packed), 1), 1.0, 0.0).astype(BF16)
        factor = jnp.where(leftward, lon_tap[q], lon_tap[q + halo + 1])
        total = total + jnp.dot((factor * turned).astype(BF16), hot, preferred_element_type=F32)
    fix_ref[...] = total.astype(BF16)

    lane = iota((slots, lanes), 1)
    e = iota((slots, lanes), 0) % (2 * halo)
    place = lane == rim_lane(e, lanes, halo)
    turn = iota((slots, lanes), 0) // (2 * halo)
    for pair in range(tall // 2):
        spots = [
            jnp.where(place & (turn == i % group), 1.0, 0.0).astype(BF16)
            for i in (2 * pair, 2 * pair + 1)
        ]
        q = (2 * pair) // group
        columns = slice(2 * pair * lanes, (2 * pair + 2) * lanes)
        along_ref[:, columns] = part_ref[:, columns] + jnp.dot(
            fix_ref[:, q * lanes : (q + 1) * lanes],
            jnp.concatenate(spots, axis=1),
            preferred_element_type=F32,
        )

    flat = out_ref.reshape(size * rows, lanes)

    def filter_rows(block, base):
        lat = [lat_tap[k, pl.ds(base, 8), :] for k in range(taps)]
        start = block * 8
        along = [
            along_ref[pl.ds(base, 8), i * lanes : (i + 1) * lanes]
            for i in range(start, start + 8 + 2 * halo)
        ]
        for r in range(8):
            out = lat[0] * along[r]
            for k in range(1, taps):
                out = out + lat[k] * along[r + k]
            flat[pl.ds(base * rows + start + r, 8, stride=rows), :] = out

    copies = []
    for block in range(rows // 8):

        @pl.loop(0, size // 32)
        def _(step):
            for part in range(4):
                filter_rows(block, pl.multiple_of(step * 32 + part * 8, 8))

        copy = pltpu.make_async_copy(
            out_ref.at[:, pl.ds(0, levels), pl.ds(block * 8, 8), :],
            out_hbm.at[:, :, pl.ds(block * 8, 8), :],
            sem.at[block],
        )
        copy.start()
        copies.append(copy)
    for copy in copies:
        copy.wait()


def grid_call(tables, corners, pos, lon_tap, lat_tap, part, levels, rows, lanes):
    halo = 4
    size = tables.shape[1]
    tall = rows + 2 * halo
    packed = -(-tall * 2 * halo // lanes) * lanes
    vmem = pl.BlockSpec(memory_space=pltpu.VMEM)
    return pl.pallas_call(
        functools.partial(grid_kernel, rows, halo, lanes, levels),
        out_shape=jax.ShapeDtypeStruct((2, levels, rows, lanes), F32),
        in_specs=[vmem] * 6,
        out_specs=pl.BlockSpec(memory_space=pl.ANY),
        scratch_shapes=[
            pltpu.VMEM((size, packed), BF16),
            pltpu.VMEM((size, tall * lanes), F32),
            pltpu.VMEM((2, size // 2, rows, lanes), F32),
            pltpu.SemaphoreType.DMA((rows // 8,)),
        ],
        compiler_params=pltpu.CompilerParams(vmem_limit_bytes=24 << 20),
        name="grid",
    )(tables, corners, pos, lon_tap, lat_tap, part)


def body(
    state_field,
    jacobian,
    observed,
    inverse_var,
    valid_count,
    destination,
    column,
    vertical,
    lon_taps,
    lat_taps,
):
    variables, levels, rows, lanes = state_field.shape
    records, channels = jacobian.shape[1], jacobian.shape[-1]
    sizes = (
        lax.axis_size("lon"), lax.axis_size("lat"), levels, rows, lanes, records, channels,
    )
    tables, corners, pos, lon_tap, lat_tap, part = exchange_call(
        sizes,
        state_field.reshape(variables * levels * rows, lanes),
        jacobian.transpose(0, 1, 3, 2, 4).reshape(records * levels * variables, channels),
        observed.reshape(records, channels),
        inverse_var.reshape(records, channels),
        valid_count.reshape(1, records),
        destination.reshape(1, records),
        column.reshape(1, records),
        vertical.transpose(1, 0, 2),
        lon_taps.transpose(2, 0, 1),
        lat_taps.transpose(2, 0, 1),
    )
    return grid_call(tables, corners, pos, lon_tap, lat_tap, part, levels, rows, lanes)


def solution(mesh):
    placed = (
        P(None, None, "lat", "lon"),
        P("lat", "lon", None, None, None),
        P("lat", "lon", None),
        P("lat", "lon", None),
        P("lat", "lon"),
        P("lat", "lon", None),
        P("lat", "lon"),
        P(),
        P(),
        P(),
    )
    return jax.shard_map(
        body, mesh=mesh, in_specs=placed, out_specs=P(None, None, "lat", "lon"), check_vma=False
    )
```

```python
import functools

import jax
import jax.numpy as jnp
from jax import lax
from jax.experimental import pallas as pl
from jax.experimental.pallas import tpu as pltpu
from jax.sharding import PartitionSpec as P

F32 = jnp.float32
BF16 = jnp.bfloat16


MESH = pl.DeviceIdType.MESH
NT = (((1,), (1,)), ((), ()))
TN = (((0,), (0,)), ((), ()))


def iota(shape, dim):
    return lax.broadcasted_iota(jnp.int32, shape, dim)


def far_first(ring):
    steps = [
        (z, x, c) for z in range(ring[0]) for x in range(ring[1]) for c in range(ring[2])
    ][1:]
    return sorted(
        steps, key=lambda s: -(min(s[0], ring[0] - s[0]) + min(s[1], ring[1] - s[1]) + 0.5 * s[2])
    )


def peer_at(me, step, ring):
    z, x, c = me // (ring[1] * ring[2]), (me // ring[2]) % ring[1], me % ring[2]
    z, x, c = (lax.rem(at + go, size) for at, go, size in zip((z, x, c), step, ring))
    return (z * ring[1] + x) * ring[2] + c


def exchange_kernel(
    sizes,
    state_hbm, jac_hbm, obs_hbm, inv_hbm, count_hbm, dest_hbm, col_hbm, vert_hbm, lon_hbm, lat_hbm,
    fix_ref, lat_tap, along_ref,
    state_ref, low_ref, jac_ref, map_ref, part_ref, model_ref,
    obs_ref, inv_ref, count_ref, dest_ref, col_ref, vert_ref, lon_ref, lat_ref, square_ref, mix_ref, tap_ref, lon_tap, lhs_ref, hot_ref, row_ref, pick_ref,
    rim_lhs, rim_hot,
    ask, asked, reply, replied, give, given,
    table, tables, corner, corners, spot, spots,
    load_sem, a2a_send, a2a_recv, near_send, near_recv,
):
    lons, lats, levels, rows, lanes, records, channels = sizes
    ring = (lons // 8, 4, 2)
    half = low_ref.shape[1]
    slots = 2 * table.shape[1]
    points = table.shape[1]
    span = 512
    feats = 2 * levels
    wide = 8 * feats
    me = lax.axis_index("lon")
    band = lax.axis_index("lat")
    east, west = lax.rem(me + 1, lons), lax.rem(me + lons - 1, lons)
    south, north = lax.rem(band + 1, lats), lax.rem(band + lats - 1, lats)

    loads = [
        pltpu.make_async_copy(source, target, load_sem.at[q])
        for q, (source, target) in enumerate(
            (
                (dest_hbm, dest_ref), (col_hbm, col_ref), (count_hbm, count_ref),
                (vert_hbm, vert_ref), (lon_hbm, lon_ref), (lat_hbm, lat_ref),
                (obs_hbm, obs_ref), (inv_hbm, inv_ref),
                (state_hbm, state_ref), (jac_hbm, jac_ref),
            )
        )
    ]
    for load in loads:
        load.start()

    barrier = pltpu.get_barrier_semaphore()
    peers = [peer_at(me, step, ring) for step in far_first(ring)]
    for peer in peers:
        pl.semaphore_signal(barrier, inc=1, device_id={"lon": peer}, device_id_type=MESH)

    for there in (north, south):
        pl.semaphore_signal(barrier, inc=1, device_id={"lat": there}, device_id_type=MESH)
        for side in (west, east):
            pl.semaphore_signal(
                barrier, inc=1, device_id={"lat": there, "lon": side}, device_id_type=MESH
            )

    for load in loads[:3]:
        load.wait()
    drow = dest_ref[...].astype(F32)
    prow = col_ref[...]
    irow = (prow // lanes).astype(F32)
    jrow = (prow % lanes).astype(F32)
    krow = count_ref[...].astype(F32)
    eye = iota((records, records), 0) == iota((records, records), 1)

    def column_of(row):
        return jnp.sum(jnp.where(eye, row, 0.0), axis=1, keepdims=True)

    dcol, icol, jcol, kcol = (column_of(row) for row in (drow, irow, jrow, krow))
    same = dcol == drow
    before = iota((records, records), 1) < iota((records, records), 0)
    after = iota((records, records), 0) < iota((records, records), 1)
    rank_col = jnp.sum(jnp.where(same & before, 1.0, 0.0), axis=1, keepdims=True)
    rank_row = jnp.sum(jnp.where(same & after, 1.0, 0.0), axis=0, keepdims=True)

    lane = iota((records, slots), 1)
    mine = ((lane % points) // 4 == me) & ((lane % 4).astype(F32) == rank_col)
    value = jnp.where(lane < points, icol + 1.0, jcol)
    values = jnp.where(mine, value, 0.0).astype(BF16)
    toward = jnp.where(iota((lons, records), 0).astype(F32) == drow, 1.0, 0.0).astype(BF16)
    asks = jnp.dot(toward, values, preferred_element_type=F32)
    ask[...] = asks.reshape(lons, 1, slots)

    pl.semaphore_wait(barrier, lons - 1 + 6)

    def send_all(source, target, phase):
        for peer in peers:
            pltpu.make_async_remote_copy(
                src_ref=source.at[peer],
                dst_ref=target.at[me],
                send_sem=a2a_send.at[phase],
                recv_sem=a2a_recv.at[phase],
                device_id={"lon": peer},
                device_id_type=MESH,
            ).start()

        target[me] = source[me]

    def all_of(source, target, phase):
        return pltpu.make_async_remote_copy(
            src_ref=source.at[pl.ds(0, lons - 1)],
            dst_ref=target.at[pl.ds(0, lons - 1)],
            send_sem=a2a_send.at[phase],
            recv_sem=a2a_recv.at[phase],
            device_id={"lon": east},
            device_id_type=MESH,
        )

    send_all(ask, asked, 0)

    loads[8].wait()
    for v in range(2):
        low_ref[v, half - 16 : half, :] = jnp.zeros((16, rows * lanes), BF16)

        @pl.loop(0, rows)
        def _(i):
            plane = state_ref[pl.ds(v * levels * rows + i, levels, stride=rows), :]
            start = pl.multiple_of(i * lanes, lanes)
            low_ref[v, 0:levels, pl.ds(start, lanes)] = plane.astype(BF16)

    for v in range(2):
        hit = iota((half, 384), 1) == 2 * iota((half, 384), 0) + v
        hit = hit & (iota((half, 384), 0) < levels)
        map_ref[v] = jnp.where(hit, 1.0, 0.0).astype(BF16)

    for load in loads[3:6]:
        load.wait()
    for v in range(2):
        square_ref[...] = jnp.zeros(square_ref.shape, F32)
        square_ref[0:levels, 0:levels] = vert_ref[...].astype(F32)[:, v, :]
        turned = jnp.transpose(square_ref[...])[0:half].astype(BF16)
        mix_ref[v * half : (v + 1) * half, :] = jnp.dot(
            turned[:, 0:half], map_ref[v], preferred_element_type=F32
        ).astype(BF16)
        square_ref[0:9, 0:levels] = lon_ref[...][:, v, :]
        square_ref[16:25, 0:levels] = lat_ref[...][:, v, :]
        tap_ref[v * half : (v + 1) * half, :] = jnp.transpose(square_ref[0:128, :])[0:half, 0:32]

    all_of(ask, asked, 0).wait_recv()
    seen = jnp.sum(asked[...], axis=0)
    spot[...] = seen
    neighbours = (
        ({"lat": north}, 2), ({"lat": south}, 1), ({"lon": east}, 3), ({"lon": west}, 4),
    )

    def near(source, target, target_index, sem, device):
        return pltpu.make_async_remote_copy(
            src_ref=source,
            dst_ref=target.at[target_index],
            send_sem=near_send.at[sem],
            recv_sem=near_recv.at[sem],
            device_id=device,
            device_id_type=MESH,
        )

    spot_copies = [
        near(spot, spots, index - 1, index - 1, device) for device, index in neighbours
    ]
    for copy in spot_copies:
        copy.start()

    points_row = jnp.concatenate(
        [seen[:, 0:points], seen[:, points:]]
        + [jnp.zeros((6, points), F32)],
        axis=0,
    )
    points_col = jnp.transpose(points_row)
    icol_own, jcol_own = points_col[:, 0:1] - 1.0, points_col[:, 1:2]
    spot_col = jnp.where(icol_own >= 0.0, icol_own * lanes + jcol_own, -1.0)
    chunk = 512
    for c in range(rows * lanes // chunk):
        at = (iota((points, chunk), 1) + c * chunk).astype(F32)
        pick_ref[:, c * chunk : (c + 1) * chunk] = jnp.where(spot_col == at, 1.0, 0.0).astype(BF16)
    states = jnp.zeros((points, 384), F32)
    for v in range(2):
        found = lax.dot_general(
            pick_ref[...], low_ref[v], NT, preferred_element_type=F32
        ).astype(BF16)
        states = states + jnp.dot(found, map_ref[v], preferred_element_type=F32)
    reply[...] = states.reshape(lons, 4, 384).astype(BF16)
    send_all(reply, replied, 1)

    for k in range(9):
        lon_tap[k] = jnp.broadcast_to(tap_ref[:, k : k + 1], (2 * half, points))
        lat_tap[k] = jnp.broadcast_to(tap_ref[:, 16 + k : 17 + k], (2 * half, points))

    def mark(index, i, j):
        lane = iota((points, lanes), 1)
        for k in range(9):
            hit = (lane + (k - 4)).astype(F32) == j
            hot_ref[index, k * points : (k + 1) * points, :] = jnp.where(hit, 1.0, 0.0).astype(BF16)
        row_ref[index] = jnp.broadcast_to(i, (points, lanes))

    def spread(index, pair):
        columns = []
        for i in (2 * pair, 2 * pair + 1):
            here = jnp.where(row_ref[index] == float(i), 1.0, 0.0).astype(BF16)
            columns.append(
                jnp.concatenate(
                    [hot_ref[index, k * points : (k + 1) * points, :] * here for k in range(9)],
                    axis=0,
                )
            )
        along_ref[:, 2 * pair * lanes : (2 * pair + 2) * lanes] = jnp.dot(
            lhs_ref[index], jnp.concatenate(columns, axis=1), preferred_element_type=F32
        )

    def scale(index, values):
        for k in range(9):
            lhs_ref[index, :, k * points : (k + 1) * points] = (lon_tap[k] * values).astype(BF16)

    mark(0, icol_own + 4.0, jcol_own)
    packed = fix_ref.shape[1]

    def mark_rim(index, spot):
        hit = jnp.where(spot == iota((points, packed), 1).astype(F32), 1.0, 0.0)
        rim_hot[index * points : (index + 1) * points, :] = hit.astype(BF16)

    r = iota((points, packed), 0)
    c, i, j = r // 32, (r // 4) % 4, r % 4
    for q in range(4):
        e = jnp.where(c % 2 == 0, 4 + j - q, j + 3 - q)
        least = jnp.where(c % 2 == 0, 4, 0)
        good = (e >= least) & (e < least + 4)
        spot_at = jnp.where(good, ((c // 2) * (rows + 4) + i) * 8 + e, -1)
        mark_rim(8 + q, spot_at.astype(F32))
    for load in (loads[6], loads[7], loads[9]):
        load.wait()
    all_of(reply, replied, 1).wait_recv()
    answers = replied[...].astype(F32).reshape(points, 384).astype(BF16)
    slane = iota((records, points), 1)
    take = ((slane // 4).astype(F32) == dcol) & ((slane % 4).astype(F32) == rank_col)
    picked = jnp.dot(
        jnp.where(take, 1.0, 0.0).astype(BF16), answers, preferred_element_type=F32
    )
    part_ref[:, 0:384] = picked
    part_ref[:, 384:span] = jnp.zeros((records, span - 384), F32)
    tiles = -(-wide // lanes)
    extra = feats - 2 * lanes
    eighth = iota((8, lanes), 0)

    def blocks(group):
        part = part_ref[8 * group : 8 * group + 8, :]
        turned = [pltpu.roll(part, extra * q, 1) if q else part for q in range(8)]
        line = []
        for tile in range(tiles):
            value = jnp.zeros((8, lanes), F32)
            for q in range(8):
                j = tile - 2 * q
                if 0 <= j < span // lanes:
                    value = jnp.where(
                        eighth == q, turned[q][:, j * lanes : (j + 1) * lanes], value
                    )
            line.append(value)
        return jnp.concatenate(line, axis=1)[:, 0:wide]

    def gather_blocks(value, group):
        total = jnp.zeros((8, span), F32)
        column = iota((8, span), 1)
        value = jnp.concatenate(
            [value, jnp.zeros((8, (tiles + 2) * lanes - wide), F32)], axis=1
        )
        for q in range(8):
            piece = value[:, 2 * lanes * q : 2 * lanes * q + span]
            piece = pltpu.roll(piece, span - extra * q, 1) if q else piece
            total = jnp.where((iota((8, span), 0) == q) & (column < feats), piece, total)
        part_ref[8 * group : 8 * group + 8, :] = total

    def two_groups(group):
        return jnp.concatenate(
            [
                jac_ref[group * wide : (group + 1) * wide, :],
                jac_ref[(group + 1) * wide : (group + 2) * wide, :],
            ],
            axis=1,
        )

    for g in range(0, records // 8, 2):
        left = jnp.concatenate([blocks(g), blocks(g + 1)], axis=0).astype(BF16)
        both = jnp.dot(left, two_groups(g), preferred_element_type=F32)
        model_ref[8 * g : 8 * g + 8, :] = both[0:8, 0:channels]
        model_ref[8 * g + 8 : 8 * g + 16, :] = both[8:16, channels:]
    alive = iota((records, channels), 1).astype(F32) < kcol
    weight = jnp.where(alive, inv_ref[...].astype(F32), 0.0)
    model_ref[...] = weight * (model_ref[...] - obs_ref[...].astype(F32))
    for g in range(0, records // 8, 2):
        none = jnp.zeros((8, channels), F32)
        one, two = model_ref[8 * g : 8 * g + 8, :], model_ref[8 * g + 8 : 8 * g + 16, :]
        left = jnp.concatenate(
            [jnp.concatenate([one, none], axis=1), jnp.concatenate([none, two], axis=1)], axis=0
        ).astype(BF16)
        both = lax.dot_general(left, two_groups(g), NT, preferred_element_type=F32)
        gather_blocks(both[0:8], g)
        gather_blocks(both[8:16], g + 1)
    srow = iota((points, records), 0)
    put = ((srow // 4).astype(F32) == drow) & ((srow % 4).astype(F32) == rank_row)
    gives = jnp.dot(
        jnp.where(put, 1.0, 0.0).astype(BF16),
        part_ref[:, 0:384].astype(BF16),
        preferred_element_type=F32,
    )
    give[...] = gives.reshape(lons, 4, 384).astype(BF16)
    send_all(give, given, 2)

    for copy in spot_copies:
        copy.wait()
    shifts = (4, 4 - rows, 4 + rows, 4, 4)
    stack = []
    for q in range(5):
        both = spot[...] if q == 0 else spots[q - 1]
        i1, j = both[:, 0:points], both[:, points : 2 * points]
        i = i1 - 1.0 + shifts[q]
        good = (i1 > 0.0) & (i >= 0.0) & (i < rows + 8.0)
        if q == 1:
            good = good & (iota((1, points), 0) + band > 0)
        if q == 2:
            good = good & (iota((1, points), 0) + band < lats - 1)
        stack += [jnp.where(good, i, -1000.0), j]
    where = jnp.transpose(jnp.concatenate(stack + stack[:6], axis=0))
    for q in range(4):
        i, j = where[:, 6:7], where[:, 7:8]
        e = j - (lanes - 8.0) - q
        good = (i >= 0.0) & (j >= lanes - 4.0) & (e >= 4.0)
        mark_rim(q, jnp.where(good, i * 8.0 + e, -1.0))
        i, j = where[:, 8:9], where[:, 9:10]
        e = j + 3.0 - q
        good = (i >= 0.0) & (j < 4.0) & (e < 4.0)
        mark_rim(4 + q, jnp.where(good, i * 8.0 + e, -1.0))
    for q in (1, 2):
        mark(q, where[:, 2 * q : 2 * q + 1], where[:, 2 * q + 1 : 2 * q + 2])

    all_of(give, given, 2).wait_recv()
    terms_in = given[...].astype(F32).reshape(points, 384).astype(BF16)
    parts = [
        lax.dot_general(
            mix_ref[v * half : (v + 1) * half, :], terms_in, NT, preferred_element_type=F32
        )
        for v in range(2)
    ]
    exact = jnp.concatenate(parts, axis=0)
    own = exact.astype(BF16)
    table[...] = own
    table_copies = [
        near(table, tables, index - 1, 3 + index, device) for device, index in neighbours
    ]
    for copy in table_copies:
        copy.start()
    r = iota((128, points), 0)
    c, v, i, j = r // 32, (r // 16) % 2, (r // 4) % 4, r % 4
    at_i = jnp.where(c < 2, rows - 4, 0) + i
    at_j = jnp.where(c % 2 == 0, lanes - 4, 0) + j
    both = spot[...]
    hot = (both[:, 0:points] == (at_i + 1).astype(F32)) & (both[:, points:] == at_j.astype(F32))
    cut = jnp.zeros((128, half), F32)
    for var in range(2):
        pick = jnp.where(hot & (v == var), 1.0, 0.0).astype(BF16)
        cut = cut + lax.dot_general(
            pick, own[var * half : (var + 1) * half], NT, preferred_element_type=F32
        )
    cut = jnp.concatenate([cut, jnp.zeros((128, 256 - half), F32)], axis=1)
    corner[...] = cut.reshape(4, 32, 256).astype(BF16)
    corner_copies = [
        near(corner.at[q], corners, q, 8 + q, {"lat": there, "lon": side})
        for q, (there, side) in enumerate(
            ((south, east), (south, west), (north, east), (north, west))
        )
    ]
    for copy in corner_copies:
        copy.start()
    scale(0, exact)
    for pair in range(2, rows // 2 + 2):
        spread(0, pair)
    for copy in table_copies:
        copy.wait()
    for q in (1, 2):
        scale(q, tables[q - 1].astype(F32))
    for pair in (0, 1):
        spread(1, pair)
        spread(2, rows // 2 + 2 + pair)
    left, right = tables[2].astype(F32), tables[3].astype(F32)
    for q in range(4):
        rim_lhs[:, q * points : (q + 1) * points] = (lon_tap[q] * left).astype(BF16)
        rim_lhs[:, (4 + q) * points : (5 + q) * points] = (lon_tap[q + 5] * right).astype(BF16)
    for copy in corner_copies:
        copy.wait()
    q = iota((4, 32, 256), 0)
    keep = ((q >= 2) | (q * 0 + band > 0)) & ((q < 2) | (q * 0 + band < lats - 1))
    turned = jnp.where(keep, corners[...].astype(F32), 0.0).reshape(points, 256)
    turned = jnp.transpose(turned)[0:half]
    lane = iota((half, points), 1)
    turned = jnp.concatenate(
        [jnp.where((lane // 16) % 2 == v, turned, 0.0) for v in range(2)], axis=0
    )
    leftward = (iota((2 * half, points), 1) // 32) % 2 == 0
    for q in range(4):
        factor = jnp.where(leftward, lon_tap[q], lon_tap[q + 5])
        rim_lhs[:, (8 + q) * points : (9 + q) * points] = (factor * turned).astype(BF16)
    fix_ref[...] = jnp.dot(rim_lhs[...], rim_hot[...], preferred_element_type=F32)
    for phase, source, target in ((0, ask, asked), (1, reply, replied), (2, give, given)):
        all_of(source, target, phase).wait_send()


def exchange_call(sizes, *operands):
    lons, lats, levels, rows, lanes, records, channels = sizes
    half, slots = 144, lons * 8
    points = slots // 2
    packed = -(-(rows + 8) * 8 // lanes) * lanes
    vmem = pl.BlockSpec(memory_space=pltpu.VMEM)
    hbm = pl.BlockSpec(memory_space=pltpu.HBM)
    return pl.pallas_call(
        functools.partial(exchange_kernel, sizes),
        out_shape=(
            jax.ShapeDtypeStruct((2 * half, packed), F32),
            jax.ShapeDtypeStruct((9, 2 * half, lanes), F32),
            jax.ShapeDtypeStruct((2 * half, (rows + 8) * lanes), F32),
        ),
        in_specs=[hbm] * 10,
        out_specs=(vmem,) * 3,
        scratch_shapes=[
            pltpu.VMEM((2 * levels * rows, lanes), F32),
            pltpu.VMEM((2, half, rows * lanes), BF16),
            pltpu.VMEM((records * 2 * levels, channels), BF16),
            pltpu.VMEM((2, half, 384), BF16),
            pltpu.VMEM((records, 512), F32),
            pltpu.VMEM((records, channels), F32),
            pltpu.VMEM((records, channels), BF16),
            pltpu.VMEM((records, channels), BF16),
            pltpu.VMEM((1, records), jnp.int32),
            pltpu.VMEM((1, records), jnp.int32),
            pltpu.VMEM((1, records), jnp.int32),
            pltpu.VMEM((levels, 2, levels), BF16),
            pltpu.VMEM((9, 2, levels), F32),
            pltpu.VMEM((9, 2, levels), F32),
            pltpu.VMEM((256, 256), F32),
            pltpu.VMEM((2 * half, 384), BF16),
            pltpu.VMEM((2 * half, 32), F32),
            pltpu.VMEM((9, 2 * half, lanes), F32),
            pltpu.VMEM((3, 2 * half, 9 * points), BF16),
            pltpu.VMEM((3, 9 * points, lanes), BF16),
            pltpu.VMEM((3, points, lanes), F32),
            pltpu.VMEM((points, rows * lanes), BF16),
            pltpu.VMEM((2 * half, 12 * points), BF16),
            pltpu.VMEM((12 * points, packed), BF16),
            pltpu.VMEM((lons, 1, slots), F32),
            pltpu.VMEM((lons, 1, slots), F32),
            pltpu.VMEM((lons, 4, 384), BF16),
            pltpu.VMEM((lons, 4, 384), BF16),
            pltpu.VMEM((lons, 4, 384), BF16),
            pltpu.VMEM((lons, 4, 384), BF16),
            pltpu.VMEM((2 * half, points), BF16),
            pltpu.VMEM((4, 2 * half, points), BF16),
            pltpu.VMEM((4, 32, 256), BF16),
            pltpu.VMEM((4, 32, 256), BF16),
            pltpu.VMEM((1, slots), F32),
            pltpu.VMEM((4, 1, slots), F32),
            pltpu.SemaphoreType.DMA((10,)),
            pltpu.SemaphoreType.DMA((3,)),
            pltpu.SemaphoreType.DMA((3,)),
            pltpu.SemaphoreType.DMA((12,)),
            pltpu.SemaphoreType.DMA((12,)),
        ],
        compiler_params=pltpu.CompilerParams(
            collective_id=0, has_side_effects=True, vmem_limit_bytes=36 << 20
        ),
        name="exchange",
    )(*[pltpu.with_memory_space_constraint(x, pltpu.HBM) for x in operands])


def grid_kernel(rows, halo, lanes, levels, fix_ref, lat_tap, part_ref, out_hbm, rim_ref, out_ref, sem):
    size = fix_ref.shape[0]
    wide = 2 * halo
    taps = wide + 1
    group = lanes // wide
    lane = iota((8, lanes), 1)

    def filter_rim(base):
        lat = [lat_tap[k, pl.ds(base, 8), :] for k in range(taps)]
        parts = [
            fix_ref[pl.ds(base, 8), q * lanes : (q + 1) * lanes] for q in range(rows // group + 1)
        ]
        sums = [lat[0] * part for part in parts[:-1]]
        for k in range(1, taps):
            turned = [pltpu.roll(part, lanes - wide * k, 1) for part in parts]
            here = lane < lanes - wide * k
            sums = [
                value + lat[k] * jnp.where(here, turned[q], turned[q + 1])
                for q, value in enumerate(sums)
            ]
        for q, value in enumerate(sums):
            rim_ref[pl.ds(base, 8), q * lanes : (q + 1) * lanes] = value

    @pl.loop(0, size // 32)
    def _(step):
        for part in range(4):
            filter_rim(pl.multiple_of(step * 32 + part * 8, 8))

    flat = out_ref.reshape(size * rows, lanes)
    outer = (lane < halo) | (lane >= lanes - halo)

    def filter_rows(block, base):
        lat = [lat_tap[k, pl.ds(base, 8), :] for k in range(taps)]
        start = block * 8
        q, first = divmod(start, group)
        rim = rim_ref[pl.ds(base, 8), q * lanes : (q + 1) * lanes]
        along = [
            part_ref[pl.ds(base, 8), i * lanes : (i + 1) * lanes]
            for i in range(start, start + 8 + 2 * halo)
        ]
        for r in range(8):
            turned = pltpu.roll(rim, (-(wide * (first + r) + halo)) % lanes, 1)
            out = jnp.where(outer, turned, 0.0)
            for k in range(taps):
                out = out + lat[k] * along[r + k]
            flat[pl.ds(base * rows + start + r, 8, stride=rows), :] = out

    copies = []
    for block in range(rows // 8):

        @pl.loop(0, size // 32)
        def _(step):
            for part in range(4):
                filter_rows(block, pl.multiple_of(step * 32 + part * 8, 8))

        copy = pltpu.make_async_copy(
            out_ref.at[:, pl.ds(0, levels), pl.ds(block * 8, 8), :],
            out_hbm.at[:, :, pl.ds(block * 8, 8), :],
            sem.at[block],
        )
        copy.start()
        copies.append(copy)
    for copy in copies:
        copy.wait()


def grid_call(fix, lat_tap, part, levels, rows, lanes):
    size = fix.shape[0]
    vmem = pl.BlockSpec(memory_space=pltpu.VMEM)
    return pl.pallas_call(
        functools.partial(grid_kernel, rows, 4, lanes, levels),
        out_shape=jax.ShapeDtypeStruct((2, levels, rows, lanes), F32),
        in_specs=[vmem] * 3,
        out_specs=pl.BlockSpec(memory_space=pl.ANY),
        scratch_shapes=[
            pltpu.VMEM((size, rows * 8), F32),
            pltpu.VMEM((2, size // 2, rows, lanes), F32),
            pltpu.SemaphoreType.DMA((rows // 8,)),
        ],
        compiler_params=pltpu.CompilerParams(vmem_limit_bytes=24 << 20),
        name="grid",
    )(fix, lat_tap, part)


def body(
    state_field,
    jacobian,
    observed,
    inverse_var,
    valid_count,
    destination,
    column,
    vertical,
    lon_taps,
    lat_taps,
):
    variables, levels, rows, lanes = state_field.shape
    records, channels = jacobian.shape[1], jacobian.shape[-1]
    sizes = (
        lax.axis_size("lon"), lax.axis_size("lat"), levels, rows, lanes, records, channels,
    )
    fix, lat_tap, part = exchange_call(
        sizes,
        state_field.reshape(variables * levels * rows, lanes),
        jacobian.transpose(0, 1, 3, 2, 4).reshape(records * levels * variables, channels),
        observed.reshape(records, channels),
        inverse_var.reshape(records, channels),
        valid_count.reshape(1, records),
        destination.reshape(1, records),
        column.reshape(1, records),
        vertical.transpose(1, 0, 2),
        lon_taps.transpose(2, 0, 1),
        lat_taps.transpose(2, 0, 1),
    )
    return grid_call(fix, lat_tap, part, levels, rows, lanes)


def solution(mesh):
    placed = (
        P(None, None, "lat", "lon"),
        P("lat", "lon", None, None, None),
        P("lat", "lon", None),
        P("lat", "lon", None),
        P("lat", "lon"),
        P("lat", "lon", None),
        P("lat", "lon"),
        P(),
        P(),
        P(),
    )
    return jax.shard_map(
        body, mesh=mesh, in_specs=placed, out_specs=P(None, None, "lat", "lon"), check_vma=False
    )
```

```python
import functools

import jax
import jax.numpy as jnp
from jax import lax
from jax.experimental import pallas as pl
from jax.experimental.pallas import tpu as pltpu
from jax.sharding import PartitionSpec as P

F32 = jnp.float32
BF16 = jnp.bfloat16


MESH = pl.DeviceIdType.MESH
NT = (((1,), (1,)), ((), ()))
TN = (((0,), (0,)), ((), ()))


def iota(shape, dim):
    return lax.broadcasted_iota(jnp.int32, shape, dim)


def far_first(ring):
    steps = [
        (z, x, c) for z in range(ring[0]) for x in range(ring[1]) for c in range(ring[2])
    ][1:]
    return sorted(
        steps, key=lambda s: -(min(s[0], ring[0] - s[0]) + min(s[1], ring[1] - s[1]) + 0.5 * s[2])
    )


def peer_at(me, step, ring):
    z, x, c = me // (ring[1] * ring[2]), (me // ring[2]) % ring[1], me % ring[2]
    z, x, c = (lax.rem(at + go, size) for at, go, size in zip((z, x, c), step, ring))
    return (z * ring[1] + x) * ring[2] + c


def exchange_kernel(
    sizes,
    state_hbm, jac_hbm, obs_hbm, inv_hbm, count_hbm, dest_hbm, col_hbm, vert_hbm, lon_hbm, lat_hbm,
    fix_ref, lat_tap, along_ref,
    state_ref, low_ref, jac_ref, map_ref, part_ref, model_ref,
    obs_ref, inv_ref, count_ref, dest_ref, col_ref, vert_ref, lon_ref, lat_ref, square_ref, mix_ref, tap_ref, lon_tap, lhs_ref, hot_ref, row_ref, pick_ref,
    rim_lhs, rim_hot,
    ask, asked, reply, replied, give, given,
    table, tables, corner, corners, spot, spots,
    load_sem, a2a_send, a2a_recv, near_send, near_recv,
):
    lons, lats, levels, rows, lanes, records, channels = sizes
    ring = (lons // 8, 4, 2)
    half = low_ref.shape[1]
    slots = 2 * table.shape[1]
    points = table.shape[1]
    span = 512
    feats = 2 * levels
    wide = 8 * feats
    me = lax.axis_index("lon")
    band = lax.axis_index("lat")
    east, west = lax.rem(me + 1, lons), lax.rem(me + lons - 1, lons)
    south, north = lax.rem(band + 1, lats), lax.rem(band + lats - 1, lats)

    barrier = pltpu.get_barrier_semaphore()
    peers = [peer_at(me, step, ring) for step in far_first(ring)]
    for peer in peers:
        pl.semaphore_signal(barrier, inc=1, device_id={"lon": peer}, device_id_type=MESH)

    for there in (north, south):
        pl.semaphore_signal(barrier, inc=1, device_id={"lat": there}, device_id_type=MESH)
        for side in (west, east):
            pl.semaphore_signal(
                barrier, inc=1, device_id={"lat": there, "lon": side}, device_id_type=MESH
            )

    loads = [
        pltpu.make_async_copy(source, target, load_sem.at[q])
        for q, (source, target) in enumerate(
            (
                (dest_hbm, dest_ref), (col_hbm, col_ref), (count_hbm, count_ref),
                (vert_hbm, vert_ref), (lon_hbm, lon_ref), (lat_hbm, lat_ref),
                (obs_hbm, obs_ref), (inv_hbm, inv_ref),
                (state_hbm, state_ref), (jac_hbm, jac_ref),
            )
        )
    ]
    for load in loads:
        load.start()

    for load in loads[:3]:
        load.wait()
    drow = dest_ref[...].astype(F32)
    prow = col_ref[...]
    irow = (prow // lanes).astype(F32)
    jrow = (prow % lanes).astype(F32)
    krow = count_ref[...].astype(F32)
    eye = iota((records, records), 0) == iota((records, records), 1)

    def column_of(row):
        return jnp.sum(jnp.where(eye, row, 0.0), axis=1, keepdims=True)

    dcol, icol, jcol, kcol = (column_of(row) for row in (drow, irow, jrow, krow))
    same = dcol == drow
    before = iota((records, records), 1) < iota((records, records), 0)
    after = iota((records, records), 0) < iota((records, records), 1)
    rank_col = jnp.sum(jnp.where(same & before, 1.0, 0.0), axis=1, keepdims=True)
    rank_row = jnp.sum(jnp.where(same & after, 1.0, 0.0), axis=0, keepdims=True)

    lane = iota((records, slots), 1)
    mine = ((lane % points) // 4 == me) & ((lane % 4).astype(F32) == rank_col)
    value = jnp.where(lane < points, icol + 1.0, jcol)
    values = jnp.where(mine, value, 0.0).astype(BF16)
    toward = jnp.where(iota((lons, records), 0).astype(F32) == drow, 1.0, 0.0).astype(BF16)
    asks = jnp.dot(toward, values, preferred_element_type=F32)
    ask[...] = asks.reshape(lons, 1, slots)

    pl.semaphore_wait(barrier, lons - 1 + 6)

    def send_all(source, target, phase):
        for peer in peers:
            pltpu.make_async_remote_copy(
                src_ref=source.at[peer],
                dst_ref=target.at[me],
                send_sem=a2a_send.at[phase],
                recv_sem=a2a_recv.at[phase],
                device_id={"lon": peer},
                device_id_type=MESH,
            ).start()

        target[me] = source[me]

    def all_of(source, target, phase):
        return pltpu.make_async_remote_copy(
            src_ref=source.at[pl.ds(0, lons - 1)],
            dst_ref=target.at[pl.ds(0, lons - 1)],
            send_sem=a2a_send.at[phase],
            recv_sem=a2a_recv.at[phase],
            device_id={"lon": east},
            device_id_type=MESH,
        )

    send_all(ask, asked, 0)

    loads[8].wait()
    for v in range(2):
        low_ref[v, half - 16 : half, :] = jnp.zeros((16, rows * lanes), BF16)

        @pl.loop(0, rows)
        def _(i):
            plane = state_ref[pl.ds(v * levels * rows + i, levels, stride=rows), :]
            start = pl.multiple_of(i * lanes, lanes)
            low_ref[v, 0:levels, pl.ds(start, lanes)] = plane.astype(BF16)

    for v in range(2):
        hit = iota((half, 384), 1) == 2 * iota((half, 384), 0) + v
        hit = hit & (iota((half, 384), 0) < levels)
        map_ref[v] = jnp.where(hit, 1.0, 0.0).astype(BF16)

    for load in loads[3:6]:
        load.wait()
    for v in range(2):
        square_ref[...] = jnp.zeros(square_ref.shape, F32)
        square_ref[0:levels, 0:levels] = vert_ref[...].astype(F32)[:, v, :]
        turned = jnp.transpose(square_ref[...])[0:half].astype(BF16)
        mix_ref[v * half : (v + 1) * half, :] = jnp.dot(
            turned[:, 0:half], map_ref[v], preferred_element_type=F32
        ).astype(BF16)
        square_ref[0:9, 0:levels] = lon_ref[...][:, v, :]
        square_ref[16:25, 0:levels] = lat_ref[...][:, v, :]
        tap_ref[v * half : (v + 1) * half, :] = jnp.transpose(square_ref[0:128, :])[0:half, 0:32]

    all_of(ask, asked, 0).wait_recv()
    seen = jnp.sum(asked[...], axis=0)
    spot[...] = seen
    neighbours = (
        ({"lat": north}, 2), ({"lat": south}, 1), ({"lon": east}, 3), ({"lon": west}, 4),
    )

    def near(source, target, target_index, sem, device):
        return pltpu.make_async_remote_copy(
            src_ref=source,
            dst_ref=target.at[target_index],
            send_sem=near_send.at[sem],
            recv_sem=near_recv.at[sem],
            device_id=device,
            device_id_type=MESH,
        )

    spot_copies = [
        near(spot, spots, index - 1, index - 1, device) for device, index in neighbours
    ]
    for copy in spot_copies:
        copy.start()

    points_row = jnp.concatenate(
        [seen[:, 0:points], seen[:, points:]]
        + [jnp.zeros((6, points), F32)],
        axis=0,
    )
    points_col = jnp.transpose(points_row)
    icol_own, jcol_own = points_col[:, 0:1] - 1.0, points_col[:, 1:2]
    spot_col = jnp.where(icol_own >= 0.0, icol_own * lanes + jcol_own, -1.0)
    chunk = 512
    for c in range(rows * lanes // chunk):
        at = (iota((points, chunk), 1) + c * chunk).astype(F32)
        pick_ref[:, c * chunk : (c + 1) * chunk] = jnp.where(spot_col == at, 1.0, 0.0).astype(BF16)
    states = jnp.zeros((points, 384), F32)
    for v in range(2):
        found = lax.dot_general(
            pick_ref[...], low_ref[v], NT, preferred_element_type=F32
        ).astype(BF16)
        states = states + jnp.dot(found, map_ref[v], preferred_element_type=F32)
    reply[...] = states.reshape(lons, 4, 384).astype(BF16)
    send_all(reply, replied, 1)

    for k in range(9):
        lon_tap[k] = jnp.broadcast_to(tap_ref[:, k : k + 1], (2 * half, points))
        lat_tap[k] = jnp.broadcast_to(tap_ref[:, 16 + k : 17 + k], (2 * half, points))

    def mark(index, i, j):
        lane = iota((points, lanes), 1)
        for k in range(9):
            hit = (lane + (k - 4)).astype(F32) == j
            hot_ref[index, k * points : (k + 1) * points, :] = jnp.where(hit, 1.0, 0.0).astype(BF16)
        row_ref[index] = jnp.broadcast_to(i, (points, lanes))

    def spread(index, pair):
        columns = []
        for i in (2 * pair, 2 * pair + 1):
            here = jnp.where(row_ref[index] == float(i), 1.0, 0.0).astype(BF16)
            columns.append(
                jnp.concatenate(
                    [hot_ref[index, k * points : (k + 1) * points, :] * here for k in range(9)],
                    axis=0,
                )
            )
        along_ref[:, 2 * pair * lanes : (2 * pair + 2) * lanes] = jnp.dot(
            lhs_ref[index], jnp.concatenate(columns, axis=1), preferred_element_type=F32
        )

    def scale(index, values):
        for k in range(9):
            lhs_ref[index, :, k * points : (k + 1) * points] = (lon_tap[k] * values).astype(BF16)

    mark(0, icol_own + 4.0, jcol_own)
    packed = fix_ref.shape[1]

    def mark_rim(index, spot):
        hit = jnp.where(spot == iota((points, packed), 1).astype(F32), 1.0, 0.0)
        rim_hot[index * points : (index + 1) * points, :] = hit.astype(BF16)

    r = iota((points, packed), 0)
    c, i, j = r // 32, (r // 4) % 4, r % 4
    for q in range(4):
        e = jnp.where(c % 2 == 0, 4 + j - q, j + 3 - q)
        least = jnp.where(c % 2 == 0, 4, 0)
        good = (e >= least) & (e < least + 4)
        spot_at = jnp.where(good, ((c // 2) * (rows + 4) + i) * 8 + e, -1)
        mark_rim(8 + q, spot_at.astype(F32))
    for load in (loads[6], loads[7], loads[9]):
        load.wait()
    all_of(reply, replied, 1).wait_recv()
    answers = replied[...].astype(F32).reshape(points, 384).astype(BF16)
    slane = iota((records, points), 1)
    take = ((slane // 4).astype(F32) == dcol) & ((slane % 4).astype(F32) == rank_col)
    picked = jnp.dot(
        jnp.where(take, 1.0, 0.0).astype(BF16), answers, preferred_element_type=F32
    )
    part_ref[:, 0:384] = picked
    part_ref[:, 384:span] = jnp.zeros((records, span - 384), F32)
    tiles = -(-wide // lanes)
    extra = feats - 2 * lanes
    eighth = iota((8, lanes), 0)

    def blocks(group):
        part = part_ref[8 * group : 8 * group + 8, :]
        turned = [pltpu.roll(part, extra * q, 1) if q else part for q in range(8)]
        line = []
        for tile in range(tiles):
            value = jnp.zeros((8, lanes), F32)
            for q in range(8):
                j = tile - 2 * q
                if 0 <= j < span // lanes:
                    value = jnp.where(
                        eighth == q, turned[q][:, j * lanes : (j + 1) * lanes], value
                    )
            line.append(value)
        return jnp.concatenate(line, axis=1)[:, 0:wide]

    def gather_blocks(value, group):
        total = jnp.zeros((8, span), F32)
        column = iota((8, span), 1)
        value = jnp.concatenate(
            [value, jnp.zeros((8, (tiles + 2) * lanes - wide), F32)], axis=1
        )
        for q in range(8):
            piece = value[:, 2 * lanes * q : 2 * lanes * q + span]
            piece = pltpu.roll(piece, span - extra * q, 1) if q else piece
            total = jnp.where((iota((8, span), 0) == q) & (column < feats), piece, total)
        part_ref[8 * group : 8 * group + 8, :] = total

    def two_groups(group):
        return jnp.concatenate(
            [
                jac_ref[group * wide : (group + 1) * wide, :],
                jac_ref[(group + 1) * wide : (group + 2) * wide, :],
            ],
            axis=1,
        )

    for g in range(0, records // 8, 2):
        left = jnp.concatenate([blocks(g), blocks(g + 1)], axis=0).astype(BF16)
        both = jnp.dot(left, two_groups(g), preferred_element_type=F32)
        model_ref[8 * g : 8 * g + 8, :] = both[0:8, 0:channels]
        model_ref[8 * g + 8 : 8 * g + 16, :] = both[8:16, channels:]
    alive = iota((records, channels), 1).astype(F32) < kcol
    weight = jnp.where(alive, inv_ref[...].astype(F32), 0.0)
    model_ref[...] = weight * (model_ref[...] - obs_ref[...].astype(F32))
    for g in range(0, records // 8, 2):
        none = jnp.zeros((8, channels), F32)
        one, two = model_ref[8 * g : 8 * g + 8, :], model_ref[8 * g + 8 : 8 * g + 16, :]
        left = jnp.concatenate(
            [jnp.concatenate([one, none], axis=1), jnp.concatenate([none, two], axis=1)], axis=0
        ).astype(BF16)
        both = lax.dot_general(left, two_groups(g), NT, preferred_element_type=F32)
        gather_blocks(both[0:8], g)
        gather_blocks(both[8:16], g + 1)
    srow = iota((points, records), 0)
    put = ((srow // 4).astype(F32) == drow) & ((srow % 4).astype(F32) == rank_row)
    gives = jnp.dot(
        jnp.where(put, 1.0, 0.0).astype(BF16),
        part_ref[:, 0:384].astype(BF16),
        preferred_element_type=F32,
    )
    give[...] = gives.reshape(lons, 4, 384).astype(BF16)
    send_all(give, given, 2)

    for copy in spot_copies:
        copy.wait()
    shifts = (4, 4 - rows, 4 + rows, 4, 4)
    stack = []
    for q in range(5):
        both = spot[...] if q == 0 else spots[q - 1]
        i1, j = both[:, 0:points], both[:, points : 2 * points]
        i = i1 - 1.0 + shifts[q]
        good = (i1 > 0.0) & (i >= 0.0) & (i < rows + 8.0)
        if q == 1:
            good = good & (iota((1, points), 0) + band > 0)
        if q == 2:
            good = good & (iota((1, points), 0) + band < lats - 1)
        stack += [jnp.where(good, i, -1000.0), j]
    where = jnp.transpose(jnp.concatenate(stack + stack[:6], axis=0))
    for q in range(4):
        i, j = where[:, 6:7], where[:, 7:8]
        e = j - (lanes - 8.0) - q
        good = (i >= 0.0) & (j >= lanes - 4.0) & (e >= 4.0)
        mark_rim(q, jnp.where(good, i * 8.0 + e, -1.0))
        i, j = where[:, 8:9], where[:, 9:10]
        e = j + 3.0 - q
        good = (i >= 0.0) & (j < 4.0) & (e < 4.0)
        mark_rim(4 + q, jnp.where(good, i * 8.0 + e, -1.0))
    for q in (1, 2):
        mark(q, where[:, 2 * q : 2 * q + 1], where[:, 2 * q + 1 : 2 * q + 2])

    all_of(give, given, 2).wait_recv()
    terms_in = given[...].astype(F32).reshape(points, 384).astype(BF16)
    parts = [
        lax.dot_general(
            mix_ref[v * half : (v + 1) * half, :], terms_in, NT, preferred_element_type=F32
        )
        for v in range(2)
    ]
    exact = jnp.concatenate(parts, axis=0)
    own = exact.astype(BF16)
    table[...] = own
    table_copies = [
        near(table, tables, index - 1, 3 + index, device) for device, index in neighbours
    ]
    for copy in table_copies:
        copy.start()
    r = iota((128, points), 0)
    c, v, i, j = r // 32, (r // 16) % 2, (r // 4) % 4, r % 4
    at_i = jnp.where(c < 2, rows - 4, 0) + i
    at_j = jnp.where(c % 2 == 0, lanes - 4, 0) + j
    both = spot[...]
    hot = (both[:, 0:points] == (at_i + 1).astype(F32)) & (both[:, points:] == at_j.astype(F32))
    cut = jnp.zeros((128, half), F32)
    for var in range(2):
        pick = jnp.where(hot & (v == var), 1.0, 0.0).astype(BF16)
        cut = cut + lax.dot_general(
            pick, own[var * half : (var + 1) * half], NT, preferred_element_type=F32
        )
    cut = jnp.concatenate([cut, jnp.zeros((128, 256 - half), F32)], axis=1)
    corner[...] = cut.reshape(4, 32, 256).astype(BF16)
    corner_copies = [
        near(corner.at[q], corners, q, 8 + q, {"lat": there, "lon": side})
        for q, (there, side) in enumerate(
            ((south, east), (south, west), (north, east), (north, west))
        )
    ]
    for copy in corner_copies:
        copy.start()
    scale(0, exact)
    for pair in range(2, rows // 2 + 2):
        spread(0, pair)
    for copy in table_copies:
        copy.wait()
    for q in (1, 2):
        scale(q, tables[q - 1].astype(F32))
    for pair in (0, 1):
        spread(1, pair)
        spread(2, rows // 2 + 2 + pair)
    left, right = tables[2].astype(F32), tables[3].astype(F32)
    for q in range(4):
        rim_lhs[:, q * points : (q + 1) * points] = (lon_tap[q] * left).astype(BF16)
        rim_lhs[:, (4 + q) * points : (5 + q) * points] = (lon_tap[q + 5] * right).astype(BF16)
    for copy in corner_copies:
        copy.wait()
    q = iota((4, 32, 256), 0)
    keep = ((q >= 2) | (q * 0 + band > 0)) & ((q < 2) | (q * 0 + band < lats - 1))
    turned = jnp.where(keep, corners[...].astype(F32), 0.0).reshape(points, 256)
    turned = jnp.transpose(turned)[0:half]
    lane = iota((half, points), 1)
    turned = jnp.concatenate(
        [jnp.where((lane // 16) % 2 == v, turned, 0.0) for v in range(2)], axis=0
    )
    leftward = (iota((2 * half, points), 1) // 32) % 2 == 0
    for q in range(4):
        factor = jnp.where(leftward, lon_tap[q], lon_tap[q + 5])
        rim_lhs[:, (8 + q) * points : (9 + q) * points] = (factor * turned).astype(BF16)
    fix_ref[...] = jnp.dot(rim_lhs[...], rim_hot[...], preferred_element_type=F32)
    for phase, source, target in ((0, ask, asked), (1, reply, replied), (2, give, given)):
        all_of(source, target, phase).wait_send()


def exchange_call(sizes, *operands):
    lons, lats, levels, rows, lanes, records, channels = sizes
    half, slots = 144, lons * 8
    points = slots // 2
    packed = -(-(rows + 8) * 8 // lanes) * lanes
    vmem = pl.BlockSpec(memory_space=pltpu.VMEM)
    hbm = pl.BlockSpec(memory_space=pltpu.HBM)
    return pl.pallas_call(
        functools.partial(exchange_kernel, sizes),
        out_shape=(
            jax.ShapeDtypeStruct((2 * half, packed), F32),
            jax.ShapeDtypeStruct((9, 2 * half, lanes), F32),
            jax.ShapeDtypeStruct((2 * half, (rows + 8) * lanes), F32),
        ),
        in_specs=[hbm] * 10,
        out_specs=(vmem,) * 3,
        scratch_shapes=[
            pltpu.VMEM((2 * levels * rows, lanes), F32),
            pltpu.VMEM((2, half, rows * lanes), BF16),
            pltpu.VMEM((records * 2 * levels, channels), BF16),
            pltpu.VMEM((2, half, 384), BF16),
            pltpu.VMEM((records, 512), F32),
            pltpu.VMEM((records, channels), F32),
            pltpu.VMEM((records, channels), BF16),
            pltpu.VMEM((records, channels), BF16),
            pltpu.VMEM((1, records), jnp.int32),
            pltpu.VMEM((1, records), jnp.int32),
            pltpu.VMEM((1, records), jnp.int32),
            pltpu.VMEM((levels, 2, levels), BF16),
            pltpu.VMEM((9, 2, levels), F32),
            pltpu.VMEM((9, 2, levels), F32),
            pltpu.VMEM((256, 256), F32),
            pltpu.VMEM((2 * half, 384), BF16),
            pltpu.VMEM((2 * half, 32), F32),
            pltpu.VMEM((9, 2 * half, lanes), F32),
            pltpu.VMEM((3, 2 * half, 9 * points), BF16),
            pltpu.VMEM((3, 9 * points, lanes), BF16),
            pltpu.VMEM((3, points, lanes), F32),
            pltpu.VMEM((points, rows * lanes), BF16),
            pltpu.VMEM((2 * half, 12 * points), BF16),
            pltpu.VMEM((12 * points, packed), BF16),
            pltpu.VMEM((lons, 1, slots), F32),
            pltpu.VMEM((lons, 1, slots), F32),
            pltpu.VMEM((lons, 4, 384), BF16),
            pltpu.VMEM((lons, 4, 384), BF16),
            pltpu.VMEM((lons, 4, 384), BF16),
            pltpu.VMEM((lons, 4, 384), BF16),
            pltpu.VMEM((2 * half, points), BF16),
            pltpu.VMEM((4, 2 * half, points), BF16),
            pltpu.VMEM((4, 32, 256), BF16),
            pltpu.VMEM((4, 32, 256), BF16),
            pltpu.VMEM((1, slots), F32),
            pltpu.VMEM((4, 1, slots), F32),
            pltpu.SemaphoreType.DMA((10,)),
            pltpu.SemaphoreType.DMA((3,)),
            pltpu.SemaphoreType.DMA((3,)),
            pltpu.SemaphoreType.DMA((12,)),
            pltpu.SemaphoreType.DMA((12,)),
        ],
        compiler_params=pltpu.CompilerParams(
            collective_id=0, has_side_effects=True, vmem_limit_bytes=36 << 20
        ),
        name="exchange",
    )(*[pltpu.with_memory_space_constraint(x, pltpu.HBM) for x in operands])


def grid_kernel(rows, halo, lanes, levels, fix_ref, lat_tap, part_ref, out_hbm, rim_ref, out_ref, sem):
    size = fix_ref.shape[0]
    wide = 2 * halo
    taps = wide + 1
    group = lanes // wide
    lane = iota((8, lanes), 1)

    def filter_rim(base):
        lat = [lat_tap[k, pl.ds(base, 8), :] for k in range(taps)]
        parts = [
            fix_ref[pl.ds(base, 8), q * lanes : (q + 1) * lanes] for q in range(rows // group + 1)
        ]
        sums = [lat[0] * part for part in parts[:-1]]
        for k in range(1, taps):
            turned = [pltpu.roll(part, lanes - wide * k, 1) for part in parts]
            here = lane < lanes - wide * k
            sums = [
                value + lat[k] * jnp.where(here, turned[q], turned[q + 1])
                for q, value in enumerate(sums)
            ]
        for q, value in enumerate(sums):
            rim_ref[pl.ds(base, 8), q * lanes : (q + 1) * lanes] = value

    for base in range(0, size, 8):
        filter_rim(base)

    flat = out_ref.reshape(size * rows, lanes)
    outer = (lane < halo) | (lane >= lanes - halo)

    def filter_rows(block, base):
        lat = [lat_tap[k, pl.ds(base, 8), :] for k in range(taps)]
        start = block * 8
        q, first = divmod(start, group)
        rim = rim_ref[pl.ds(base, 8), q * lanes : (q + 1) * lanes]
        along = [
            part_ref[pl.ds(base, 8), i * lanes : (i + 1) * lanes]
            for i in range(start, start + 8 + 2 * halo)
        ]
        for r in range(8):
            turned = pltpu.roll(rim, (-(wide * (first + r) + halo)) % lanes, 1)
            out = lat[0] * along[r]
            for k in range(1, taps):
                out = out + lat[k] * along[r + k]
            out = out + jnp.where(outer, turned, 0.0)
            flat[pl.ds(base * rows + start + r, 8, stride=rows), :] = out

    copies = []
    for block in range(rows // 8):
        for v in range(2):
            for part in range(size // 16):
                filter_rows(block, v * (size // 2) + part * 8)
            copy = pltpu.make_async_copy(
                out_ref.at[v, pl.ds(0, levels), pl.ds(block * 8, 8), :],
                out_hbm.at[v, :, pl.ds(block * 8, 8), :],
                sem.at[2 * block + v],
            )
            copy.start()
            copies.append(copy)
    for copy in copies:
        copy.wait()


def grid_call(fix, lat_tap, part, levels, rows, lanes):
    size = fix.shape[0]
    vmem = pl.BlockSpec(memory_space=pltpu.VMEM)
    return pl.pallas_call(
        functools.partial(grid_kernel, rows, 4, lanes, levels),
        out_shape=jax.ShapeDtypeStruct((2, levels, rows, lanes), F32),
        in_specs=[vmem] * 3,
        out_specs=pl.BlockSpec(memory_space=pl.ANY),
        scratch_shapes=[
            pltpu.VMEM((size, rows * 8), F32),
            pltpu.VMEM((2, size // 2, rows, lanes), F32),
            pltpu.SemaphoreType.DMA((rows // 4,)),
        ],
        compiler_params=pltpu.CompilerParams(vmem_limit_bytes=24 << 20),
        name="grid",
    )(fix, lat_tap, part)


def body(
    state_field,
    jacobian,
    observed,
    inverse_var,
    valid_count,
    destination,
    column,
    vertical,
    lon_taps,
    lat_taps,
):
    variables, levels, rows, lanes = state_field.shape
    records, channels = jacobian.shape[1], jacobian.shape[-1]
    sizes = (
        lax.axis_size("lon"), lax.axis_size("lat"), levels, rows, lanes, records, channels,
    )
    fix, lat_tap, part = exchange_call(
        sizes,
        state_field.reshape(variables * levels * rows, lanes),
        jacobian.transpose(0, 1, 3, 2, 4).reshape(records * levels * variables, channels),
        observed.reshape(records, channels),
        inverse_var.reshape(records, channels),
        valid_count.reshape(1, records),
        destination.reshape(1, records),
        column.reshape(1, records),
        vertical.transpose(1, 0, 2),
        lon_taps.transpose(2, 0, 1),
        lat_taps.transpose(2, 0, 1),
    )
    return grid_call(fix, lat_tap, part, levels, rows, lanes)


def solution(mesh):
    placed = (
        P(None, None, "lat", "lon"),
        P("lat", "lon", None, None, None),
        P("lat", "lon", None),
        P("lat", "lon", None),
        P("lat", "lon"),
        P("lat", "lon", None),
        P("lat", "lon"),
        P(),
        P(),
        P(),
    )
    return jax.shard_map(
        body, mesh=mesh, in_specs=placed, out_specs=P(None, None, "lat", "lon"), check_vma=False
    )
```

```python
import functools

import jax
import jax.numpy as jnp
from jax import lax
from jax.experimental import pallas as pl
from jax.experimental.pallas import tpu as pltpu
from jax.sharding import PartitionSpec as P

F32 = jnp.float32
BF16 = jnp.bfloat16


MESH = pl.DeviceIdType.MESH
NT = (((1,), (1,)), ((), ()))
TN = (((0,), (0,)), ((), ()))


def iota(shape, dim):
    return lax.broadcasted_iota(jnp.int32, shape, dim)


def far_first(ring):
    steps = [
        (z, x, c) for z in range(ring[0]) for x in range(ring[1]) for c in range(ring[2])
    ][1:]
    return sorted(
        steps, key=lambda s: -(min(s[0], ring[0] - s[0]) + min(s[1], ring[1] - s[1]) + 0.5 * s[2])
    )


def peer_at(me, step, ring):
    z, x, c = me // (ring[1] * ring[2]), (me // ring[2]) % ring[1], me % ring[2]
    z, x, c = (lax.rem(at + go, size) for at, go, size in zip((z, x, c), step, ring))
    return (z * ring[1] + x) * ring[2] + c


def exchange_kernel(
    sizes,
    state_hbm, jac_hbm, obs_hbm, inv_hbm, count_hbm, dest_hbm, col_hbm, vert_hbm, lon_hbm, lat_hbm,
    fix_ref, lat_tap, along_ref,
    state_ref, low_ref, jac_ref, map_ref, part_ref, model_ref,
    obs_ref, inv_ref, count_ref, dest_ref, col_ref, vert_ref, lon_ref, lat_ref, square_ref, mix_ref, tap_ref, lon_tap, lhs_ref, hot_ref, row_ref, pick_ref,
    rim_lhs, rim_hot,
    ask, asked, reply, replied, give, given,
    table, tables, corner, corners, spot, spots,
    load_sem, a2a_send, a2a_recv, near_send, near_recv,
):
    lons, lats, levels, rows, lanes, records, channels = sizes
    ring = (lons // 8, 4, 2)
    half = low_ref.shape[1]
    slots = 2 * table.shape[1]
    points = table.shape[1]
    span = 512
    feats = 2 * levels
    wide = 8 * feats
    me = lax.axis_index("lon")
    band = lax.axis_index("lat")
    east, west = lax.rem(me + 1, lons), lax.rem(me + lons - 1, lons)
    south, north = lax.rem(band + 1, lats), lax.rem(band + lats - 1, lats)

    barrier = pltpu.get_barrier_semaphore()
    peers = [peer_at(me, step, ring) for step in far_first(ring)]
    for peer in peers:
        pl.semaphore_signal(barrier, inc=1, device_id={"lon": peer}, device_id_type=MESH)

    for there in (north, south):
        pl.semaphore_signal(barrier, inc=1, device_id={"lat": there}, device_id_type=MESH)
        for side in (west, east):
            pl.semaphore_signal(
                barrier, inc=1, device_id={"lat": there, "lon": side}, device_id_type=MESH
            )

    loads = [
        pltpu.make_async_copy(source, target, load_sem.at[q])
        for q, (source, target) in enumerate(
            (
                (dest_hbm, dest_ref), (col_hbm, col_ref), (count_hbm, count_ref),
                (vert_hbm, vert_ref), (lon_hbm, lon_ref), (lat_hbm, lat_ref),
                (obs_hbm, obs_ref), (inv_hbm, inv_ref),
                (state_hbm, state_ref), (jac_hbm, jac_ref),
            )
        )
    ]
    for load in loads:
        load.start()

    for load in loads[:3]:
        load.wait()
    drow = dest_ref[...].astype(F32)
    prow = col_ref[...]
    irow = (prow // lanes).astype(F32)
    jrow = (prow % lanes).astype(F32)
    krow = count_ref[...].astype(F32)
    eye = iota((records, records), 0) == iota((records, records), 1)

    def column_of(row):
        return jnp.sum(jnp.where(eye, row, 0.0), axis=1, keepdims=True)

    dcol, icol, jcol, kcol = (column_of(row) for row in (drow, irow, jrow, krow))
    same = dcol == drow
    before = iota((records, records), 1) < iota((records, records), 0)
    after = iota((records, records), 0) < iota((records, records), 1)
    rank_col = jnp.sum(jnp.where(same & before, 1.0, 0.0), axis=1, keepdims=True)
    rank_row = jnp.sum(jnp.where(same & after, 1.0, 0.0), axis=0, keepdims=True)

    lane = iota((records, slots), 1)
    mine = ((lane % points) // 4 == me) & ((lane % 4).astype(F32) == rank_col)
    value = jnp.where(lane < points, icol + 1.0, jcol)
    values = jnp.where(mine, value, 0.0).astype(BF16)
    toward = jnp.where(iota((lons, records), 0).astype(F32) == drow, 1.0, 0.0).astype(BF16)
    asks = jnp.dot(toward, values, preferred_element_type=F32)
    ask[...] = asks.reshape(lons, 1, slots)

    pl.semaphore_wait(barrier, lons - 1 + 6)

    def send_all(source, target, phase):
        for peer in peers:
            pltpu.make_async_remote_copy(
                src_ref=source.at[peer],
                dst_ref=target.at[me],
                send_sem=a2a_send.at[phase],
                recv_sem=a2a_recv.at[phase],
                device_id={"lon": peer},
                device_id_type=MESH,
            ).start()

        target[me] = source[me]

    def all_of(source, target, phase):
        return pltpu.make_async_remote_copy(
            src_ref=source.at[pl.ds(0, lons - 1)],
            dst_ref=target.at[pl.ds(0, lons - 1)],
            send_sem=a2a_send.at[phase],
            recv_sem=a2a_recv.at[phase],
            device_id={"lon": east},
            device_id_type=MESH,
        )

    send_all(ask, asked, 0)

    loads[8].wait()
    for v in range(2):
        low_ref[v, half - 16 : half, :] = jnp.zeros((16, rows * lanes), BF16)

        @pl.loop(0, rows)
        def _(i):
            plane = state_ref[pl.ds(v * levels * rows + i, levels, stride=rows), :]
            start = pl.multiple_of(i * lanes, lanes)
            low_ref[v, 0:levels, pl.ds(start, lanes)] = plane.astype(BF16)

    for v in range(2):
        hit = iota((half, 384), 1) == 2 * iota((half, 384), 0) + v
        hit = hit & (iota((half, 384), 0) < levels)
        map_ref[v] = jnp.where(hit, 1.0, 0.0).astype(BF16)

    for load in loads[3:6]:
        load.wait()
    for v in range(2):
        square_ref[...] = jnp.zeros(square_ref.shape, F32)
        square_ref[0:levels, 0:levels] = vert_ref[...].astype(F32)[:, v, :]
        turned = jnp.transpose(square_ref[...])[0:half].astype(BF16)
        mix_ref[v * half : (v + 1) * half, :] = jnp.dot(
            turned[:, 0:half], map_ref[v], preferred_element_type=F32
        ).astype(BF16)
        square_ref[0:9, 0:levels] = lon_ref[...][:, v, :]
        square_ref[16:25, 0:levels] = lat_ref[...][:, v, :]
        tap_ref[v * half : (v + 1) * half, :] = jnp.transpose(square_ref[0:128, :])[0:half, 0:32]

    all_of(ask, asked, 0).wait_recv()
    seen = jnp.sum(asked[...], axis=0)
    spot[...] = seen
    neighbours = (
        ({"lat": north}, 2), ({"lat": south}, 1), ({"lon": east}, 3), ({"lon": west}, 4),
    )

    def near(source, target, target_index, sem, device):
        return pltpu.make_async_remote_copy(
            src_ref=source,
            dst_ref=target.at[target_index],
            send_sem=near_send.at[sem],
            recv_sem=near_recv.at[sem],
            device_id=device,
            device_id_type=MESH,
        )

    spot_copies = [
        near(spot, spots, index - 1, index - 1, device) for device, index in neighbours
    ]
    for copy in spot_copies:
        copy.start()

    points_row = jnp.concatenate(
        [seen[:, 0:points], seen[:, points:]]
        + [jnp.zeros((6, points), F32)],
        axis=0,
    )
    points_col = jnp.transpose(points_row)
    icol_own, jcol_own = points_col[:, 0:1] - 1.0, points_col[:, 1:2]
    spot_col = jnp.where(icol_own >= 0.0, icol_own * lanes + jcol_own, -1.0)
    chunk = 512
    for c in range(rows * lanes // chunk):
        at = (iota((points, chunk), 1) + c * chunk).astype(F32)
        pick_ref[:, c * chunk : (c + 1) * chunk] = jnp.where(spot_col == at, 1.0, 0.0).astype(BF16)
    states = jnp.zeros((points, 384), F32)
    for v in range(2):
        found = lax.dot_general(
            pick_ref[...], low_ref[v], NT, preferred_element_type=F32
        ).astype(BF16)
        states = states + jnp.dot(found, map_ref[v], preferred_element_type=F32)
    reply[...] = states.reshape(lons, 4, 384).astype(BF16)
    send_all(reply, replied, 1)

    for k in range(9):
        lon_tap[k] = jnp.broadcast_to(tap_ref[:, k : k + 1], (2 * half, points))
        lat_tap[k] = jnp.broadcast_to(tap_ref[:, 16 + k : 17 + k], (2 * half, points))

    def mark(index, i, j):
        lane = iota((points, lanes), 1)
        for k in range(9):
            hit = (lane + (k - 4)).astype(F32) == j
            hot_ref[index, k * points : (k + 1) * points, :] = jnp.where(hit, 1.0, 0.0).astype(BF16)
        row_ref[index] = jnp.broadcast_to(i, (points, lanes))

    def spread(index, pair):
        columns = []
        for i in (2 * pair, 2 * pair + 1):
            here = jnp.where(row_ref[index] == float(i), 1.0, 0.0).astype(BF16)
            columns.append(
                jnp.concatenate(
                    [hot_ref[index, k * points : (k + 1) * points, :] * here for k in range(9)],
                    axis=0,
                )
            )
        along_ref[:, 2 * pair * lanes : (2 * pair + 2) * lanes] = jnp.dot(
            lhs_ref[index], jnp.concatenate(columns, axis=1), preferred_element_type=F32
        )

    def scale(index, values):
        for k in range(9):
            lhs_ref[index, :, k * points : (k + 1) * points] = (lon_tap[k] * values).astype(BF16)

    mark(0, icol_own + 4.0, jcol_own)
    packed = fix_ref.shape[1]

    def mark_rim(index, spot):
        hit = jnp.where(spot == iota((points, packed), 1).astype(F32), 1.0, 0.0)
        rim_hot[index * points : (index + 1) * points, :] = hit.astype(BF16)

    r = iota((points, packed), 0)
    c, i, j = (r // 16) % 4, (r // 4) % 4, r % 4
    for p in range(2):
        q = 2 * p + r // 64
        e = jnp.where(c % 2 == 0, 4 + j - q, j + 3 - q)
        least = jnp.where(c % 2 == 0, 4, 0)
        good = (e >= least) & (e < least + 4)
        spot_at = jnp.where(good, ((c // 2) * (rows + 4) + i) * 8 + e, -1)
        mark_rim(8 + p, spot_at.astype(F32))
    for load in (loads[6], loads[7], loads[9]):
        load.wait()
    all_of(reply, replied, 1).wait_recv()
    answers = replied[...].astype(F32).reshape(points, 384).astype(BF16)
    slane = iota((records, points), 1)
    take = ((slane // 4).astype(F32) == dcol) & ((slane % 4).astype(F32) == rank_col)
    picked = jnp.dot(
        jnp.where(take, 1.0, 0.0).astype(BF16), answers, preferred_element_type=F32
    )
    part_ref[:, 0:384] = picked
    part_ref[:, 384:span] = jnp.zeros((records, span - 384), F32)
    tiles = -(-wide // lanes)
    extra = feats - 2 * lanes
    eighth = iota((8, lanes), 0)

    def blocks(group):
        part = part_ref[8 * group : 8 * group + 8, :]
        turned = [pltpu.roll(part, extra * q, 1) if q else part for q in range(8)]
        line = []
        for tile in range(tiles):
            value = jnp.zeros((8, lanes), F32)
            for q in range(8):
                j = tile - 2 * q
                if 0 <= j < span // lanes:
                    value = jnp.where(
                        eighth == q, turned[q][:, j * lanes : (j + 1) * lanes], value
                    )
            line.append(value)
        return jnp.concatenate(line, axis=1)[:, 0:wide]

    def gather_blocks(value, group):
        total = jnp.zeros((8, span), F32)
        column = iota((8, span), 1)
        value = jnp.concatenate(
            [value, jnp.zeros((8, (tiles + 2) * lanes - wide), F32)], axis=1
        )
        for q in range(8):
            piece = value[:, 2 * lanes * q : 2 * lanes * q + span]
            piece = pltpu.roll(piece, span - extra * q, 1) if q else piece
            total = jnp.where((iota((8, span), 0) == q) & (column < feats), piece, total)
        part_ref[8 * group : 8 * group + 8, :] = total

    def two_groups(group):
        return jnp.concatenate(
            [
                jac_ref[group * wide : (group + 1) * wide, :],
                jac_ref[(group + 1) * wide : (group + 2) * wide, :],
            ],
            axis=1,
        )

    for g in range(0, records // 8, 2):
        left = jnp.concatenate([blocks(g), blocks(g + 1)], axis=0).astype(BF16)
        both = jnp.dot(left, two_groups(g), preferred_element_type=F32)
        model_ref[8 * g : 8 * g + 8, :] = both[0:8, 0:channels]
        model_ref[8 * g + 8 : 8 * g + 16, :] = both[8:16, channels:]
    alive = iota((records, channels), 1).astype(F32) < kcol
    weight = jnp.where(alive, inv_ref[...].astype(F32), 0.0)
    model_ref[...] = weight * (model_ref[...] - obs_ref[...].astype(F32))
    for g in range(0, records // 8, 2):
        none = jnp.zeros((8, channels), F32)
        one, two = model_ref[8 * g : 8 * g + 8, :], model_ref[8 * g + 8 : 8 * g + 16, :]
        left = jnp.concatenate(
            [jnp.concatenate([one, none], axis=1), jnp.concatenate([none, two], axis=1)], axis=0
        ).astype(BF16)
        both = lax.dot_general(left, two_groups(g), NT, preferred_element_type=F32)
        gather_blocks(both[0:8], g)
        gather_blocks(both[8:16], g + 1)
    srow = iota((points, records), 0)
    put = ((srow // 4).astype(F32) == drow) & ((srow % 4).astype(F32) == rank_row)
    gives = jnp.dot(
        jnp.where(put, 1.0, 0.0).astype(BF16),
        part_ref[:, 0:384].astype(BF16),
        preferred_element_type=F32,
    )
    give[...] = gives.reshape(lons, 4, 384).astype(BF16)
    send_all(give, given, 2)

    for copy in spot_copies:
        copy.wait()
    shifts = (4, 4 - rows, 4 + rows, 4, 4)
    stack = []
    for q in range(5):
        both = spot[...] if q == 0 else spots[q - 1]
        i1, j = both[:, 0:points], both[:, points : 2 * points]
        i = i1 - 1.0 + shifts[q]
        good = (i1 > 0.0) & (i >= 0.0) & (i < rows + 8.0)
        if q == 1:
            good = good & (iota((1, points), 0) + band > 0)
        if q == 2:
            good = good & (iota((1, points), 0) + band < lats - 1)
        stack += [jnp.where(good, i, -1000.0), j]
    where = jnp.transpose(jnp.concatenate(stack + stack[:6], axis=0))
    for q in range(4):
        i, j = where[:, 6:7], where[:, 7:8]
        e = j - (lanes - 8.0) - q
        good = (i >= 0.0) & (j >= lanes - 4.0) & (e >= 4.0)
        mark_rim(q, jnp.where(good, i * 8.0 + e, -1.0))
        i, j = where[:, 8:9], where[:, 9:10]
        e = j + 3.0 - q
        good = (i >= 0.0) & (j < 4.0) & (e < 4.0)
        mark_rim(4 + q, jnp.where(good, i * 8.0 + e, -1.0))
    for q in (1, 2):
        mark(q, where[:, 2 * q : 2 * q + 1], where[:, 2 * q + 1 : 2 * q + 2])

    r = iota((64, points), 0)
    c, i, j = r // 16, (r // 4) % 4, r % 4
    at_i = jnp.where(c < 2, rows - 4, 0) + i
    at_j = jnp.where(c % 2 == 0, lanes - 4, 0) + j
    both = spot[...]
    hot = (both[:, 0:points] == (at_i + 1).astype(F32)) & (both[:, points:] == at_j.astype(F32))
    hot = jnp.where(hot, 1.0, 0.0).astype(BF16)

    all_of(give, given, 2).wait_recv()
    terms_in = given[...].astype(F32).reshape(points, 384).astype(BF16)
    cut = jnp.dot(hot, terms_in, preferred_element_type=F32)
    corner[...] = cut.reshape(4, 16, 384).astype(BF16)
    corner_copies = [
        near(corner.at[q], corners, q, 8 + q, {"lat": there, "lon": side})
        for q, (there, side) in enumerate(
            ((south, east), (south, west), (north, east), (north, west))
        )
    ]
    for copy in corner_copies:
        copy.start()
    parts = [
        lax.dot_general(
            mix_ref[v * half : (v + 1) * half, :], terms_in, NT, preferred_element_type=F32
        )
        for v in range(2)
    ]
    exact = jnp.concatenate(parts, axis=0)
    own = exact.astype(BF16)
    table[...] = own
    table_copies = [
        near(table, tables, index - 1, 3 + index, device) for device, index in neighbours
    ]
    for copy in table_copies:
        copy.start()
    scale(0, exact)
    for pair in range(2, rows // 2 + 2):
        spread(0, pair)
    for copy in table_copies[2:]:
        copy.wait()
    left, right = tables[2].astype(F32), tables[3].astype(F32)
    for q in range(4):
        rim_lhs[:, q * points : (q + 1) * points] = (lon_tap[q] * left).astype(BF16)
        rim_lhs[:, (4 + q) * points : (5 + q) * points] = (lon_tap[q + 5] * right).astype(BF16)
    for copy in table_copies[:2]:
        copy.wait()
    for q in (1, 2):
        scale(q, tables[q - 1].astype(F32))
    for pair in (0, 1):
        spread(1, pair)
        spread(2, rows // 2 + 2 + pair)
    for copy in corner_copies:
        copy.wait()
    q = iota((4, 16, 384), 0)
    keep = ((q >= 2) | (q * 0 + band > 0)) & ((q < 2) | (q * 0 + band < lats - 1))
    pieces = jnp.where(keep, corners[...].astype(F32), 0.0).reshape(64, 384)
    pieces = jnp.concatenate([pieces, pieces], axis=0).astype(BF16)
    turned = jnp.concatenate(
        [
            lax.dot_general(
                mix_ref[v * half : (v + 1) * half, :], pieces, NT, preferred_element_type=F32
            )
            for v in range(2)
        ],
        axis=0,
    )
    lane = iota((2 * half, points), 1)
    leftward = (lane // 16) % 2 == 0
    for p in range(2):
        even = jnp.where(leftward, lon_tap[2 * p], lon_tap[2 * p + 5])
        odd = jnp.where(leftward, lon_tap[2 * p + 1], lon_tap[2 * p + 6])
        factor = jnp.where(lane < 64, even, odd)
        rim_lhs[:, (8 + p) * points : (9 + p) * points] = (factor * turned).astype(BF16)
    fix_ref[...] = jnp.dot(rim_lhs[...], rim_hot[...], preferred_element_type=F32)
    for phase, source, target in ((0, ask, asked), (1, reply, replied), (2, give, given)):
        all_of(source, target, phase).wait_send()


def exchange_call(sizes, *operands):
    lons, lats, levels, rows, lanes, records, channels = sizes
    half, slots = 144, lons * 8
    points = slots // 2
    packed = -(-(rows + 8) * 8 // lanes) * lanes
    vmem = pl.BlockSpec(memory_space=pltpu.VMEM)
    hbm = pl.BlockSpec(memory_space=pltpu.HBM)
    return pl.pallas_call(
        functools.partial(exchange_kernel, sizes),
        out_shape=(
            jax.ShapeDtypeStruct((2 * half, packed), F32),
            jax.ShapeDtypeStruct((9, 2 * half, lanes), F32),
            jax.ShapeDtypeStruct((2 * half, (rows + 8) * lanes), F32),
        ),
        in_specs=[hbm] * 10,
        out_specs=(vmem,) * 3,
        scratch_shapes=[
            pltpu.VMEM((2 * levels * rows, lanes), F32),
            pltpu.VMEM((2, half, rows * lanes), BF16),
            pltpu.VMEM((records * 2 * levels, channels), BF16),
            pltpu.VMEM((2, half, 384), BF16),
            pltpu.VMEM((records, 512), F32),
            pltpu.VMEM((records, channels), F32),
            pltpu.VMEM((records, channels), BF16),
            pltpu.VMEM((records, channels), BF16),
            pltpu.VMEM((1, records), jnp.int32),
            pltpu.VMEM((1, records), jnp.int32),
            pltpu.VMEM((1, records), jnp.int32),
            pltpu.VMEM((levels, 2, levels), BF16),
            pltpu.VMEM((9, 2, levels), F32),
            pltpu.VMEM((9, 2, levels), F32),
            pltpu.VMEM((256, 256), F32),
            pltpu.VMEM((2 * half, 384), BF16),
            pltpu.VMEM((2 * half, 32), F32),
            pltpu.VMEM((9, 2 * half, lanes), F32),
            pltpu.VMEM((3, 2 * half, 9 * points), BF16),
            pltpu.VMEM((3, 9 * points, lanes), BF16),
            pltpu.VMEM((3, points, lanes), F32),
            pltpu.VMEM((points, rows * lanes), BF16),
            pltpu.VMEM((2 * half, 10 * points), BF16),
            pltpu.VMEM((10 * points, packed), BF16),
            pltpu.VMEM((lons, 1, slots), F32),
            pltpu.VMEM((lons, 1, slots), F32),
            pltpu.VMEM((lons, 4, 384), BF16),
            pltpu.VMEM((lons, 4, 384), BF16),
            pltpu.VMEM((lons, 4, 384), BF16),
            pltpu.VMEM((lons, 4, 384), BF16),
            pltpu.VMEM((2 * half, points), BF16),
            pltpu.VMEM((4, 2 * half, points), BF16),
            pltpu.VMEM((4, 16, 384), BF16),
            pltpu.VMEM((4, 16, 384), BF16),
            pltpu.VMEM((1, slots), F32),
            pltpu.VMEM((4, 1, slots), F32),
            pltpu.SemaphoreType.DMA((10,)),
            pltpu.SemaphoreType.DMA((3,)),
            pltpu.SemaphoreType.DMA((3,)),
            pltpu.SemaphoreType.DMA((12,)),
            pltpu.SemaphoreType.DMA((12,)),
        ],
        compiler_params=pltpu.CompilerParams(
            collective_id=0, has_side_effects=True, vmem_limit_bytes=36 << 20
        ),
        name="exchange",
    )(*[pltpu.with_memory_space_constraint(x, pltpu.HBM) for x in operands])


def grid_kernel(rows, halo, lanes, levels, fix_ref, lat_tap, part_ref, out_hbm, rim_ref, out_ref, sem):
    size = fix_ref.shape[0]
    wide = 2 * halo
    taps = wide + 1
    group = lanes // wide
    lane = iota((8, lanes), 1)

    def filter_rim(base):
        lat = [lat_tap[k, pl.ds(base, 8), :] for k in range(taps)]
        parts = [
            fix_ref[pl.ds(base, 8), q * lanes : (q + 1) * lanes] for q in range(rows // group + 1)
        ]
        sums = [lat[0] * part for part in parts[:-1]]
        for k in range(1, taps):
            turned = [pltpu.roll(part, lanes - wide * k, 1) for part in parts]
            here = lane < lanes - wide * k
            sums = [
                value + lat[k] * jnp.where(here, turned[q], turned[q + 1])
                for q, value in enumerate(sums)
            ]
        for q, value in enumerate(sums):
            rim_ref[pl.ds(base, 8), q * lanes : (q + 1) * lanes] = value

    for base in range(0, size, 8):
        filter_rim(base)

    flat = out_ref.reshape(size * rows, lanes)
    outer = (lane < halo) | (lane >= lanes - halo)

    def filter_rows(block, base):
        lat = [lat_tap[k, pl.ds(base, 8), :] for k in range(taps)]
        start = block * 8
        q, first = divmod(start, group)
        rim = rim_ref[pl.ds(base, 8), q * lanes : (q + 1) * lanes]
        along = [
            part_ref[pl.ds(base, 8), i * lanes : (i + 1) * lanes]
            for i in range(start, start + 8 + 2 * halo)
        ]
        for r in range(8):
            turned = pltpu.roll(rim, (-(wide * (first + r) + halo)) % lanes, 1)
            out = lat[0] * along[r]
            for k in range(1, taps):
                out = out + lat[k] * along[r + k]
            out = out + jnp.where(outer, turned, 0.0)
            flat[pl.ds(base * rows + start + r, 8, stride=rows), :] = out

    copies = []
    for block in range(rows // 8):
        for v in range(2):
            for part in range(size // 16):
                filter_rows(block, v * (size // 2) + part * 8)
            copy = pltpu.make_async_copy(
                out_ref.at[v, pl.ds(0, levels), pl.ds(block * 8, 8), :],
                out_hbm.at[v, :, pl.ds(block * 8, 8), :],
                sem.at[2 * block + v],
            )
            copy.start()
            copies.append(copy)
    for copy in copies:
        copy.wait()


def grid_call(fix, lat_tap, part, levels, rows, lanes):
    size = fix.shape[0]
    vmem = pl.BlockSpec(memory_space=pltpu.VMEM)
    return pl.pallas_call(
        functools.partial(grid_kernel, rows, 4, lanes, levels),
        out_shape=jax.ShapeDtypeStruct((2, levels, rows, lanes), F32),
        in_specs=[vmem] * 3,
        out_specs=pl.BlockSpec(memory_space=pl.ANY),
        scratch_shapes=[
            pltpu.VMEM((size, rows * 8), F32),
            pltpu.VMEM((2, size // 2, rows, lanes), F32),
            pltpu.SemaphoreType.DMA((rows // 4,)),
        ],
        compiler_params=pltpu.CompilerParams(vmem_limit_bytes=24 << 20),
        name="grid",
    )(fix, lat_tap, part)


def body(
    state_field,
    jacobian,
    observed,
    inverse_var,
    valid_count,
    destination,
    column,
    vertical,
    lon_taps,
    lat_taps,
):
    variables, levels, rows, lanes = state_field.shape
    records, channels = jacobian.shape[1], jacobian.shape[-1]
    sizes = (
        lax.axis_size("lon"), lax.axis_size("lat"), levels, rows, lanes, records, channels,
    )
    fix, lat_tap, part = exchange_call(
        sizes,
        state_field.reshape(variables * levels * rows, lanes),
        jacobian.transpose(0, 1, 3, 2, 4).reshape(records * levels * variables, channels),
        observed.reshape(records, channels),
        inverse_var.reshape(records, channels),
        valid_count.reshape(1, records),
        destination.reshape(1, records),
        column.reshape(1, records),
        vertical.transpose(1, 0, 2),
        lon_taps.transpose(2, 0, 1),
        lat_taps.transpose(2, 0, 1),
    )
    return grid_call(fix, lat_tap, part, levels, rows, lanes)


def solution(mesh):
    placed = (
        P(None, None, "lat", "lon"),
        P("lat", "lon", None, None, None),
        P("lat", "lon", None),
        P("lat", "lon", None),
        P("lat", "lon"),
        P("lat", "lon", None),
        P("lat", "lon"),
        P(),
        P(),
        P(),
    )
    return jax.shard_map(
        body, mesh=mesh, in_specs=placed, out_specs=P(None, None, "lat", "lon"), check_vma=False
    )
```

```python
import functools

import jax
import jax.numpy as jnp
from jax import lax
from jax.experimental import pallas as pl
from jax.experimental.pallas import tpu as pltpu
from jax.sharding import PartitionSpec as P

F32 = jnp.float32
BF16 = jnp.bfloat16


MESH = pl.DeviceIdType.MESH
NT = (((1,), (1,)), ((), ()))
TN = (((0,), (0,)), ((), ()))


def iota(shape, dim):
    return lax.broadcasted_iota(jnp.int32, shape, dim)


def far_first(ring):
    steps = [
        (z, x, c) for z in range(ring[0]) for x in range(ring[1]) for c in range(ring[2])
    ][1:]
    return sorted(
        steps, key=lambda s: -(min(s[0], ring[0] - s[0]) + min(s[1], ring[1] - s[1]) + 0.5 * s[2])
    )


def peer_at(me, step, ring):
    z, x, c = me // (ring[1] * ring[2]), (me // ring[2]) % ring[1], me % ring[2]
    z, x, c = (lax.rem(at + go, size) for at, go, size in zip((z, x, c), step, ring))
    return (z * ring[1] + x) * ring[2] + c


def exchange_kernel(
    sizes,
    state_hbm, jac_hbm, obs_hbm, inv_hbm, count_hbm, dest_hbm, col_hbm, vert_hbm, lon_hbm, lat_hbm,
    fix_ref, lat_tap, along_ref, mid_ref,
    state_ref, low_ref, jac_ref, map_ref, part_ref, model_ref,
    obs_ref, inv_ref, count_ref, dest_ref, col_ref, vert_ref, lon_ref, lat_ref, square_ref, mix_ref, tap_ref, lon_tap, lhs_ref, hot_ref, row_ref, pick_ref,
    rim_lhs, rim_hot,
    ask, asked, reply, replied, give, given,
    table, tables, corner, corners, spot, spots,
    load_sem, a2a_send, a2a_recv, near_send, near_recv,
):
    lons, lats, levels, rows, lanes, records, channels = sizes
    ring = (lons // 8, 4, 2)
    half = low_ref.shape[1]
    slots = 2 * table.shape[1]
    points = table.shape[1]
    span = 512
    feats = 2 * levels
    wide = 8 * feats
    me = lax.axis_index("lon")
    band = lax.axis_index("lat")
    east, west = lax.rem(me + 1, lons), lax.rem(me + lons - 1, lons)
    south, north = lax.rem(band + 1, lats), lax.rem(band + lats - 1, lats)

    barrier = pltpu.get_barrier_semaphore()
    peers = [peer_at(me, step, ring) for step in far_first(ring)]
    for peer in peers:
        pl.semaphore_signal(barrier, inc=1, device_id={"lon": peer}, device_id_type=MESH)

    for there in (north, south):
        pl.semaphore_signal(barrier, inc=1, device_id={"lat": there}, device_id_type=MESH)
        for side in (west, east):
            pl.semaphore_signal(
                barrier, inc=1, device_id={"lat": there, "lon": side}, device_id_type=MESH
            )

    loads = [
        pltpu.make_async_copy(source, target, load_sem.at[q])
        for q, (source, target) in enumerate(
            (
                (dest_hbm, dest_ref), (col_hbm, col_ref), (count_hbm, count_ref),
                (vert_hbm, vert_ref), (lon_hbm, lon_ref), (lat_hbm, lat_ref),
                (obs_hbm, obs_ref), (inv_hbm, inv_ref),
                (state_hbm, state_ref), (jac_hbm, jac_ref),
            )
        )
    ]
    for load in loads:
        load.start()

    for load in loads[:3]:
        load.wait()
    drow = dest_ref[...].astype(F32)
    prow = col_ref[...]
    irow = (prow // lanes).astype(F32)
    jrow = (prow % lanes).astype(F32)
    krow = count_ref[...].astype(F32)
    eye = iota((records, records), 0) == iota((records, records), 1)

    def column_of(row):
        return jnp.sum(jnp.where(eye, row, 0.0), axis=1, keepdims=True)

    dcol, icol, jcol, kcol = (column_of(row) for row in (drow, irow, jrow, krow))
    same = dcol == drow
    before = iota((records, records), 1) < iota((records, records), 0)
    after = iota((records, records), 0) < iota((records, records), 1)
    rank_col = jnp.sum(jnp.where(same & before, 1.0, 0.0), axis=1, keepdims=True)
    rank_row = jnp.sum(jnp.where(same & after, 1.0, 0.0), axis=0, keepdims=True)

    lane = iota((records, slots), 1)
    mine = ((lane % points) // 4 == me) & ((lane % 4).astype(F32) == rank_col)
    value = jnp.where(lane < points, icol + 1.0, jcol)
    values = jnp.where(mine, value, 0.0).astype(BF16)
    toward = jnp.where(iota((lons, records), 0).astype(F32) == drow, 1.0, 0.0).astype(BF16)
    asks = jnp.dot(toward, values, preferred_element_type=F32)
    ask[...] = asks.reshape(lons, 1, slots)

    pl.semaphore_wait(barrier, lons - 1 + 6)

    def send_all(source, target, phase):
        for peer in peers:
            pltpu.make_async_remote_copy(
                src_ref=source.at[peer],
                dst_ref=target.at[me],
                send_sem=a2a_send.at[phase],
                recv_sem=a2a_recv.at[phase],
                device_id={"lon": peer},
                device_id_type=MESH,
            ).start()

        target[me] = source[me]

    def all_of(source, target, phase):
        return pltpu.make_async_remote_copy(
            src_ref=source.at[pl.ds(0, lons - 1)],
            dst_ref=target.at[pl.ds(0, lons - 1)],
            send_sem=a2a_send.at[phase],
            recv_sem=a2a_recv.at[phase],
            device_id={"lon": east},
            device_id_type=MESH,
        )

    send_all(ask, asked, 0)

    loads[8].wait()
    for v in range(2):
        low_ref[v, half - 16 : half, :] = jnp.zeros((16, rows * lanes), BF16)

        @pl.loop(0, rows)
        def _(i):
            plane = state_ref[pl.ds(v * levels * rows + i, levels, stride=rows), :]
            start = pl.multiple_of(i * lanes, lanes)
            low_ref[v, 0:levels, pl.ds(start, lanes)] = plane.astype(BF16)

    for v in range(2):
        hit = iota((half, 384), 1) == 2 * iota((half, 384), 0) + v
        hit = hit & (iota((half, 384), 0) < levels)
        map_ref[v] = jnp.where(hit, 1.0, 0.0).astype(BF16)

    for load in loads[3:6]:
        load.wait()
    for v in range(2):
        square_ref[...] = jnp.zeros(square_ref.shape, F32)
        square_ref[0:levels, 0:levels] = vert_ref[...].astype(F32)[:, v, :]
        turned = jnp.transpose(square_ref[...])[0:half].astype(BF16)
        mix_ref[v * half : (v + 1) * half, :] = jnp.dot(
            turned[:, 0:half], map_ref[v], preferred_element_type=F32
        ).astype(BF16)
        square_ref[0:9, 0:levels] = lon_ref[...][:, v, :]
        square_ref[16:25, 0:levels] = lat_ref[...][:, v, :]
        tap_ref[v * half : (v + 1) * half, :] = jnp.transpose(square_ref[0:128, :])[0:half, 0:32]

    all_of(ask, asked, 0).wait_recv()
    seen = jnp.sum(asked[...], axis=0)
    spot[...] = seen
    neighbours = (
        ({"lat": north}, 2), ({"lat": south}, 1), ({"lon": east}, 3), ({"lon": west}, 4),
    )

    def near(source, target, target_index, sem, device):
        return pltpu.make_async_remote_copy(
            src_ref=source,
            dst_ref=target.at[target_index],
            send_sem=near_send.at[sem],
            recv_sem=near_recv.at[sem],
            device_id=device,
            device_id_type=MESH,
        )

    spot_copies = [
        near(spot, spots, index - 1, index - 1, device) for device, index in neighbours
    ]
    for copy in spot_copies:
        copy.start()

    points_row = jnp.concatenate(
        [seen[:, 0:points], seen[:, points:]]
        + [jnp.zeros((6, points), F32)],
        axis=0,
    )
    points_col = jnp.transpose(points_row)
    icol_own, jcol_own = points_col[:, 0:1] - 1.0, points_col[:, 1:2]
    spot_col = jnp.where(icol_own >= 0.0, icol_own * lanes + jcol_own, -1.0)
    chunk = 512
    for c in range(rows * lanes // chunk):
        at = (iota((points, chunk), 1) + c * chunk).astype(F32)
        pick_ref[:, c * chunk : (c + 1) * chunk] = jnp.where(spot_col == at, 1.0, 0.0).astype(BF16)
    states = jnp.zeros((points, 384), F32)
    for v in range(2):
        found = lax.dot_general(
            pick_ref[...], low_ref[v], NT, preferred_element_type=F32
        ).astype(BF16)
        states = states + jnp.dot(found, map_ref[v], preferred_element_type=F32)
    reply[...] = states.reshape(lons, 4, 384).astype(BF16)
    send_all(reply, replied, 1)

    for k in range(9):
        lon_tap[k] = jnp.broadcast_to(tap_ref[:, k : k + 1], (2 * half, points))
        lat_tap[k] = jnp.broadcast_to(tap_ref[:, 16 + k : 17 + k], (2 * half, points))

    def mark(index, i, j):
        lane = iota((points, lanes), 1)
        for k in range(9):
            hit = (lane + (k - 4)).astype(F32) == j
            hot_ref[index, k * points : (k + 1) * points, :] = jnp.where(hit, 1.0, 0.0).astype(BF16)
        row_ref[index] = jnp.broadcast_to(i, (points, lanes))

    def spread(index, pair):
        columns = []
        for i in (2 * pair, 2 * pair + 1):
            here = jnp.where(row_ref[index] == float(i), 1.0, 0.0).astype(BF16)
            columns.append(
                jnp.concatenate(
                    [hot_ref[index, k * points : (k + 1) * points, :] * here for k in range(9)],
                    axis=0,
                )
            )
        along_ref[:, 2 * pair * lanes : (2 * pair + 2) * lanes] = jnp.dot(
            lhs_ref[index], jnp.concatenate(columns, axis=1), preferred_element_type=F32
        )

    def scale(index, values):
        for k in range(9):
            lhs_ref[index, :, k * points : (k + 1) * points] = (lon_tap[k] * values).astype(BF16)

    mark(0, icol_own + 4.0, jcol_own)
    packed = fix_ref.shape[1]

    def mark_rim(index, spot):
        hit = jnp.where(spot == iota((points, packed), 1).astype(F32), 1.0, 0.0)
        rim_hot[index * points : (index + 1) * points, :] = hit.astype(BF16)

    r = iota((points, packed), 0)
    c, i, j = r // 32, (r // 4) % 4, r % 4
    for q in range(4):
        e = jnp.where(c % 2 == 0, 4 + j - q, j + 3 - q)
        least = jnp.where(c % 2 == 0, 4, 0)
        good = (e >= least) & (e < least + 4)
        spot_at = jnp.where(good, ((c // 2) * (rows + 4) + i) * 8 + e, -1)
        mark_rim(8 + q, spot_at.astype(F32))
    for load in (loads[6], loads[7], loads[9]):
        load.wait()
    all_of(reply, replied, 1).wait_recv()
    answers = replied[...].astype(F32).reshape(points, 384).astype(BF16)
    slane = iota((records, points), 1)
    take = ((slane // 4).astype(F32) == dcol) & ((slane % 4).astype(F32) == rank_col)
    picked = jnp.dot(
        jnp.where(take, 1.0, 0.0).astype(BF16), answers, preferred_element_type=F32
    )
    part_ref[:, 0:384] = picked
    part_ref[:, 384:span] = jnp.zeros((records, span - 384), F32)
    tiles = -(-wide // lanes)
    extra = feats - 2 * lanes
    eighth = iota((8, lanes), 0)

    def blocks(group):
        part = part_ref[8 * group : 8 * group + 8, :]
        turned = [pltpu.roll(part, extra * q, 1) if q else part for q in range(8)]
        line = []
        for tile in range(tiles):
            value = jnp.zeros((8, lanes), F32)
            for q in range(8):
                j = tile - 2 * q
                if 0 <= j < span // lanes:
                    value = jnp.where(
                        eighth == q, turned[q][:, j * lanes : (j + 1) * lanes], value
                    )
            line.append(value)
        return jnp.concatenate(line, axis=1)[:, 0:wide]

    def gather_blocks(value, group):
        total = jnp.zeros((8, span), F32)
        column = iota((8, span), 1)
        value = jnp.concatenate(
            [value, jnp.zeros((8, (tiles + 2) * lanes - wide), F32)], axis=1
        )
        for q in range(8):
            piece = value[:, 2 * lanes * q : 2 * lanes * q + span]
            piece = pltpu.roll(piece, span - extra * q, 1) if q else piece
            total = jnp.where((iota((8, span), 0) == q) & (column < feats), piece, total)
        part_ref[8 * group : 8 * group + 8, :] = total

    def two_groups(group):
        return jnp.concatenate(
            [
                jac_ref[group * wide : (group + 1) * wide, :],
                jac_ref[(group + 1) * wide : (group + 2) * wide, :],
            ],
            axis=1,
        )

    for g in range(0, records // 8, 2):
        left = jnp.concatenate([blocks(g), blocks(g + 1)], axis=0).astype(BF16)
        both = jnp.dot(left, two_groups(g), preferred_element_type=F32)
        model_ref[8 * g : 8 * g + 8, :] = both[0:8, 0:channels]
        model_ref[8 * g + 8 : 8 * g + 16, :] = both[8:16, channels:]
    alive = iota((records, channels), 1).astype(F32) < kcol
    weight = jnp.where(alive, inv_ref[...].astype(F32), 0.0)
    model_ref[...] = weight * (model_ref[...] - obs_ref[...].astype(F32))
    for g in range(0, records // 8, 2):
        none = jnp.zeros((8, channels), F32)
        one, two = model_ref[8 * g : 8 * g + 8, :], model_ref[8 * g + 8 : 8 * g + 16, :]
        left = jnp.concatenate(
            [jnp.concatenate([one, none], axis=1), jnp.concatenate([none, two], axis=1)], axis=0
        ).astype(BF16)
        both = lax.dot_general(left, two_groups(g), NT, preferred_element_type=F32)
        gather_blocks(both[0:8], g)
        gather_blocks(both[8:16], g + 1)
    srow = iota((points, records), 0)
    put = ((srow // 4).astype(F32) == drow) & ((srow % 4).astype(F32) == rank_row)
    gives = jnp.dot(
        jnp.where(put, 1.0, 0.0).astype(BF16),
        part_ref[:, 0:384].astype(BF16),
        preferred_element_type=F32,
    )
    give[...] = gives.reshape(lons, 4, 384).astype(BF16)
    send_all(give, given, 2)

    for copy in spot_copies:
        copy.wait()
    shifts = (4, 4 - rows, 4 + rows, 4, 4)
    stack = []
    for q in range(5):
        both = spot[...] if q == 0 else spots[q - 1]
        i1, j = both[:, 0:points], both[:, points : 2 * points]
        i = i1 - 1.0 + shifts[q]
        good = (i1 > 0.0) & (i >= 0.0) & (i < rows + 8.0)
        if q == 1:
            good = good & (iota((1, points), 0) + band > 0)
        if q == 2:
            good = good & (iota((1, points), 0) + band < lats - 1)
        stack += [jnp.where(good, i, -1000.0), j]
    where = jnp.transpose(jnp.concatenate(stack + stack[:6], axis=0))
    for q in range(4):
        i, j = where[:, 6:7], where[:, 7:8]
        e = j - (lanes - 8.0) - q
        good = (i >= 0.0) & (j >= lanes - 4.0) & (e >= 4.0)
        mark_rim(q, jnp.where(good, i * 8.0 + e, -1.0))
        i, j = where[:, 8:9], where[:, 9:10]
        e = j + 3.0 - q
        good = (i >= 0.0) & (j < 4.0) & (e < 4.0)
        mark_rim(4 + q, jnp.where(good, i * 8.0 + e, -1.0))
    for q in (1, 2):
        mark(q, where[:, 2 * q : 2 * q + 1], where[:, 2 * q + 1 : 2 * q + 2])

    all_of(give, given, 2).wait_recv()
    terms_in = given[...].astype(F32).reshape(points, 384).astype(BF16)
    parts = [
        lax.dot_general(
            mix_ref[v * half : (v + 1) * half, :], terms_in, NT, preferred_element_type=F32
        )
        for v in range(2)
    ]
    exact = jnp.concatenate(parts, axis=0)
    own = exact.astype(BF16)
    table[...] = own
    table_copies = [
        near(table, tables, index - 1, 3 + index, device) for device, index in neighbours
    ]
    for copy in table_copies:
        copy.start()
    r = iota((128, points), 0)
    c, v, i, j = r // 32, (r // 16) % 2, (r // 4) % 4, r % 4
    at_i = jnp.where(c < 2, rows - 4, 0) + i
    at_j = jnp.where(c % 2 == 0, lanes - 4, 0) + j
    both = spot[...]
    hot = (both[:, 0:points] == (at_i + 1).astype(F32)) & (both[:, points:] == at_j.astype(F32))
    cut = jnp.zeros((128, half), F32)
    for var in range(2):
        pick = jnp.where(hot & (v == var), 1.0, 0.0).astype(BF16)
        cut = cut + lax.dot_general(
            pick, own[var * half : (var + 1) * half], NT, preferred_element_type=F32
        )
    cut = jnp.concatenate([cut, jnp.zeros((128, 256 - half), F32)], axis=1)
    corner[...] = cut.reshape(4, 32, 256).astype(BF16)
    corner_copies = [
        near(corner.at[q], corners, q, 8 + q, {"lat": there, "lon": side})
        for q, (there, side) in enumerate(
            ((south, east), (south, west), (north, east), (north, west))
        )
    ]
    for copy in corner_copies:
        copy.start()
    scale(0, exact)
    for pair in range(2, rows // 2 + 2):
        spread(0, pair)
    for base in range(0, 2 * half, 8):
        lat = [lat_tap[k, base : base + 8, :] for k in range(9)]
        lines = [along_ref[base : base + 8, i * lanes : (i + 1) * lanes] for i in range(8, rows)]
        for r in range(rows - 16):
            value = lat[0] * lines[r]
            for k in range(1, 9):
                value = value + lat[k] * lines[r + k]
            mid_ref[base : base + 8, r * lanes : (r + 1) * lanes] = value
    for copy in table_copies:
        copy.wait()
    for q in (1, 2):
        scale(q, tables[q - 1].astype(F32))
    for pair in (0, 1):
        spread(1, pair)
        spread(2, rows // 2 + 2 + pair)
    left, right = tables[2].astype(F32), tables[3].astype(F32)
    for q in range(4):
        rim_lhs[:, q * points : (q + 1) * points] = (lon_tap[q] * left).astype(BF16)
        rim_lhs[:, (4 + q) * points : (5 + q) * points] = (lon_tap[q + 5] * right).astype(BF16)
    for copy in corner_copies:
        copy.wait()
    q = iota((4, 32, 256), 0)
    keep = ((q >= 2) | (q * 0 + band > 0)) & ((q < 2) | (q * 0 + band < lats - 1))
    turned = jnp.where(keep, corners[...].astype(F32), 0.0).reshape(points, 256)
    turned = jnp.transpose(turned)[0:half]
    lane = iota((half, points), 1)
    turned = jnp.concatenate(
        [jnp.where((lane // 16) % 2 == v, turned, 0.0) for v in range(2)], axis=0
    )
    leftward = (iota((2 * half, points), 1) // 32) % 2 == 0
    for q in range(4):
        factor = jnp.where(leftward, lon_tap[q], lon_tap[q + 5])
        rim_lhs[:, (8 + q) * points : (9 + q) * points] = (factor * turned).astype(BF16)
    fix_ref[...] = jnp.dot(rim_lhs[...], rim_hot[...], preferred_element_type=F32)
    for phase, source, target in ((0, ask, asked), (1, reply, replied), (2, give, given)):
        all_of(source, target, phase).wait_send()


def exchange_call(sizes, *operands):
    lons, lats, levels, rows, lanes, records, channels = sizes
    half, slots = 144, lons * 8
    points = slots // 2
    packed = -(-(rows + 8) * 8 // lanes) * lanes
    vmem = pl.BlockSpec(memory_space=pltpu.VMEM)
    hbm = pl.BlockSpec(memory_space=pltpu.HBM)
    return pl.pallas_call(
        functools.partial(exchange_kernel, sizes),
        out_shape=(
            jax.ShapeDtypeStruct((2 * half, packed), F32),
            jax.ShapeDtypeStruct((9, 2 * half, lanes), F32),
            jax.ShapeDtypeStruct((2 * half, (rows + 8) * lanes), F32),
            jax.ShapeDtypeStruct((2 * half, (rows - 16) * lanes), F32),
        ),
        in_specs=[hbm] * 10,
        out_specs=(vmem,) * 4,
        scratch_shapes=[
            pltpu.VMEM((2 * levels * rows, lanes), F32),
            pltpu.VMEM((2, half, rows * lanes), BF16),
            pltpu.VMEM((records * 2 * levels, channels), BF16),
            pltpu.VMEM((2, half, 384), BF16),
            pltpu.VMEM((records, 512), F32),
            pltpu.VMEM((records, channels), F32),
            pltpu.VMEM((records, channels), BF16),
            pltpu.VMEM((records, channels), BF16),
            pltpu.VMEM((1, records), jnp.int32),
            pltpu.VMEM((1, records), jnp.int32),
            pltpu.VMEM((1, records), jnp.int32),
            pltpu.VMEM((levels, 2, levels), BF16),
            pltpu.VMEM((9, 2, levels), F32),
            pltpu.VMEM((9, 2, levels), F32),
            pltpu.VMEM((256, 256), F32),
            pltpu.VMEM((2 * half, 384), BF16),
            pltpu.VMEM((2 * half, 32), F32),
            pltpu.VMEM((9, 2 * half, lanes), F32),
            pltpu.VMEM((3, 2 * half, 9 * points), BF16),
            pltpu.VMEM((3, 9 * points, lanes), BF16),
            pltpu.VMEM((3, points, lanes), F32),
            pltpu.VMEM((points, rows * lanes), BF16),
            pltpu.VMEM((2 * half, 12 * points), BF16),
            pltpu.VMEM((12 * points, packed), BF16),
            pltpu.VMEM((lons, 1, slots), F32),
            pltpu.VMEM((lons, 1, slots), F32),
            pltpu.VMEM((lons, 4, 384), BF16),
            pltpu.VMEM((lons, 4, 384), BF16),
            pltpu.VMEM((lons, 4, 384), BF16),
            pltpu.VMEM((lons, 4, 384), BF16),
            pltpu.VMEM((2 * half, points), BF16),
            pltpu.VMEM((4, 2 * half, points), BF16),
            pltpu.VMEM((4, 32, 256), BF16),
            pltpu.VMEM((4, 32, 256), BF16),
            pltpu.VMEM((1, slots), F32),
            pltpu.VMEM((4, 1, slots), F32),
            pltpu.SemaphoreType.DMA((10,)),
            pltpu.SemaphoreType.DMA((3,)),
            pltpu.SemaphoreType.DMA((3,)),
            pltpu.SemaphoreType.DMA((12,)),
            pltpu.SemaphoreType.DMA((12,)),
        ],
        compiler_params=pltpu.CompilerParams(
            collective_id=0, has_side_effects=True, vmem_limit_bytes=36 << 20
        ),
        name="exchange",
    )(*[pltpu.with_memory_space_constraint(x, pltpu.HBM) for x in operands])


def grid_kernel(
    rows, halo, lanes, levels,
    fix_ref, lat_tap, part_ref, mid_ref, out_hbm,
    rim_ref, out_ref, sem,
):
    size = fix_ref.shape[0]
    wide = 2 * halo
    taps = wide + 1
    group = lanes // wide
    lane = iota((8, lanes), 1)

    def filter_rim(base):
        lat = [lat_tap[k, pl.ds(base, 8), :] for k in range(taps)]
        parts = [
            fix_ref[pl.ds(base, 8), q * lanes : (q + 1) * lanes] for q in range(rows // group + 1)
        ]
        sums = [lat[0] * part for part in parts[:-1]]
        for k in range(1, taps):
            turned = [pltpu.roll(part, lanes - wide * k, 1) for part in parts]
            here = lane < lanes - wide * k
            sums = [
                value + lat[k] * jnp.where(here, turned[q], turned[q + 1])
                for q, value in enumerate(sums)
            ]
        for q, value in enumerate(sums):
            rim_ref[pl.ds(base, 8), q * lanes : (q + 1) * lanes] = value

    for base in range(0, size, 8):
        filter_rim(base)

    flat = out_ref.reshape(size * rows, lanes)
    outer = (lane < halo) | (lane >= lanes - halo)

    def filter_rows(block, base):
        lat = [lat_tap[k, pl.ds(base, 8), :] for k in range(taps)]
        start = block * 8
        q, first = divmod(start, group)
        rim = rim_ref[pl.ds(base, 8), q * lanes : (q + 1) * lanes]
        inner = 8 <= start < rows - 8
        along = [
            part_ref[pl.ds(base, 8), i * lanes : (i + 1) * lanes]
            for i in range(start, start + 8 + 2 * halo)
        ]
        for r in range(8):
            turned = pltpu.roll(rim, (-(wide * (first + r) + halo)) % lanes, 1)
            if inner:
                at = (start - 8 + r) * lanes
                out = mid_ref[pl.ds(base, 8), at : at + lanes]
            else:
                out = lat[0] * along[r]
                for k in range(1, taps):
                    out = out + lat[k] * along[r + k]
            out = out + jnp.where(outer, turned, 0.0)
            flat[pl.ds(base * rows + start + r, 8, stride=rows), :] = out

    copies = []
    for block in range(rows // 8):
        for v in range(2):
            for part in range(size // 16):
                filter_rows(block, v * (size // 2) + part * 8)
            copy = pltpu.make_async_copy(
                out_ref.at[v, pl.ds(0, levels), pl.ds(block * 8, 8), :],
                out_hbm.at[v, :, pl.ds(block * 8, 8), :],
                sem.at[2 * block + v],
            )
            copy.start()
            copies.append(copy)
    for copy in copies:
        copy.wait()


def grid_call(fix, lat_tap, part, mid, levels, rows, lanes):
    size = fix.shape[0]
    vmem = pl.BlockSpec(memory_space=pltpu.VMEM)
    return pl.pallas_call(
        functools.partial(grid_kernel, rows, 4, lanes, levels),
        out_shape=jax.ShapeDtypeStruct((2, levels, rows, lanes), F32),
        in_specs=[vmem] * 4,
        out_specs=pl.BlockSpec(memory_space=pl.ANY),
        scratch_shapes=[
            pltpu.VMEM((size, rows * 8), F32),
            pltpu.VMEM((2, size // 2, rows, lanes), F32),
            pltpu.SemaphoreType.DMA((rows // 4,)),
        ],
        compiler_params=pltpu.CompilerParams(vmem_limit_bytes=24 << 20),
        name="grid",
    )(fix, lat_tap, part, mid)


def body(
    state_field,
    jacobian,
    observed,
    inverse_var,
    valid_count,
    destination,
    column,
    vertical,
    lon_taps,
    lat_taps,
):
    variables, levels, rows, lanes = state_field.shape
    records, channels = jacobian.shape[1], jacobian.shape[-1]
    sizes = (
        lax.axis_size("lon"), lax.axis_size("lat"), levels, rows, lanes, records, channels,
    )
    fix, lat_tap, part, mid = exchange_call(
        sizes,
        state_field.reshape(variables * levels * rows, lanes),
        jacobian.transpose(0, 1, 3, 2, 4).reshape(records * levels * variables, channels),
        observed.reshape(records, channels),
        inverse_var.reshape(records, channels),
        valid_count.reshape(1, records),
        destination.reshape(1, records),
        column.reshape(1, records),
        vertical.transpose(1, 0, 2),
        lon_taps.transpose(2, 0, 1),
        lat_taps.transpose(2, 0, 1),
    )
    return grid_call(fix, lat_tap, part, mid, levels, rows, lanes)


def solution(mesh):
    placed = (
        P(None, None, "lat", "lon"),
        P("lat", "lon", None, None, None),
        P("lat", "lon", None),
        P("lat", "lon", None),
        P("lat", "lon"),
        P("lat", "lon", None),
        P("lat", "lon"),
        P(),
        P(),
        P(),
    )
    return jax.shard_map(
        body, mesh=mesh, in_specs=placed, out_specs=P(None, None, "lat", "lon"), check_vma=False
    )
```

```python
import functools

import jax
import jax.numpy as jnp
from jax import lax
from jax.experimental import pallas as pl
from jax.experimental.pallas import tpu as pltpu
from jax.sharding import PartitionSpec as P

F32 = jnp.float32
BF16 = jnp.bfloat16


MESH = pl.DeviceIdType.MESH
NT = (((1,), (1,)), ((), ()))
TN = (((0,), (0,)), ((), ()))


def iota(shape, dim):
    return lax.broadcasted_iota(jnp.int32, shape, dim)


def far_first(ring):
    steps = [
        (z, x, c) for z in range(ring[0]) for x in range(ring[1]) for c in range(ring[2])
    ][1:]
    return sorted(
        steps, key=lambda s: -(min(s[0], ring[0] - s[0]) + min(s[1], ring[1] - s[1]) + 0.5 * s[2])
    )


def peer_at(me, step, ring):
    z, x, c = me // (ring[1] * ring[2]), (me // ring[2]) % ring[1], me % ring[2]
    z, x, c = (lax.rem(at + go, size) for at, go, size in zip((z, x, c), step, ring))
    return (z * ring[1] + x) * ring[2] + c


def exchange_kernel(
    sizes,
    state_hbm, jac_hbm, obs_hbm, inv_hbm, count_hbm, dest_hbm, col_hbm, vert_hbm, lon_hbm, lat_hbm,
    fix_ref, lat_tap, along_ref,
    state_ref, low_ref, jac_ref, map_ref, part_ref, model_ref,
    obs_ref, inv_ref, count_ref, dest_ref, col_ref, vert_ref, lon_ref, lat_ref, square_ref, mix_ref, tap_ref, lon_tap, lhs_ref, hot_ref, row_ref, pick_ref,
    rim_lhs, rim_hot,
    ask, asked, reply, replied, give, given,
    table, tables, corner, corners, spot, spots,
    load_sem, a2a_send, a2a_recv, near_send, near_recv,
):
    lons, lats, levels, rows, lanes, records, channels = sizes
    ring = (lons // 8, 4, 2)
    half = low_ref.shape[1]
    slots = 2 * table.shape[1]
    points = table.shape[1]
    span = 512
    feats = 2 * levels
    wide = 8 * feats
    me = lax.axis_index("lon")
    band = lax.axis_index("lat")
    east, west = lax.rem(me + 1, lons), lax.rem(me + lons - 1, lons)
    south, north = lax.rem(band + 1, lats), lax.rem(band + lats - 1, lats)

    barrier = pltpu.get_barrier_semaphore()
    peers = [peer_at(me, step, ring) for step in far_first(ring)]
    for peer in peers:
        pl.semaphore_signal(barrier, inc=1, device_id={"lon": peer}, device_id_type=MESH)

    for there in (north, south):
        pl.semaphore_signal(barrier, inc=1, device_id={"lat": there}, device_id_type=MESH)
        for side in (west, east):
            pl.semaphore_signal(
                barrier, inc=1, device_id={"lat": there, "lon": side}, device_id_type=MESH
            )

    loads = [
        pltpu.make_async_copy(source, target, load_sem.at[q])
        for q, (source, target) in enumerate(
            (
                (dest_hbm, dest_ref), (col_hbm, col_ref), (count_hbm, count_ref),
                (vert_hbm, vert_ref), (lon_hbm, lon_ref), (lat_hbm, lat_ref),
                (obs_hbm, obs_ref), (inv_hbm, inv_ref),
                (state_hbm, state_ref), (jac_hbm, jac_ref),
            )
        )
    ]
    for load in loads:
        load.start()

    for load in loads[:3]:
        load.wait()
    drow = dest_ref[...].astype(F32)
    prow = col_ref[...]
    irow = (prow // lanes).astype(F32)
    jrow = (prow % lanes).astype(F32)
    krow = count_ref[...].astype(F32)
    eye = iota((records, records), 0) == iota((records, records), 1)

    def column_of(row):
        return jnp.sum(jnp.where(eye, row, 0.0), axis=1, keepdims=True)

    dcol, icol, jcol, kcol = (column_of(row) for row in (drow, irow, jrow, krow))
    same = dcol == drow
    before = iota((records, records), 1) < iota((records, records), 0)
    after = iota((records, records), 0) < iota((records, records), 1)
    rank_col = jnp.sum(jnp.where(same & before, 1.0, 0.0), axis=1, keepdims=True)
    rank_row = jnp.sum(jnp.where(same & after, 1.0, 0.0), axis=0, keepdims=True)

    lane = iota((records, slots), 1)
    mine = ((lane % points) // 4 == me) & ((lane % 4).astype(F32) == rank_col)
    value = jnp.where(lane < points, icol + 1.0, jcol)
    values = jnp.where(mine, value, 0.0).astype(BF16)
    toward = jnp.where(iota((lons, records), 0).astype(F32) == drow, 1.0, 0.0).astype(BF16)
    asks = jnp.dot(toward, values, preferred_element_type=F32)
    ask[...] = asks.reshape(lons, 1, slots)

    pl.semaphore_wait(barrier, lons - 1 + 6)

    def send_all(source, target, phase):
        for peer in peers:
            pltpu.make_async_remote_copy(
                src_ref=source.at[peer],
                dst_ref=target.at[me],
                send_sem=a2a_send.at[phase],
                recv_sem=a2a_recv.at[phase],
                device_id={"lon": peer},
                device_id_type=MESH,
            ).start()

        target[me] = source[me]

    def all_of(source, target, phase):
        return pltpu.make_async_remote_copy(
            src_ref=source.at[pl.ds(0, lons - 1)],
            dst_ref=target.at[pl.ds(0, lons - 1)],
            send_sem=a2a_send.at[phase],
            recv_sem=a2a_recv.at[phase],
            device_id={"lon": east},
            device_id_type=MESH,
        )

    send_all(ask, asked, 0)

    loads[8].wait()
    for v in range(2):
        low_ref[v, half - 16 : half, :] = jnp.zeros((16, rows * lanes), BF16)

        @pl.loop(0, rows)
        def _(i):
            plane = state_ref[pl.ds(v * levels * rows + i, levels, stride=rows), :]
            start = pl.multiple_of(i * lanes, lanes)
            low_ref[v, 0:levels, pl.ds(start, lanes)] = plane.astype(BF16)

    for v in range(2):
        hit = iota((half, 384), 1) == 2 * iota((half, 384), 0) + v
        hit = hit & (iota((half, 384), 0) < levels)
        map_ref[v] = jnp.where(hit, 1.0, 0.0).astype(BF16)

    for load in loads[3:6]:
        load.wait()
    for v in range(2):
        square_ref[...] = jnp.zeros(square_ref.shape, F32)
        square_ref[0:levels, 0:levels] = vert_ref[...].astype(F32)[:, v, :]
        turned = jnp.transpose(square_ref[...])[0:half].astype(BF16)
        mix_ref[v * half : (v + 1) * half, :] = jnp.dot(
            turned[:, 0:half], map_ref[v], preferred_element_type=F32
        ).astype(BF16)
        square_ref[0:9, 0:levels] = lon_ref[...][:, v, :]
        square_ref[16:25, 0:levels] = lat_ref[...][:, v, :]
        tap_ref[v * half : (v + 1) * half, :] = jnp.transpose(square_ref[0:128, :])[0:half, 0:32]

    all_of(ask, asked, 0).wait_recv()
    seen = jnp.sum(asked[...], axis=0)
    spot[...] = seen
    neighbours = (
        ({"lat": north}, 2), ({"lat": south}, 1), ({"lon": east}, 3), ({"lon": west}, 4),
    )

    def near(source, target, target_index, sem, device):
        return pltpu.make_async_remote_copy(
            src_ref=source,
            dst_ref=target.at[target_index],
            send_sem=near_send.at[sem],
            recv_sem=near_recv.at[sem],
            device_id=device,
            device_id_type=MESH,
        )

    spot_copies = [
        near(spot, spots, index - 1, index - 1, device) for device, index in neighbours
    ]
    for copy in spot_copies:
        copy.start()

    points_row = jnp.concatenate(
        [seen[:, 0:points], seen[:, points:]]
        + [jnp.zeros((6, points), F32)],
        axis=0,
    )
    points_col = jnp.transpose(points_row)
    icol_own, jcol_own = points_col[:, 0:1] - 1.0, points_col[:, 1:2]
    spot_col = jnp.where(icol_own >= 0.0, icol_own * lanes + jcol_own, -1.0)
    chunk = 512
    for c in range(rows * lanes // chunk):
        at = (iota((points, chunk), 1) + c * chunk).astype(F32)
        pick_ref[:, c * chunk : (c + 1) * chunk] = jnp.where(spot_col == at, 1.0, 0.0).astype(BF16)
    states = jnp.zeros((points, 384), F32)
    for v in range(2):
        found = lax.dot_general(
            pick_ref[...], low_ref[v], NT, preferred_element_type=F32
        ).astype(BF16)
        states = states + jnp.dot(found, map_ref[v], preferred_element_type=F32)
    reply[...] = states.reshape(lons, 4, 384).astype(BF16)
    send_all(reply, replied, 1)

    for k in range(9):
        lon_tap[k] = jnp.broadcast_to(tap_ref[:, k : k + 1], (2 * half, points))
        lat_tap[k] = jnp.broadcast_to(tap_ref[:, 16 + k : 17 + k], (2 * half, points))

    def mark(index, i, j):
        lane = iota((points, lanes), 1)
        for k in range(9):
            hit = (lane + (k - 4)).astype(F32) == j
            hot_ref[index, k * points : (k + 1) * points, :] = jnp.where(hit, 1.0, 0.0).astype(BF16)
        row_ref[index] = jnp.broadcast_to(i, (points, lanes))

    def spread(index, pair):
        columns = []
        for i in (2 * pair, 2 * pair + 1):
            here = jnp.where(row_ref[index] == float(i), 1.0, 0.0).astype(BF16)
            columns.append(
                jnp.concatenate(
                    [hot_ref[index, k * points : (k + 1) * points, :] * here for k in range(9)],
                    axis=0,
                )
            )
        along_ref[:, 2 * pair * lanes : (2 * pair + 2) * lanes] = jnp.dot(
            lhs_ref[index], jnp.concatenate(columns, axis=1), preferred_element_type=F32
        )

    def scale(index, values):
        for k in range(9):
            lhs_ref[index, :, k * points : (k + 1) * points] = (lon_tap[k] * values).astype(BF16)

    mark(0, icol_own + 4.0, jcol_own)
    packed = fix_ref.shape[1]

    def mark_rim(index, spot):
        hit = jnp.where(spot == iota((points, packed), 1).astype(F32), 1.0, 0.0)
        rim_hot[index * points : (index + 1) * points, :] = hit.astype(BF16)

    r = iota((points, packed), 0)
    c, i, j = r // 32, (r // 4) % 4, r % 4
    for q in range(4):
        e = jnp.where(c % 2 == 0, 4 + j - q, j + 3 - q)
        least = jnp.where(c % 2 == 0, 4, 0)
        good = (e >= least) & (e < least + 4)
        spot_at = jnp.where(good, ((c // 2) * (rows + 4) + i) * 8 + e, -1)
        mark_rim(8 + q, spot_at.astype(F32))
    for load in (loads[6], loads[7], loads[9]):
        load.wait()
    all_of(reply, replied, 1).wait_recv()
    answers = replied[...].astype(F32).reshape(points, 384).astype(BF16)
    slane = iota((records, points), 1)
    take = ((slane // 4).astype(F32) == dcol) & ((slane % 4).astype(F32) == rank_col)
    picked = jnp.dot(
        jnp.where(take, 1.0, 0.0).astype(BF16), answers, preferred_element_type=F32
    )
    part_ref[:, 0:384] = picked
    part_ref[:, 384:span] = jnp.zeros((records, span - 384), F32)
    tiles = -(-wide // lanes)
    extra = feats - 2 * lanes
    eighth = iota((8, lanes), 0)

    def blocks(group):
        part = part_ref[8 * group : 8 * group + 8, :]
        turned = [pltpu.roll(part, extra * q, 1) if q else part for q in range(8)]
        line = []
        for tile in range(tiles):
            value = jnp.zeros((8, lanes), F32)
            for q in range(8):
                j = tile - 2 * q
                if 0 <= j < span // lanes:
                    value = jnp.where(
                        eighth == q, turned[q][:, j * lanes : (j + 1) * lanes], value
                    )
            line.append(value)
        return jnp.concatenate(line, axis=1)[:, 0:wide]

    def gather_blocks(value, group):
        total = jnp.zeros((8, span), F32)
        column = iota((8, span), 1)
        value = jnp.concatenate(
            [value, jnp.zeros((8, (tiles + 2) * lanes - wide), F32)], axis=1
        )
        for q in range(8):
            piece = value[:, 2 * lanes * q : 2 * lanes * q + span]
            piece = pltpu.roll(piece, span - extra * q, 1) if q else piece
            total = jnp.where((iota((8, span), 0) == q) & (column < feats), piece, total)
        part_ref[8 * group : 8 * group + 8, :] = total

    def two_groups(group):
        return jnp.concatenate(
            [
                jac_ref[group * wide : (group + 1) * wide, :],
                jac_ref[(group + 1) * wide : (group + 2) * wide, :],
            ],
            axis=1,
        )

    for g in range(0, records // 8, 2):
        left = jnp.concatenate([blocks(g), blocks(g + 1)], axis=0).astype(BF16)
        both = jnp.dot(left, two_groups(g), preferred_element_type=F32)
        model_ref[8 * g : 8 * g + 8, :] = both[0:8, 0:channels]
        model_ref[8 * g + 8 : 8 * g + 16, :] = both[8:16, channels:]
    alive = iota((records, channels), 1).astype(F32) < kcol
    weight = jnp.where(alive, inv_ref[...].astype(F32), 0.0)
    model_ref[...] = weight * (model_ref[...] - obs_ref[...].astype(F32))
    for g in range(0, records // 8, 2):
        none = jnp.zeros((8, channels), F32)
        one, two = model_ref[8 * g : 8 * g + 8, :], model_ref[8 * g + 8 : 8 * g + 16, :]
        left = jnp.concatenate(
            [jnp.concatenate([one, none], axis=1), jnp.concatenate([none, two], axis=1)], axis=0
        ).astype(BF16)
        both = lax.dot_general(left, two_groups(g), NT, preferred_element_type=F32)
        gather_blocks(both[0:8], g)
        gather_blocks(both[8:16], g + 1)
    srow = iota((points, records), 0)
    put = ((srow // 4).astype(F32) == drow) & ((srow % 4).astype(F32) == rank_row)
    gives = jnp.dot(
        jnp.where(put, 1.0, 0.0).astype(BF16),
        part_ref[:, 0:384].astype(BF16),
        preferred_element_type=F32,
    )
    give[...] = gives.reshape(lons, 4, 384).astype(BF16)
    send_all(give, given, 2)

    for copy in spot_copies:
        copy.wait()
    shifts = (4, 4 - rows, 4 + rows, 4, 4)
    stack = []
    for q in range(5):
        both = spot[...] if q == 0 else spots[q - 1]
        i1, j = both[:, 0:points], both[:, points : 2 * points]
        i = i1 - 1.0 + shifts[q]
        good = (i1 > 0.0) & (i >= 0.0) & (i < rows + 8.0)
        if q == 1:
            good = good & (iota((1, points), 0) + band > 0)
        if q == 2:
            good = good & (iota((1, points), 0) + band < lats - 1)
        stack += [jnp.where(good, i, -1000.0), j]
    where = jnp.transpose(jnp.concatenate(stack + stack[:6], axis=0))
    for q in range(4):
        i, j = where[:, 6:7], where[:, 7:8]
        e = j - (lanes - 8.0) - q
        good = (i >= 0.0) & (j >= lanes - 4.0) & (e >= 4.0)
        mark_rim(q, jnp.where(good, i * 8.0 + e, -1.0))
        i, j = where[:, 8:9], where[:, 9:10]
        e = j + 3.0 - q
        good = (i >= 0.0) & (j < 4.0) & (e < 4.0)
        mark_rim(4 + q, jnp.where(good, i * 8.0 + e, -1.0))
    for q in (1, 2):
        mark(q, where[:, 2 * q : 2 * q + 1], where[:, 2 * q + 1 : 2 * q + 2])

    all_of(give, given, 2).wait_recv()
    terms_in = given[...].astype(F32).reshape(points, 384).astype(BF16)
    parts = [
        lax.dot_general(
            mix_ref[v * half : (v + 1) * half, :], terms_in, NT, preferred_element_type=F32
        )
        for v in range(2)
    ]
    exact = jnp.concatenate(parts, axis=0)
    own = exact.astype(BF16)
    table[...] = own
    table_copies = [
        near(table, tables, index - 1, 3 + index, device) for device, index in neighbours
    ]
    for copy in table_copies:
        copy.start()
    r = iota((128, points), 0)
    c, v, i, j = r // 32, (r // 16) % 2, (r // 4) % 4, r % 4
    at_i = jnp.where(c < 2, rows - 4, 0) + i
    at_j = jnp.where(c % 2 == 0, lanes - 4, 0) + j
    both = spot[...]
    hot = (both[:, 0:points] == (at_i + 1).astype(F32)) & (both[:, points:] == at_j.astype(F32))
    cut = jnp.zeros((128, half), F32)
    for var in range(2):
        pick = jnp.where(hot & (v == var), 1.0, 0.0).astype(BF16)
        cut = cut + lax.dot_general(
            pick, own[var * half : (var + 1) * half], NT, preferred_element_type=F32
        )
    cut = jnp.concatenate([cut, jnp.zeros((128, 256 - half), F32)], axis=1)
    corner[...] = cut.reshape(4, 32, 256).astype(BF16)
    corner_copies = [
        near(corner.at[q], corners, q, 8 + q, {"lat": there, "lon": side})
        for q, (there, side) in enumerate(
            ((south, east), (south, west), (north, east), (north, west))
        )
    ]
    for copy in corner_copies:
        copy.start()
    scale(0, exact)
    for pair in range(2, rows // 2 + 2):
        spread(0, pair)
    for copy in table_copies[2:]:
        copy.wait()
    left, right = tables[2].astype(F32), tables[3].astype(F32)
    for q in range(4):
        rim_lhs[:, q * points : (q + 1) * points] = (lon_tap[q] * left).astype(BF16)
        rim_lhs[:, (4 + q) * points : (5 + q) * points] = (lon_tap[q + 5] * right).astype(BF16)
    for copy in table_copies[:2]:
        copy.wait()
    for q in (1, 2):
        scale(q, tables[q - 1].astype(F32))
    for pair in (0, 1):
        spread(1, pair)
        spread(2, rows // 2 + 2 + pair)
    for copy in corner_copies:
        copy.wait()
    q = iota((4, 32, 256), 0)
    keep = ((q >= 2) | (q * 0 + band > 0)) & ((q < 2) | (q * 0 + band < lats - 1))
    turned = jnp.where(keep, corners[...].astype(F32), 0.0).reshape(points, 256)
    turned = jnp.transpose(turned)[0:half]
    lane = iota((half, points), 1)
    turned = jnp.concatenate(
        [jnp.where((lane // 16) % 2 == v, turned, 0.0) for v in range(2)], axis=0
    )
    leftward = (iota((2 * half, points), 1) // 32) % 2 == 0
    for q in range(4):
        factor = jnp.where(leftward, lon_tap[q], lon_tap[q + 5])
        rim_lhs[:, (8 + q) * points : (9 + q) * points] = (factor * turned).astype(BF16)
    fix_ref[...] = jnp.dot(rim_lhs[...], rim_hot[...], preferred_element_type=F32)
    for phase, source, target in ((0, ask, asked), (1, reply, replied), (2, give, given)):
        all_of(source, target, phase).wait_send()


def exchange_call(sizes, *operands):
    lons, lats, levels, rows, lanes, records, channels = sizes
    half, slots = 144, lons * 8
    points = slots // 2
    packed = -(-(rows + 8) * 8 // lanes) * lanes
    vmem = pl.BlockSpec(memory_space=pltpu.VMEM)
    hbm = pl.BlockSpec(memory_space=pltpu.HBM)
    return pl.pallas_call(
        functools.partial(exchange_kernel, sizes),
        out_shape=(
            jax.ShapeDtypeStruct((2 * half, packed), F32),
            jax.ShapeDtypeStruct((9, 2 * half, lanes), F32),
            jax.ShapeDtypeStruct((2 * half, (rows + 8) * lanes), F32),
        ),
        in_specs=[hbm] * 10,
        out_specs=(vmem,) * 3,
        scratch_shapes=[
            pltpu.VMEM((2 * levels * rows, lanes), F32),
            pltpu.VMEM((2, half, rows * lanes), BF16),
            pltpu.VMEM((records * 2 * levels, channels), BF16),
            pltpu.VMEM((2, half, 384), BF16),
            pltpu.VMEM((records, 512), F32),
            pltpu.VMEM((records, channels), F32),
            pltpu.VMEM((records, channels), BF16),
            pltpu.VMEM((records, channels), BF16),
            pltpu.VMEM((1, records), jnp.int32),
            pltpu.VMEM((1, records), jnp.int32),
            pltpu.VMEM((1, records), jnp.int32),
            pltpu.VMEM((levels, 2, levels), BF16),
            pltpu.VMEM((9, 2, levels), F32),
            pltpu.VMEM((9, 2, levels), F32),
            pltpu.VMEM((256, 256), F32),
            pltpu.VMEM((2 * half, 384), BF16),
            pltpu.VMEM((2 * half, 32), F32),
            pltpu.VMEM((9, 2 * half, lanes), F32),
            pltpu.VMEM((3, 2 * half, 9 * points), BF16),
            pltpu.VMEM((3, 9 * points, lanes), BF16),
            pltpu.VMEM((3, points, lanes), F32),
            pltpu.VMEM((points, rows * lanes), BF16),
            pltpu.VMEM((2 * half, 12 * points), BF16),
            pltpu.VMEM((12 * points, packed), BF16),
            pltpu.VMEM((lons, 1, slots), F32),
            pltpu.VMEM((lons, 1, slots), F32),
            pltpu.VMEM((lons, 4, 384), BF16),
            pltpu.VMEM((lons, 4, 384), BF16),
            pltpu.VMEM((lons, 4, 384), BF16),
            pltpu.VMEM((lons, 4, 384), BF16),
            pltpu.VMEM((2 * half, points), BF16),
            pltpu.VMEM((4, 2 * half, points), BF16),
            pltpu.VMEM((4, 32, 256), BF16),
            pltpu.VMEM((4, 32, 256), BF16),
            pltpu.VMEM((1, slots), F32),
            pltpu.VMEM((4, 1, slots), F32),
            pltpu.SemaphoreType.DMA((10,)),
            pltpu.SemaphoreType.DMA((3,)),
            pltpu.SemaphoreType.DMA((3,)),
            pltpu.SemaphoreType.DMA((12,)),
            pltpu.SemaphoreType.DMA((12,)),
        ],
        compiler_params=pltpu.CompilerParams(
            collective_id=0, has_side_effects=True, vmem_limit_bytes=36 << 20
        ),
        name="exchange",
    )(*[pltpu.with_memory_space_constraint(x, pltpu.HBM) for x in operands])


def grid_kernel(rows, halo, lanes, levels, fix_ref, lat_tap, part_ref, out_hbm, rim_ref, out_ref, sem):
    size = fix_ref.shape[0]
    wide = 2 * halo
    taps = wide + 1
    group = lanes // wide
    lane = iota((8, lanes), 1)

    def filter_rim(base):
        lat = [lat_tap[k, pl.ds(base, 8), :] for k in range(taps)]
        parts = [
            fix_ref[pl.ds(base, 8), q * lanes : (q + 1) * lanes] for q in range(rows // group + 1)
        ]
        sums = [lat[0] * part for part in parts[:-1]]
        for k in range(1, taps):
            turned = [pltpu.roll(part, lanes - wide * k, 1) for part in parts]
            here = lane < lanes - wide * k
            sums = [
                value + lat[k] * jnp.where(here, turned[q], turned[q + 1])
                for q, value in enumerate(sums)
            ]
        for q, value in enumerate(sums):
            rim_ref[pl.ds(base, 8), q * lanes : (q + 1) * lanes] = value

    for base in range(0, size, 8):
        filter_rim(base)

    flat = out_ref.reshape(size * rows, lanes)
    outer = (lane < halo) | (lane >= lanes - halo)

    def filter_rows(block, base):
        lat = [lat_tap[k, pl.ds(base, 8), :] for k in range(taps)]
        start = block * 8
        q, first = divmod(start, group)
        rim = rim_ref[pl.ds(base, 8), q * lanes : (q + 1) * lanes]
        along = [
            part_ref[pl.ds(base, 8), i * lanes : (i + 1) * lanes]
            for i in range(start, start + 8 + 2 * halo)
        ]
        for r in range(8):
            turned = pltpu.roll(rim, (-(wide * (first + r) + halo)) % lanes, 1)
            out = lat[0] * along[r]
            for k in range(1, taps):
                out = out + lat[k] * along[r + k]
            out = out + jnp.where(outer, turned, 0.0)
            flat[pl.ds(base * rows + start + r, 8, stride=rows), :] = out

    copies = []
    for block in range(rows // 8):
        for v in range(2):
            for part in range(size // 16):
                filter_rows(block, v * (size // 2) + part * 8)
            copy = pltpu.make_async_copy(
                out_ref.at[v, pl.ds(0, levels), pl.ds(block * 8, 8), :],
                out_hbm.at[v, :, pl.ds(block * 8, 8), :],
                sem.at[2 * block + v],
            )
            copy.start()
            copies.append(copy)
    for copy in copies:
        copy.wait()


def grid_call(fix, lat_tap, part, levels, rows, lanes):
    size = fix.shape[0]
    vmem = pl.BlockSpec(memory_space=pltpu.VMEM)
    return pl.pallas_call(
        functools.partial(grid_kernel, rows, 4, lanes, levels),
        out_shape=jax.ShapeDtypeStruct((2, levels, rows, lanes), F32),
        in_specs=[vmem] * 3,
        out_specs=pl.BlockSpec(memory_space=pl.ANY),
        scratch_shapes=[
            pltpu.VMEM((size, rows * 8), F32),
            pltpu.VMEM((2, size // 2, rows, lanes), F32),
            pltpu.SemaphoreType.DMA((rows // 4,)),
        ],
        compiler_params=pltpu.CompilerParams(vmem_limit_bytes=24 << 20),
        name="grid",
    )(fix, lat_tap, part)


def body(
    state_field,
    jacobian,
    observed,
    inverse_var,
    valid_count,
    destination,
    column,
    vertical,
    lon_taps,
    lat_taps,
):
    variables, levels, rows, lanes = state_field.shape
    records, channels = jacobian.shape[1], jacobian.shape[-1]
    sizes = (
        lax.axis_size("lon"), lax.axis_size("lat"), levels, rows, lanes, records, channels,
    )
    fix, lat_tap, part = exchange_call(
        sizes,
        state_field.reshape(variables * levels * rows, lanes),
        jacobian.transpose(0, 1, 3, 2, 4).reshape(records * levels * variables, channels),
        observed.reshape(records, channels),
        inverse_var.reshape(records, channels),
        valid_count.reshape(1, records),
        destination.reshape(1, records),
        column.reshape(1, records),
        vertical.transpose(1, 0, 2),
        lon_taps.transpose(2, 0, 1),
        lat_taps.transpose(2, 0, 1),
    )
    return grid_call(fix, lat_tap, part, levels, rows, lanes)


def solution(mesh):
    placed = (
        P(None, None, "lat", "lon"),
        P("lat", "lon", None, None, None),
        P("lat", "lon", None),
        P("lat", "lon", None),
        P("lat", "lon"),
        P("lat", "lon", None),
        P("lat", "lon"),
        P(),
        P(),
        P(),
    )
    return jax.shard_map(
        body, mesh=mesh, in_specs=placed, out_specs=P(None, None, "lat", "lon"), check_vma=False
    )
```
